32 devices in a mesh: clus: 8 (over z, core), node: 4 (over y, x).
Axes of the slice: x: 2, y: 2, z: 4, core: 2. Of those that a mesh axis runs over, the one named last changes fastest.
Arguments:
- node_feats: bfloat16 [8, 512, 1024], P('clus', 'node'), may hold values from -6 to 6
- cotangent: bfloat16 [8, 512, 1024], P('clus', 'node'), may hold values from -6 to 6
- w_query: bfloat16 [1024, 1024], replicated, may hold values from -0.1875 to 0.1875
- w_key: bfloat16 [1024, 1024], replicated, may hold values from -0.1875 to 0.1875
- w_value: bfloat16 [1024, 1024], replicated, may hold values from -0.1875 to 0.1875
- w_out: bfloat16 [1024, 1024], replicated, may hold values from -0.1875 to 0.1875
- eigvec: bfloat16 [8, 64, 512], P('clus'), may hold values from -3.5 to 3.5
- eig_weight: float32 [16, 64], P('node'), may hold values from 0.1 to 1
- block_mask: int32 [8, 16, 4, 4], P('clus', 'node'), may hold values from 0 to 1, as said below
Outputs:
- grad_nodes: bfloat16 [8, 512, 1024], P('clus', 'node')
- grad_eigvec: float32 [8, 64, 512], P('clus', None, 'node')
- grad_weight: float32 [16, 64], P('node')
- grad_proj: float32 [4, 1024, 1024], P(None, 'clus', 'node')
The draws below stay inside these ranges and needn't reach their ends.
Inputs may be any that keep to these rules, and one draw needn't show every extreme that they name: `block_mask`: each entry is 0 or 1; every diagonal tile is 1; the share of present tiles differs between clusters and heads.
All inputs are finite; a program needn't handle non-finite values.
Results may differ from the reference program's by a relative error of at most 0.012.
The reference program's roundings to bfloat16 on the way (of `weighted`, `prob_half`, `output` and `dscore`) count: a program that leaves them out, or rounds other values in their place, can miss the bound.
Values may be sent and summed in bfloat16 or wider, within the bound.
No kernel may reach another device: no remote copies, remote signals or barrier semaphores. Data moves between devices by JAX's collectives and lax.ppermute only.
A program may use at most 128 MiB of HBM per device.

```python
import math
import jax
import jax.numpy as jnp
from jax import lax

H = 16
EIG = 64
TILE = 128
D = 1024
NC = 512
NB = 4
CLUSTERS = 8


def draw_eigvec(key, part):
    sub_keys = jax.random.split(key, 2)
    values = jnp.clip(0.3 * jax.random.normal(sub_keys[1], (CLUSTERS, EIG, NC), jnp.float32), -3.5, 3.5)
    return values.astype(jnp.bfloat16)


def draw_block_mask(key, part):
    sub_keys = jax.random.split(key, 2)
    levels = jax.random.randint(sub_keys[0], (CLUSTERS, H, 1, 1), 2, 7)
    chosen = jax.random.randint(sub_keys[1], (CLUSTERS, H, NB, NB), 0, 8) < levels
    diagonal = jnp.arange(NB)[:, None] == jnp.arange(NB)[None, :]
    return jnp.where(chosen | diagonal[None, None], 1, 0).astype(jnp.int32)


def spiked(array, own_key, source, target, parts, factor):
    owner, partner = [(jnp.arange(array.shape[axis_at]) // (array.shape[axis_at] // parts)).reshape([-1 if axis == axis_at else 1 for axis in range(array.ndim)]) for axis_at in (source, target)]
    chosen = jax.random.permutation(own_key, parts)[partner]
    strong = (owner == chosen) | (owner == (partner + parts // 2) % parts)
    return jnp.where(strong, factor * array, array)


def shard_levels(rng, shape, shards, low, largest):
    gain = 1.0
    for position, blocks in shards:
        steps = jax.random.uniform(jax.random.fold_in(jax.random.fold_in(rng, 6), position), (blocks,), jnp.float32, low / len(shards), largest / len(shards))
        gain = gain * jnp.repeat(jnp.exp(steps), shape[position] // blocks).reshape((-1,) + (1,) * (len(shape) - 1 - position))
    return gain


def normal_values(rng, shape, scale, reach, cuts=(), held_as=jnp.bfloat16):
    level = shard_levels(rng, shape, cuts, -0.22, 0.18) if cuts else 1.0
    values = jax.random.normal(rng, shape, jnp.float32) * scale * level
    return jnp.minimum(jnp.maximum(values, -reach), reach).astype(held_as)


def noise_with(rng, extent, scale, bound, shards, heavy, held_as=jnp.bfloat16):
    drawn = scale * jax.random.normal(rng, extent, jnp.float32)
    if shards:
        drawn = drawn * shard_levels(rng, extent, shards, -0.22, 0.18)
    return jnp.clip(spiked(drawn, jax.random.fold_in(rng, 3), *heavy), -bound, bound).astype(held_as)


def setup_inputs(seed: int = 0) -> dict:
    splits = jax.random.split(jax.random.key(seed), 10)
    return {
        "node_feats": noise_with(splits[0], (CLUSTERS, NC, D), 1.0, 6.0, ((0, 8), (1, 4)), (1, 2, 4, 2.0)),
        "cotangent": normal_values(splits[1], (CLUSTERS, NC, D), 1.0, 6.0, ((0, 8), (1, 4))),
        "w_query": normal_values(splits[2], (D, D), D ** -0.5, 0.1875),
        "w_key": normal_values(splits[3], (D, D), D ** -0.5, 0.1875),
        "w_value": normal_values(splits[4], (D, D), D ** -0.5, 0.1875),
        "w_out": normal_values(splits[5], (D, D), D ** -0.5, 0.1875),
        "eigvec": draw_eigvec(jax.random.fold_in(splits[9], 71), 0),
        "eig_weight": jnp.clip(jnp.exp(math.log(1.0) - 2.3025851 * jax.random.uniform(splits[7], (H, EIG), jnp.float32) ** shard_levels(splits[7], (H, EIG), ((0, 4),), -0.2, 0.2)), 0.1, 1.0),
        "block_mask": draw_block_mask(jax.random.fold_in(splits[9], 71), 0),
    }


def attend_head(eigvec_c, query, keys_all, values_all, dout_head, lam_head, mask_head):
    score_scale = query.shape[1] ** -0.5
    eig_float = eigvec_c.astype(jnp.float32)
    weighted = (lam_head[:, None] * eig_float).astype(jnp.bfloat16)
    eig_bias = jnp.dot(eigvec_c.T, weighted, preferred_element_type=jnp.float32)
    scores = jnp.dot(query, keys_all.T, preferred_element_type=jnp.float32) * score_scale + eig_bias
    present = jnp.repeat(jnp.repeat(mask_head, TILE, axis=0), TILE, axis=1) > 0
    masked = jnp.where(present, scores, -jnp.inf)
    row_max = jnp.max(masked, axis=1, keepdims=True)
    raised = jnp.exp(masked - row_max)
    attn_prob = raised / jnp.sum(raised, axis=1, keepdims=True)
    prob_half = attn_prob.astype(jnp.bfloat16)
    output = jnp.dot(prob_half, values_all, preferred_element_type=jnp.float32).astype(jnp.bfloat16)
    dprob = jnp.dot(dout_head, values_all.T, preferred_element_type=jnp.float32)
    row_delta = jnp.sum(attn_prob * dprob, axis=1, keepdims=True)
    dscore = (attn_prob * (dprob - row_delta)).astype(jnp.bfloat16)
    query_grad = (jnp.dot(dscore, keys_all, preferred_element_type=jnp.float32) * score_scale).astype(jnp.bfloat16)
    key_grad = (jnp.dot(dscore.T, query, preferred_element_type=jnp.float32) * score_scale).astype(jnp.bfloat16)
    value_grad = jnp.dot(prob_half.T, dout_head, preferred_element_type=jnp.float32).astype(jnp.bfloat16)
    eig_left = jnp.dot(dscore, eigvec_c.T, preferred_element_type=jnp.float32)
    eig_right = jnp.dot(dscore.T, eigvec_c.T, preferred_element_type=jnp.float32)
    weight_grad = jnp.sum(eig_float.T * eig_left, axis=0)
    eig_grad = lam_head[None, :] * (eig_left + eig_right)
    return output, query_grad, key_grad, value_grad, weight_grad, eig_grad


def reference(node_feats, cotangent, w_query, w_key, w_value, w_out, eigvec, eig_weight, block_mask):
    node_count = node_feats.shape[1]
    model_width = node_feats.shape[2]
    head_count = eig_weight.shape[0]
    head_size = model_width // head_count

    def by_head(matrix):
        return matrix.reshape(node_count, head_count, head_size).transpose(1, 0, 2)

    def merged(stacked):
        return stacked.transpose(1, 0, 2).reshape(node_count, model_width)

    def one_cluster(totals, inputs):
        node_rows, grads_in, eigvec_c, mask_c = inputs
        query = jnp.dot(node_rows, w_query, preferred_element_type=jnp.float32).astype(jnp.bfloat16)
        keys_all = jnp.dot(node_rows, w_key, preferred_element_type=jnp.float32).astype(jnp.bfloat16)
        values_all = jnp.dot(node_rows, w_value, preferred_element_type=jnp.float32).astype(jnp.bfloat16)
        d_att = jnp.dot(grads_in, w_out, preferred_element_type=jnp.float32).astype(jnp.bfloat16)

        def one_head(items):
            return attend_head(eigvec_c, items[0], items[1], items[2], items[3], items[4], items[5])

        results = lax.map(one_head, (by_head(query), by_head(keys_all), by_head(values_all), by_head(d_att), eig_weight, mask_c))
        output = merged(results[0])
        query_grad = merged(results[1])
        key_grad = merged(results[2])
        value_grad = merged(results[3])
        grad_rows = (jnp.dot(query_grad, w_query.T, preferred_element_type=jnp.float32)
                     + jnp.dot(key_grad, w_key.T, preferred_element_type=jnp.float32)
                     + jnp.dot(value_grad, w_value.T, preferred_element_type=jnp.float32)).astype(jnp.bfloat16)
        grad_terms = jnp.stack([
            jnp.dot(node_rows.T, query_grad, preferred_element_type=jnp.float32),
            jnp.dot(node_rows.T, key_grad, preferred_element_type=jnp.float32),
            jnp.dot(node_rows.T, value_grad, preferred_element_type=jnp.float32),
            jnp.dot(grads_in.T, output, preferred_element_type=jnp.float32)])
        new_totals = (totals[0] + grad_terms, totals[1] + results[4])
        return new_totals, (grad_rows, jnp.sum(results[5], axis=0).T)

    initial = (jnp.zeros((4, model_width, model_width), jnp.float32), jnp.zeros(eig_weight.shape, jnp.float32))
    totals, stacked = lax.scan(one_cluster, initial, (node_feats, cotangent, eigvec, block_mask))
    return stacked[0], stacked[1], totals[1], totals[0]
```

```python
import functools
import math

import jax
import jax.numpy as jnp
from jax import lax
from jax.experimental import pallas as pl
from jax.experimental.pallas import tpu as pltpu
from jax.sharding import PartitionSpec as P

BF16 = jnp.bfloat16
F32 = jnp.float32


def mm(a, b):
    return jnp.dot(a, b, preferred_element_type=F32)


def partner(me, step, size):
    return me ^ step if size & (size - 1) == 0 else lax.rem(me + step, size)


def send(value, axis, step, size):
    if size & (size - 1) == 0:
        pairs = [(i, i ^ step) for i in range(size)]
    else:
        pairs = [((i + step) % size, i) for i in range(size)]
    return lax.ppermute(value, axis, pairs)


def send_back(value, axis, step, size):
    if size & (size - 1) == 0:
        return send(value, axis, step, size)
    return lax.ppermute(value, axis, [(i, (i + step) % size) for i in range(size)])


def gather_blocks(own, axis, size):
    if size == 4:
        half = own.shape[0] // 2
        top, bottom = own[:half], own[half:]
        top2 = send(top, axis, 2, size)
        bottom1 = send(bottom, axis, 1, size)
        bottom2 = send(bottom, axis, 2, size)
        top1 = send(top, axis, 1, size)
        top3 = send(top2, axis, 1, size)
        bottom3 = send(bottom1, axis, 2, size)
        return [own, top1, bottom1, top2, bottom2, top3, bottom3]
    return [own] + [send(own, axis, step, size) for step in range(1, size)]


def forward_kernel(scale, heads, head_size, pieces, mask_ref, *refs):
    row_refs = refs[:pieces]
    (w_ref, eig_ref, eig_t_ref, lam_ref) = refs[pieces : pieces + 4]
    (prob_ref, out_ref, q_ref, k_t_ref, v_ref, kw, qe, v_t) = refs[pieces + 4 :]
    head, block = pl.program_id(0), pl.program_id(1)
    nodes = eig_ref.shape[1]
    width = heads * head_size
    cols = prob_ref.shape[2]
    tile_count = mask_ref.shape[1]
    tile = nodes // tile_count

    @pl.when((head == 0) & (block == 0))
    def _():
        rows = jnp.concatenate([r[...] for r in row_refs], axis=0)
        eig_t = eig_t_ref[...]
        eig = eig_ref[...]
        query = mm(rows, w_ref[:, :width]).astype(BF16)
        query_s = (query.astype(F32) * scale).astype(BF16)
        query_t = query_s.T
        for h in range(heads):
            part = slice(h * head_size, (h + 1) * head_size)
            q_ref[h] = jnp.concatenate([query[:, part], eig_t], axis=1)
            qe[h] = jnp.concatenate([query_t[part], eig], axis=0)
        keys = mm(rows, w_ref[:, width : 2 * width]).astype(BF16)
        keys_t = keys.T
        for h in range(heads):
            part = slice(h * head_size, (h + 1) * head_size)
            weighted_t = (eig_t.astype(F32) * lam_ref[h : h + 1, :]).astype(BF16)
            kw[h] = jnp.concatenate([keys[:, part], weighted_t], axis=1)
            k_t_ref[h] = jnp.concatenate([keys_t[part], eig], axis=0)
        values = mm(rows, w_ref[:, 2 * width :]).astype(BF16)
        values_t = values.T
        for h in range(heads):
            part = slice(h * head_size, (h + 1) * head_size)
            v_ref[h] = values[:, part]
            v_t[h] = values_t[part]

    at = pl.multiple_of(block * cols, cols)
    scores = mm(kw[head], qe[head, :, pl.ds(at, cols)])
    tiles_here = cols // tile
    columns = []
    for i in range(tiles_here):
        rows = []
        for j in range(tile_count):
            here = scores[j * tile : (j + 1) * tile, i * tile : (i + 1) * tile]
            present = mask_ref[head, block * tiles_here + i, j] > 0
            rows.append(jnp.where(present, here, -jnp.inf))
        columns.append(jnp.concatenate(rows, axis=0))
    masked = jnp.concatenate(columns, axis=1)
    top = jnp.max(masked, axis=0, keepdims=True)
    raised = jnp.exp(masked - top)
    total = jnp.sum(raised, axis=0, keepdims=True)
    prob = raised * (1.0 / total)
    prob_ref[0] = prob
    out_ref[...] = mm(v_t[head], prob.astype(BF16)).astype(BF16)


def backward_kernel(scale, heads, head_size, pieces, blocks, *refs):
    row_refs = refs[:pieces]
    (w_ref, lam_ref, lam_t_ref, eig_t_ref, prob_ref, q_ref, k_t_ref, v_ref) = refs[
        pieces : pieces + 8
    ]
    outs = refs[pieces + 8 :]
    grads_ref, eig_out, gw_ref = outs[0], outs[1], outs[2]
    ret_refs = outs[3 : 3 + blocks]
    d_all, d_t, acc_k, acc_v, eig_acc = outs[3 + blocks :]
    head, block = pl.program_id(0), pl.program_id(1)
    last_head, last_block = pl.num_programs(0) - 1, pl.num_programs(1) - 1
    nodes = eig_t_ref.shape[0]
    cols = prob_ref.shape[2]
    width = heads * head_size
    size = nodes // blocks

    @pl.when((head == 0) & (block == 0))
    def _():
        rows = jnp.concatenate([r[...] for r in row_refs], axis=0)
        d_att = mm(rows, w_ref[...]).astype(BF16)
        d_att_t = d_att.T
        for h in range(heads):
            part = slice(h * head_size, (h + 1) * head_size)
            d_all[h] = d_att[:, part]
            d_t[h] = d_att_t[part]
        eig_acc[...] = jnp.zeros_like(eig_acc)

    at = pl.multiple_of(block * cols, cols)
    prob = prob_ref[0]
    half = prob.astype(BF16)
    dprob = mm(v_ref[0], d_t[head, :, pl.ds(at, cols)])
    delta = jnp.sum(prob * dprob, axis=0, keepdims=True)
    dscore = (prob * (dprob - delta)).astype(BF16)
    left = mm(k_t_ref[0], dscore)
    first = pl.multiple_of(head * head_size, head_size)
    grads_ref[pl.ds(first, head_size), pl.ds(at, cols)] = (left[:head_size] * scale).astype(BF16)
    eig_acc[:, pl.ds(at, cols)] += lam_t_ref[0] * left[head_size:]
    right = mm(dscore, q_ref[0, pl.ds(at, cols), :])
    value = mm(half, d_all[head, pl.ds(at, cols), :])

    @pl.when(block == 0)
    def _():
        acc_k[...] = right
        acc_v[...] = value

    @pl.when(block > 0)
    def _():
        acc_k[...] += right
        acc_v[...] += value

    @pl.when(block == last_block)
    def _():
        whole = acc_k[...]
        flat = whole.T
        grads_ref[pl.ds(width + first, head_size), :] = (flat[:head_size] * scale).astype(BF16)
        eig_acc[...] += lam_t_ref[0] * flat[head_size:]
        gw_ref[pl.ds(head, 1), :] = jnp.sum(
            eig_t_ref[...].astype(F32) * whole[:, head_size:], axis=0, keepdims=True
        )
        grads_ref[pl.ds(2 * width + first, head_size), :] = acc_v[...].T.astype(BF16)

    @pl.when((block == last_block) & (head == last_head))
    def _():
        eig_out[...] = eig_acc[:, :size]
        for b in range(blocks):
            part = slice(b * size, (b + 1) * size)
            ret_refs[b][: 3 * width] = grads_ref[:, part]
            ret_refs[b][3 * width :] = eig_acc[:, part].astype(BF16)


def terms_kernel(pieces, columns, order_ref, *refs):
    row_refs = refs[:pieces]
    grads_ref = refs[pieces]
    keep_ref, send_ref, rows = refs[pieces + 1 :]
    count = keep_ref.shape[1]

    @pl.when(pl.program_id(0) == 0)
    def _():
        at = 0
        for r in row_refs:
            rows[at : at + r.shape[0]] = r[...]
            at += r.shape[0]

    grads = grads_ref[...]

    def block(index):
        index = order_ref[index]
        if columns % 128 == 0:
            return rows[:, pl.ds(pl.multiple_of(index * columns, columns), columns)]
        fit = 128 // columns
        both = rows[:, pl.ds(pl.multiple_of(index // fit * 128, 128), 128)]
        found = both[:, :columns]
        for part in range(1, fit):
            here = both[:, part * columns : (part + 1) * columns]
            found = jnp.where(index % fit == part, here, found)
        return found

    for target, base in ((send_ref, count), (keep_ref, 0)):
        for i in range(count):
            target[0, i] = mm(grads, block(base + i)).astype(target.dtype)


def nodes_kernel(blocks, *refs):
    out_ref = refs[2 * blocks]
    total = mm(refs[0][...], refs[blocks][: refs[0].shape[1]])
    for b in range(1, blocks):
        total += mm(refs[b][...], refs[blocks + b][: refs[b].shape[1]])
    out_ref[...] = total.T.astype(BF16)


def sum_kernel(count, *refs):
    total = refs[0][0, 0].astype(F32)
    for r in refs[1:count]:
        total += r[0, 0].astype(F32)
    refs[count][0] = total.T


def body(node_feats, cotangent, w_query, w_key, w_value, w_out, eigvec, eig_weight, block_mask):
    node_size = lax.axis_size("node")
    clus_size = lax.axis_size("clus")
    node_me = lax.axis_index("node")
    clus_me = lax.axis_index("clus")
    own_rows, own_grads = node_feats[0], cotangent[0]
    size, model = own_rows.shape
    heads, eig_count = eig_weight.shape
    nodes = size * node_size
    width = model // node_size
    head_size = width // heads
    scale = head_size ** (-0.5)
    assert math.frexp(scale)[0] == 0.5
    block = nodes
    while block * nodes > 512 * 512 and block > 128:
        block //= 2

    rows = gather_blocks(own_rows, "node", node_size)
    grads = gather_blocks(own_grads, "node", node_size)
    pieces = len(rows)

    order = [partner(node_me, s, node_size) for s in range(node_size)]

    def columns_of(weight, s):
        return lax.dynamic_slice(weight, (0, order[s] * width), (model, width))

    weights = [
        jnp.concatenate([columns_of(w, s) for w in (w_query, w_key, w_value)], axis=1)
        for s in range(node_size)
    ]
    weight_out = columns_of(w_out, 0)
    eig = jnp.concatenate(
        [lax.dynamic_slice(eigvec[0], (0, order[s] * size), (eig_count, size)) for s in range(node_size)],
        axis=1,
    )
    eig_t = eig.T
    tile_count = block_mask.shape[2]
    per = tile_count // node_size
    tiles = jnp.concatenate([order[s] * per + jnp.arange(per) for s in range(node_size)])
    mask = jnp.take(jnp.take(block_mask[0], tiles, axis=1), tiles, axis=2)
    lam_t = jnp.broadcast_to(eig_weight[:, :, None], (heads, eig_count, 128))[:, :, :1]

    def whole(shape):
        return pl.BlockSpec(shape, lambda *_: (0,) * len(shape))

    steps = nodes // block
    both = head_size + eig_count
    prob, out_t, q_all, k_t_all, v_all = pl.pallas_call(
        functools.partial(forward_kernel, scale, heads, head_size, pieces),
        grid_spec=pltpu.PrefetchScalarGridSpec(
            num_scalar_prefetch=1,
            grid=(heads, steps),
            in_specs=[whole(r.shape) for r in rows]
            + [
                whole((model, 3 * width)),
                whole((eig_count, nodes)),
                whole((nodes, eig_count)),
                whole((heads, eig_count)),
            ],
            out_specs=[
                pl.BlockSpec((1, nodes, block), lambda h, b, *_: (h, 0, b)),
                pl.BlockSpec((head_size, block), lambda h, b, *_: (h, b)),
                whole((heads, nodes, both)),
                whole((heads, both, nodes)),
                whole((heads, nodes, head_size)),
            ],
            scratch_shapes=[
                pltpu.VMEM((heads, nodes, both), BF16),
                pltpu.VMEM((heads, both, nodes), BF16),
                pltpu.VMEM((heads, head_size, nodes), BF16),
            ],
        ),
        out_shape=[
            jax.ShapeDtypeStruct((heads, nodes, nodes), F32),
            jax.ShapeDtypeStruct((width, nodes), BF16),
            jax.ShapeDtypeStruct((heads, nodes, both), BF16),
            jax.ShapeDtypeStruct((heads, both, nodes), BF16),
            jax.ShapeDtypeStruct((heads, nodes, head_size), BF16),
        ],
        cost_estimate=pl.CostEstimate(flops=3 * 10**9, bytes_accessed=8 * 2**20, transcendentals=10**6),
        name="forward",
    )(mask, *rows, weights[0], eig, eig_t, eig_weight)

    target = model // clus_size
    rest = clus_size // 2
    blocks_at = [2 * s for s in range(rest)] + [2 * s + 1 for s in range(rest)]
    assert clus_size & (clus_size - 1) == 0
    column_order = jnp.stack([clus_me ^ b for b in blocks_at]).astype(jnp.int32)

    def terms(parts, grads_t, count, name):
        return pl.pallas_call(
            functools.partial(terms_kernel, pieces, target),
            grid_spec=pltpu.PrefetchScalarGridSpec(
                num_scalar_prefetch=1,
                grid=(count,),
                in_specs=[whole(r.shape) for r in parts]
                + [pl.BlockSpec((width, nodes), lambda a, *_: (a, 0))],
                out_specs=[
                    pl.BlockSpec((1, rest, width, target), lambda a, *_: (a, 0, 0, 0)),
                    pl.BlockSpec((1, rest, width, target), lambda a, *_: (a, 0, 0, 0)),
                ],
                scratch_shapes=[pltpu.VMEM((nodes, model), BF16)],
            ),
            out_shape=[
                jax.ShapeDtypeStruct((count, rest, width, target), F32),
                jax.ShapeDtypeStruct((count, rest, width, target), BF16),
            ],
            cost_estimate=pl.CostEstimate(
                flops=count * 10**9, bytes_accessed=count * 2**21, transcendentals=0
            ),
            name=name,
        )(column_order, *parts, grads_t)

    def reduce_blocks(keep, give):
        got = send(give, "clus", 1, clus_size)
        total = keep + got.astype(F32)
        mine = [total[:, :1]]
        for s in range(1, rest):
            mine.append(send(total[:, s : s + 1].astype(BF16), "clus", 2 * s, clus_size))
        return mine

    keep_o, give_o = terms(grads, out_t, 1, "terms_out")
    sums_o = reduce_blocks(keep_o, give_o)

    results = pl.pallas_call(
        functools.partial(backward_kernel, scale, heads, head_size, pieces, node_size),
        grid=(heads, steps),
        in_specs=[whole(r.shape) for r in grads]
        + [
            whole((model, width)),
            whole((heads, eig_count)),
            pl.BlockSpec((1, eig_count, 1), lambda h, b: (h, 0, 0)),
            whole((nodes, eig_count)),
            pl.BlockSpec((1, nodes, block), lambda h, b: (h, 0, b)),
            pl.BlockSpec((1, nodes, both), lambda h, b: (h, 0, 0)),
            pl.BlockSpec((1, both, nodes), lambda h, b: (h, 0, 0)),
            pl.BlockSpec((1, nodes, head_size), lambda h, b: (h, 0, 0)),
        ],
        out_specs=[
            whole((3 * width, nodes)),
            whole((eig_count, size)),
            whole((heads, eig_count)),
        ]
        + [whole((3 * width + eig_count, size))] * node_size,
        out_shape=[
            jax.ShapeDtypeStruct((3 * width, nodes), BF16),
            jax.ShapeDtypeStruct((eig_count, size), F32),
            jax.ShapeDtypeStruct((heads, eig_count), F32),
        ]
        + [jax.ShapeDtypeStruct((3 * width + eig_count, size), BF16)] * node_size,
        scratch_shapes=[
            pltpu.VMEM((heads, nodes, head_size), BF16),
            pltpu.VMEM((heads, head_size, nodes), BF16),
            pltpu.VMEM((nodes, both), F32),
            pltpu.VMEM((nodes, head_size), F32),
            pltpu.VMEM((eig_count, nodes), F32),
        ],
        cost_estimate=pl.CostEstimate(flops=4 * 10**9, bytes_accessed=8 * 2**20, transcendentals=0),
        name="backward",
    )(*grads, weight_out, eig_weight, lam_t, eig_t, prob, q_all, k_t_all, v_all)
    grads_t, eig_own, weight_part = results[:3]
    parts = results[3:]
    returned = [parts[0]] + [send_back(parts[s], "node", s, node_size) for s in range(1, node_size)]

    keep, give = terms(rows, grads_t, 3, "terms_rows")
    sums = reduce_blocks(keep, give)

    grad_weight = weight_part
    step = 1
    while step < clus_size:
        grad_weight = grad_weight + send(grad_weight, "clus", step, clus_size)
        step *= 2

    grad_rows = pl.pallas_call(
        functools.partial(nodes_kernel, node_size),
        in_specs=[pl.BlockSpec(memory_space=pltpu.VMEM)] * (2 * node_size),
        out_specs=pl.BlockSpec(memory_space=pltpu.VMEM),
        out_shape=jax.ShapeDtypeStruct((size, model), BF16),
        cost_estimate=pl.CostEstimate(flops=10**9, bytes_accessed=6 * 2**20, transcendentals=0),
        name="nodes",
    )(*weights, *returned)
    grad_eig = eig_own
    for s in range(1, node_size):
        grad_eig = grad_eig + returned[s][3 * width :].astype(F32)

    def final(parts_in, count, name):
        spec = pl.BlockSpec((1, 1, width, target), lambda a: (a, 0, 0, 0))
        return pl.pallas_call(
            functools.partial(sum_kernel, len(parts_in)),
            grid=(count,),
            in_specs=[spec] * len(parts_in),
            out_specs=pl.BlockSpec((1, target, width), lambda a: (a, 0, 0)),
            out_shape=jax.ShapeDtypeStruct((count, target, width), F32),
            name=name,
        )(*parts_in)

    grad_proj = jnp.concatenate([final(sums, 3, "sum_rows"), final(sums_o, 1, "sum_out")], axis=0)
    return (grad_rows[None], grad_eig[None], grad_weight, grad_proj)


def solution(mesh):
    placed = (
        P("clus", "node", None),
        P("clus", "node", None),
        P(),
        P(),
        P(),
        P(),
        P("clus", None, None),
        P("node", None),
        P("clus", "node", None, None),
    )
    return jax.shard_map(
        body,
        mesh=mesh,
        in_specs=placed,
        out_specs=(
            P("clus", "node", None),
            P("clus", None, "node"),
            P("node", None),
            P(None, "clus", "node"),
        ),
        check_vma=False,
    )
```

```python
import functools
import math

import jax
import jax.numpy as jnp
from jax import lax
from jax.experimental import pallas as pl
from jax.experimental.pallas import tpu as pltpu
from jax.sharding import PartitionSpec as P

BF16 = jnp.bfloat16
F32 = jnp.float32


def mm(a, b):
    return jnp.dot(a, b, preferred_element_type=F32)


def partner(me, step, size):
    return me ^ step if size & (size - 1) == 0 else lax.rem(me + step, size)


def take(value, axis, step, size):
    if size & (size - 1) == 0:
        pairs = [(i, i ^ step) for i in range(size)]
    else:
        pairs = [((i + step) % size, i) for i in range(size)]
    return lax.ppermute(value, axis, pairs)


def give(value, axis, step, size):
    if size & (size - 1) == 0:
        return take(value, axis, step, size)
    return lax.ppermute(value, axis, [(i, (i + step) % size) for i in range(size)])


def whole(shape):
    return pl.BlockSpec(shape, lambda *_: (0,) * len(shape))


def column_blocks(weight, width):
    model = weight.shape[0]
    if width % 128 == 0:
        return weight, lambda at: pl.BlockSpec((model, width), lambda *g: (0, at(*g)))
    parts = weight.reshape(model, -1, width).transpose(1, 0, 2)
    return parts, lambda at: pl.BlockSpec((None, model, width), lambda *g: (at(*g), 0, 0))


def out_grad_kernel(count, ids_ref, rows_ref, w_ref, *out_refs):
    step = pl.program_id(0)
    value = mm(rows_ref[...], w_ref[...]).astype(BF16)
    for s in range(count):

        @pl.when(step == s)
        def _(s=s):
            out_refs[s][...] = value


def attention_kernel(scale, heads, head_size, blocks, ids_ref, mask_ref, *refs):
    row_refs, d_refs = refs[:blocks], refs[blocks : 2 * blocks]
    refs = refs[2 * blocks :]
    wq_ref, wk_ref, wv_ref, eig_ref, lam_ref, lam_t_ref = refs[:6]
    grads_ref, eig_out, gw_ref = refs[6:9]
    ret_refs = refs[9 : 9 + blocks]
    (kw, qe, qn, kt, vn, vt, dn, dt, eig_t, acc_k, acc_v, eig_acc) = refs[9 + blocks :]
    head, block = pl.program_id(0), pl.program_id(1)
    last_head, last_block = pl.num_programs(0) - 1, pl.num_programs(1) - 1
    eig_count, nodes = eig_ref.shape
    width = heads * head_size
    size = nodes // blocks
    cols = qe.shape[3]
    tile_count = mask_ref.shape[1]
    tile = nodes // tile_count
    per = tile_count // blocks

    @pl.when((head == 0) & (block == 0))
    def _():
        parts = []
        for s in range(blocks):
            at = pl.multiple_of(ids_ref[s] * size, size)
            parts.append(eig_ref[:, pl.ds(at, size)])
        eig = jnp.concatenate(parts, axis=1)
        turned = eig.T
        eig_t[...] = turned
        rows = jnp.concatenate([r[...] for r in row_refs], axis=0)
        query = mm(rows, wq_ref[...]).astype(BF16)
        query_t = (query.astype(F32) * scale).astype(BF16).T
        keys = mm(rows, wk_ref[...]).astype(BF16)
        keys_t = keys.T
        values = mm(rows, wv_ref[...]).astype(BF16)
        values_t = values.T
        d_att = jnp.concatenate([r[...] for r in d_refs], axis=0)
        d_att_t = d_att.T
        for h in range(heads):
            part = slice(h * head_size, (h + 1) * head_size)
            weighted_t = (turned.astype(F32) * lam_ref[h : h + 1, :]).astype(BF16)
            kw[h] = jnp.concatenate([keys[:, part], weighted_t], axis=1)
            qn[h] = jnp.concatenate([query[:, part], turned], axis=1)
            kt[h] = jnp.concatenate([keys_t[part], eig], axis=0)
            vn[h] = values[:, part]
            vt[h] = values_t[part]
            dn[h] = d_att[:, part]
            for b in range(nodes // cols):
                here = slice(b * cols, (b + 1) * cols)
                qe[h, b] = jnp.concatenate([query_t[part, here], eig[:, here]], axis=0)
                dt[h, b] = d_att_t[part, here]
        eig_acc[...] = jnp.zeros_like(eig_acc)

    lane = lax.broadcasted_iota(jnp.int32, (eig_count, heads), 1)
    lam = jnp.sum(jnp.where(lane == head, lam_t_ref[...], 0.0), axis=1, keepdims=True)
    at = pl.multiple_of(block * cols, cols)
    here = pl.ds(at, cols)
    scores = mm(kw[head], qe[head, block])
    tiles_here = cols // tile
    columns = []
    for i in range(tiles_here):
        i_tile = block * tiles_here + i
        i_at = ids_ref[i_tile // per] * per + i_tile % per
        rows = []
        for j in range(tile_count):
            j_at = ids_ref[j // per] * per + j % per
            part = scores[j * tile : (j + 1) * tile, i * tile : (i + 1) * tile]
            rows.append(jnp.where(mask_ref[head, i_at, j_at] > 0, part, -jnp.inf))
        columns.append(jnp.concatenate(rows, axis=0))
    masked = jnp.concatenate(columns, axis=1)
    top = jnp.max(masked, axis=0, keepdims=True)
    raised = jnp.exp(masked - top)
    total = jnp.sum(raised, axis=0, keepdims=True)
    prob = raised * (1.0 / total)
    half = prob.astype(BF16)
    first = pl.multiple_of(head * head_size, head_size)
    grads_ref[pl.ds(3 * width + first, head_size), here] = mm(vt[head], half).astype(BF16)
    dprob = mm(vn[head], dt[head, block])
    delta = jnp.sum(prob * dprob, axis=0, keepdims=True)
    dscore = (prob * (dprob - delta)).astype(BF16)
    left = mm(kt[head], dscore)
    grads_ref[pl.ds(first, head_size), here] = (left[:head_size] * scale).astype(BF16)
    eig_acc[:, here] += lam * left[head_size:]
    right = mm(dscore, qn[head, here, :])
    value = mm(half, dn[head, here, :])

    @pl.when(block == 0)
    def _():
        acc_k[...] = right
        acc_v[...] = value

    @pl.when(block > 0)
    def _():
        acc_k[...] += right
        acc_v[...] += value

    @pl.when(block == last_block)
    def _():
        full = acc_k[...]
        flat = full.T
        grads_ref[pl.ds(width + first, head_size), :] = (flat[:head_size] * scale).astype(BF16)
        eig_acc[...] += lam * flat[head_size:]
        gw_ref[pl.ds(head, 1), :] = jnp.sum(
            eig_t[...].astype(F32) * full[:, head_size:], axis=0, keepdims=True
        )
        grads_ref[pl.ds(2 * width + first, head_size), :] = acc_v[...].T.astype(BF16)

    @pl.when((block == last_block) & (head == last_head))
    def _():
        eig_out[...] = eig_acc[:, :size]
        for b in range(blocks):
            part = slice(b * size, (b + 1) * size)
            ret_refs[b][: 3 * width] = grads_ref[: 3 * width, part]
            ret_refs[b][3 * width :] = eig_acc[:, part].astype(BF16)


def terms_kernel(blocks, nodes_blocks, target, ids_ref, *refs):
    row_refs, cot_refs = refs[:nodes_blocks], refs[nodes_blocks : 2 * nodes_blocks]
    grads_ref, send_ref, keep_ref, rows, cots = refs[2 * nodes_blocks :]
    step, half = pl.program_id(0), pl.num_programs(0) // 2
    width = send_ref.shape[2]
    group = send_ref.shape[0]

    @pl.when(step == 0)
    def _():
        size = row_refs[0].shape[0]
        for s in range(nodes_blocks):
            rows[s * size : (s + 1) * size] = row_refs[s][...]
            cots[s * size : (s + 1) * size] = cot_refs[s][...]

    def columns(array, index):
        if target % 128 == 0:
            return array[:, pl.ds(pl.multiple_of(index * target, target), target)]
        fit = 128 // target
        both = array[:, pl.ds(pl.multiple_of(index // fit * 128, 128), 128)]
        found = both[:, :target]
        for part in range(1, fit):
            here = both[:, part * target : (part + 1) * target]
            found = jnp.where(index % fit == part, here, found)
        return found

    at = [ids_ref[blocks + step * group + i] for i in range(group)]
    right = jnp.concatenate([columns(rows, a) for a in at], axis=1)
    first = mm(grads_ref[: 3 * width], right).astype(BF16)
    right = jnp.concatenate([columns(cots, a) for a in at], axis=1)
    second = mm(grads_ref[3 * width :], right).astype(BF16)

    def put(out_ref):
        for i in range(group):
            lanes = slice(i * target, (i + 1) * target)
            for a in range(3):
                out_ref[i, a] = first[a * width : (a + 1) * width, lanes]
            out_ref[i, 3] = second[:, lanes]

    @pl.when(step < half)
    def _():
        put(send_ref)

    @pl.when(step >= half)
    def _():
        put(keep_ref)


def pair_kernel(count, keep_ref, got_ref, gw_ref, gw_got_ref, own_ref, gw_out, *piece_refs):
    step = pl.program_id(0)
    _, terms, width, target = keep_ref.shape
    total = keep_ref[0].astype(F32) + got_ref[0].astype(F32)

    @pl.when(step == 0)
    def _():
        own_ref[...] = total

    for s in range(1, count):

        @pl.when(step == s)
        def _(s=s):
            ref = piece_refs[s - 1]
            for a in range(terms):
                ref[a * width : (a + 1) * width] = total[a].astype(BF16)
            sums = gw_ref[...] + gw_got_ref[...]
            high = sums.astype(BF16)
            low = (sums - high.astype(F32)).astype(BF16)
            base = terms * width
            rows, lanes = sums.shape
            ref[base:] = jnp.zeros((ref.shape[0] - base, target), BF16)
            if 2 * lanes <= target:
                ref[base : base + rows] = jnp.concatenate(
                    [high, low, jnp.zeros((rows, target - 2 * lanes), BF16)][: 2 + (2 * lanes < target)],
                    axis=1,
                )
            else:
                ref[base : base + rows, :lanes] = high
                ref[base + 8 : base + 8 + rows, :lanes] = low
            gw_out[...] = sums


def final_kernel(count, own_ref, gw_ref, *refs):
    piece_refs, gw_refs = refs[: count - 1], refs[count - 1 : 2 * (count - 1)]
    out_ref, gw_out = refs[2 * (count - 1) :]
    total = own_ref[0]
    for r in piece_refs:
        total += r[...].astype(F32)
    out_ref[0] = total.T

    @pl.when(pl.program_id(0) == 0)
    def _():
        sums = gw_ref[...]
        rows, lanes = sums.shape
        target = gw_refs[0].shape[1]
        for r in gw_refs:
            got = r[...].astype(F32)
            if 2 * lanes <= target:
                sums += got[:rows, :lanes] + got[:rows, lanes : 2 * lanes]
            else:
                sums += got[:rows, :lanes] + got[8 : 8 + rows, :lanes]
        gw_out[...] = sums


def nodes_kernel(blocks, width, ids_ref, eig_ref, *refs):
    ret_refs = refs[:blocks]
    w_refs = refs[blocks : blocks + 3]
    out_ref, eig_out, joined = refs[blocks + 3 :]

    @pl.when(pl.program_id(0) == 0)
    def _():
        total = eig_ref[...]
        for s in range(blocks):
            at = pl.multiple_of(ids_ref[s] * width, width)
            for a in range(3):
                joined[a, pl.ds(at, width)] = ret_refs[s][a * width : (a + 1) * width]
            if s > 0:
                total += ret_refs[s][3 * width :].astype(F32)
        eig_out[...] = total

    total = mm(w_refs[0][...], joined[0])
    total += mm(w_refs[1][...], joined[1])
    total += mm(w_refs[2][...], joined[2])
    out_ref[...] = total.T.astype(BF16)


def body(node_feats, cotangent, w_query, w_key, w_value, w_out, eigvec, eig_weight, block_mask):
    node_size = lax.axis_size("node")
    clus_size = lax.axis_size("clus")
    node_me = lax.axis_index("node")
    clus_me = lax.axis_index("clus")
    own_rows, own_cot = node_feats[0], cotangent[0]
    size, model = own_rows.shape
    heads, eig_count = eig_weight.shape
    nodes = size * node_size
    width = model // node_size
    head_size = width // heads
    scale = head_size ** (-0.5)
    assert math.frexp(scale)[0] == 0.5
    assert clus_size & (clus_size - 1) == 0
    block = nodes
    while block * nodes > 512 * 512 and block > 128:
        block //= 2
    far_first = [s for s in range(node_size - 1, 0, -1)]

    rest = clus_size // 2
    order = jnp.arange(node_size, dtype=jnp.int32)
    order = order ^ node_me if node_size & (node_size - 1) == 0 else (order + node_me) % node_size
    slots = jnp.arange(clus_size, dtype=jnp.int32)
    slots = (2 * (slots % rest) + jnp.where(slots < rest, 1, 0)) ^ clus_me
    ids = jnp.concatenate([order, slots])

    rows = [own_rows] + [None] * (node_size - 1)
    for s in far_first:
        rows[s] = take(own_rows, "node", s, node_size)

    weight, spec = column_blocks(w_out, width)
    d_parts = pl.pallas_call(
        functools.partial(out_grad_kernel, node_size),
        grid_spec=pltpu.PrefetchScalarGridSpec(
            num_scalar_prefetch=1,
            grid=(node_size,),
            in_specs=[whole((size, model)), spec(lambda s, ids: ids[s])],
            out_specs=[whole((size, width))] * node_size,
        ),
        out_shape=[jax.ShapeDtypeStruct((size, width), BF16)] * node_size,
        cost_estimate=pl.CostEstimate(flops=3 * 10**8, bytes_accessed=3 * 2**20, transcendentals=0),
        name="out_grad",
    )(ids, own_cot, weight)
    d_att = [d_parts[0]] + [None] * (node_size - 1)
    for s in far_first:
        d_att[s] = give(d_parts[s], "node", s, node_size)
    cots = [own_cot] + [None] * (node_size - 1)
    for s in far_first:
        cots[s] = take(own_cot, "node", s, node_size)

    steps = nodes // block
    both = head_size + eig_count
    weights = [column_blocks(w, width) for w in (w_query, w_key, w_value)]
    results = pl.pallas_call(
        functools.partial(attention_kernel, scale, heads, head_size, node_size),
        grid_spec=pltpu.PrefetchScalarGridSpec(
            num_scalar_prefetch=2,
            grid=(heads, steps),
            in_specs=[whole((size, model))] * node_size
            + [whole((size, width))] * node_size
            + [w[1](lambda h, b, ids, mask: ids[0]) for w in weights]
            + [
                whole((eig_count, nodes)),
                whole((heads, eig_count)),
                whole((eig_count, heads)),
            ],
            out_specs=[
                whole((4 * width, nodes)),
                whole((eig_count, size)),
                whole((heads, eig_count)),
            ]
            + [whole((3 * width + eig_count, size))] * node_size,
            scratch_shapes=[
                pltpu.VMEM((heads, nodes, both), BF16),
                pltpu.VMEM((heads, steps, both, block), BF16),
                pltpu.VMEM((heads, nodes, both), BF16),
                pltpu.VMEM((heads, both, nodes), BF16),
                pltpu.VMEM((heads, nodes, head_size), BF16),
                pltpu.VMEM((heads, head_size, nodes), BF16),
                pltpu.VMEM((heads, nodes, head_size), BF16),
                pltpu.VMEM((heads, steps, head_size, block), BF16),
                pltpu.VMEM((nodes, eig_count), BF16),
                pltpu.VMEM((nodes, both), F32),
                pltpu.VMEM((nodes, head_size), F32),
                pltpu.VMEM((eig_count, nodes), F32),
            ],
        ),
        out_shape=[
            jax.ShapeDtypeStruct((4 * width, nodes), BF16),
            jax.ShapeDtypeStruct((eig_count, size), F32),
            jax.ShapeDtypeStruct((heads, eig_count), F32),
        ]
        + [jax.ShapeDtypeStruct((3 * width + eig_count, size), BF16)] * node_size,
        cost_estimate=pl.CostEstimate(
            flops=8 * 10**9, bytes_accessed=8 * 2**20, transcendentals=10**6
        ),
        name="attention",
    )(
        ids,
        block_mask[0],
        *rows,
        *d_att,
        *[w[0] for w in weights],
        eigvec[0],
        eig_weight,
        eig_weight.T,
    )
    grads_t, eig_own, gw_own = results[:3]
    parts = results[3:]

    target = model // clus_size
    group = 2 if rest % 2 == 0 else 1
    half_steps = rest // group
    give_half, keep_half = pl.pallas_call(
        functools.partial(terms_kernel, node_size, node_size, target),
        grid_spec=pltpu.PrefetchScalarGridSpec(
            num_scalar_prefetch=1,
            grid=(2 * half_steps,),
            in_specs=[whole((size, model))] * (2 * node_size) + [whole((4 * width, nodes))],
            out_specs=[
                pl.BlockSpec(
                    (group, 4, width, target),
                    lambda g, *_: (jnp.minimum(g, half_steps - 1), 0, 0, 0),
                ),
                pl.BlockSpec(
                    (group, 4, width, target),
                    lambda g, *_: (jnp.maximum(g - half_steps, 0), 0, 0, 0),
                ),
            ],
            scratch_shapes=[pltpu.VMEM((nodes, model), BF16)] * 2,
        ),
        out_shape=[jax.ShapeDtypeStruct((rest, 4, width, target), BF16)] * 2,
        cost_estimate=pl.CostEstimate(flops=3 * 10**9, bytes_accessed=5 * 2**20, transcendentals=0),
        name="terms",
    )(ids, *rows, *cots, grads_t)
    gw_got = give(gw_own, "clus", 1, clus_size)
    got_half = give(give_half, "clus", 1, clus_size)

    piece_rows = 4 * width + 16
    half_spec = pl.BlockSpec((1, 4, width, target), lambda s: (s, 0, 0, 0))
    paired = pl.pallas_call(
        functools.partial(pair_kernel, rest),
        grid=(rest,),
        in_specs=[half_spec, half_spec, whole(eig_weight.shape), whole(eig_weight.shape)],
        out_specs=[whole((4, width, target)), whole(eig_weight.shape)]
        + [whole((piece_rows, target))] * (rest - 1),
        out_shape=[
            jax.ShapeDtypeStruct((4, width, target), F32),
            jax.ShapeDtypeStruct(eig_weight.shape, F32),
        ]
        + [jax.ShapeDtypeStruct((piece_rows, target), BF16)] * (rest - 1),
        cost_estimate=pl.CostEstimate(flops=10**6, bytes_accessed=4 * 2**20, transcendentals=0),
        name="pair",
    )(keep_half, got_half, gw_own, gw_got)
    own_sum, gw_pair = paired[:2]
    pieces = [None] * (rest - 1)
    for s in range(rest - 1, 0, -1):
        pieces[s - 1] = give(paired[1 + s], "clus", 2 * s, clus_size)

    returned = [parts[0]] + [None] * (node_size - 1)
    for s in far_first:
        returned[s] = give(parts[s], "node", s, node_size)

    chunk = min(256, model)
    grad_rows, grad_eig = pl.pallas_call(
        functools.partial(nodes_kernel, node_size, width),
        grid_spec=pltpu.PrefetchScalarGridSpec(
            num_scalar_prefetch=1,
            grid=(model // chunk,),
            in_specs=[whole((eig_count, size))]
            + [whole((3 * width + eig_count, size))] * node_size
            + [pl.BlockSpec((chunk, model), lambda g, *_: (g, 0))] * 3,
            out_specs=[
                pl.BlockSpec((size, chunk), lambda g, *_: (0, g)),
                whole((eig_count, size)),
            ],
            scratch_shapes=[pltpu.VMEM((3, model, size), BF16)],
        ),
        out_shape=[
            jax.ShapeDtypeStruct((size, model), BF16),
            jax.ShapeDtypeStruct((eig_count, size), F32),
        ],
        cost_estimate=pl.CostEstimate(flops=10**9, bytes_accessed=7 * 2**20, transcendentals=0),
        name="nodes",
    )(ids, eig_own, *returned, w_query, w_key, w_value)

    grad_proj, grad_weight = pl.pallas_call(
        functools.partial(final_kernel, rest),
        grid=(4,),
        in_specs=[
            pl.BlockSpec((1, width, target), lambda a: (a, 0, 0)),
            whole(eig_weight.shape),
        ]
        + [pl.BlockSpec((width, target), lambda a: (a, 0))] * (rest - 1)
        + [pl.BlockSpec((16, target), lambda a: (4 * width // 16, 0))] * (rest - 1),
        out_specs=[
            pl.BlockSpec((1, target, width), lambda a: (a, 0, 0)),
            whole(eig_weight.shape),
        ],
        out_shape=[
            jax.ShapeDtypeStruct((4, target, width), F32),
            jax.ShapeDtypeStruct(eig_weight.shape, F32),
        ],
        cost_estimate=pl.CostEstimate(flops=10**6, bytes_accessed=2 * 2**20, transcendentals=0),
        name="final",
    )(own_sum, gw_pair, *pieces, *pieces)
    return (grad_rows[None], grad_eig[None], grad_weight, grad_proj)


def solution(mesh):
    placed = (
        P("clus", "node", None),
        P("clus", "node", None),
        P(),
        P(),
        P(),
        P(),
        P("clus", None, None),
        P("node", None),
        P("clus", "node", None, None),
    )
    return jax.shard_map(
        body,
        mesh=mesh,
        in_specs=placed,
        out_specs=(
            P("clus", "node", None),
            P("clus", None, "node"),
            P("node", None),
            P(None, "clus", "node"),
        ),
        check_vma=False,
    )
```

```python
import functools
import math

import jax
import jax.numpy as jnp
from jax import lax
from jax.experimental import pallas as pl
from jax.experimental.pallas import tpu as pltpu
from jax.sharding import PartitionSpec as P


BF16 = jnp.bfloat16
F32 = jnp.float32
LIMIT = pltpu.CompilerParams(vmem_limit_bytes=32 * 2**20)


def mm(a, b):
    return jnp.dot(a, b, preferred_element_type=F32)


def take(value, axis, step, size):
    if size & (size - 1) == 0:
        pairs = [(i, i ^ step) for i in range(size)]
    else:
        pairs = [((i + step) % size, i) for i in range(size)]
    return lax.ppermute(value, axis, pairs)


def give(value, axis, step, size):
    if size & (size - 1) == 0:
        return take(value, axis, step, size)
    return lax.ppermute(value, axis, [(i, (i + step) % size) for i in range(size)])


def whole(shape):
    return pl.BlockSpec(shape, lambda *_: (0,) * len(shape))


def column_blocks(weight, width):
    model = weight.shape[0]
    if width % 128 == 0:
        return weight, lambda at: pl.BlockSpec((model, width), lambda *g: (0, at(*g)))
    parts = weight.reshape(model, -1, width).transpose(1, 0, 2)
    return parts, lambda at: pl.BlockSpec((None, model, width), lambda *g: (at(*g), 0, 0))


def out_grad_kernel(count, ids_ref, rows_ref, w_ref, *out_refs):
    step = pl.program_id(0)
    value = mm(rows_ref[...], w_ref[...]).astype(BF16)
    for s in range(count):

        @pl.when(step == s)
        def _(s=s):
            out_refs[s][...] = value


def attention_kernel(scale, heads, head_size, blocks, ids_ref, mask_ref, *refs):
    row_refs, d_refs = refs[:blocks], refs[blocks : 2 * blocks]
    refs = refs[2 * blocks :]
    wq_ref, wk_ref, wv_ref, eig_ref, lam_ref, lam_t_ref = refs[:6]
    grads_ref, eig_out, gw_ref = refs[6:9]
    ret_refs = refs[9 : 9 + blocks]
    (kw, qe, qn, kt, vn, vt, dn, dt, eig_t, acc_k, acc_v, eig_acc) = refs[9 + blocks :]
    head, block = pl.program_id(0), pl.program_id(1)
    last_head, last_block = pl.num_programs(0) - 1, pl.num_programs(1) - 1
    eig_count, nodes = eig_ref.shape
    width = heads * head_size
    size = nodes // blocks
    cols = qe.shape[3]
    tile_count = mask_ref.shape[1]
    tile = nodes // tile_count
    per = tile_count // blocks

    @pl.when((head == 0) & (block == 0))
    def _():
        parts = []
        for s in range(blocks):
            at = pl.multiple_of(ids_ref[s] * size, size)
            parts.append(eig_ref[:, pl.ds(at, size)])
        eig = jnp.concatenate(parts, axis=1)
        turned = eig.T
        eig_t[...] = turned
        rows = jnp.concatenate([r[...] for r in row_refs], axis=0)
        query = mm(rows, wq_ref[...]).astype(BF16)
        query_t = (query.astype(F32) * scale).astype(BF16).T
        keys = mm(rows, wk_ref[...]).astype(BF16)
        keys_t = keys.T
        values = mm(rows, wv_ref[...]).astype(BF16)
        values_t = values.T
        d_att = jnp.concatenate([r[...] for r in d_refs], axis=0)
        d_att_t = d_att.T
        for h in range(heads):
            part = slice(h * head_size, (h + 1) * head_size)
            weighted_t = (turned.astype(F32) * lam_ref[h : h + 1, :]).astype(BF16)
            kw[h] = jnp.concatenate([keys[:, part], weighted_t], axis=1)
            qn[h] = jnp.concatenate([query[:, part], turned], axis=1)
            kt[h] = jnp.concatenate([keys_t[part], eig], axis=0)
            vn[h] = values[:, part]
            vt[h] = values_t[part]
            dn[h] = d_att[:, part]
            for b in range(nodes // cols):
                here = slice(b * cols, (b + 1) * cols)
                qe[h, b] = jnp.concatenate([query_t[part, here], eig[:, here]], axis=0)
                dt[h, b] = d_att_t[part, here]
        eig_acc[...] = jnp.zeros_like(eig_acc)

    lane = lax.broadcasted_iota(jnp.int32, (eig_count, heads), 1)
    lam = jnp.sum(jnp.where(lane == head, lam_t_ref[...], 0.0), axis=1, keepdims=True)
    at = pl.multiple_of(block * cols, cols)
    here = pl.ds(at, cols)
    scores = mm(kw[head], qe[head, block])
    tiles_here = cols // tile
    columns = []
    for i in range(tiles_here):
        i_tile = block * tiles_here + i
        i_at = ids_ref[i_tile // per] * per + i_tile % per
        rows = []
        for j in range(tile_count):
            j_at = ids_ref[j // per] * per + j % per
            part = scores[j * tile : (j + 1) * tile, i * tile : (i + 1) * tile]
            rows.append(jnp.where(mask_ref[head, i_at, j_at] > 0, part, -jnp.inf))
        columns.append(jnp.concatenate(rows, axis=0))
    masked = jnp.concatenate(columns, axis=1)
    top = jnp.max(masked, axis=0, keepdims=True)
    raised = jnp.exp(masked - top)
    total = jnp.sum(raised, axis=0, keepdims=True)
    prob = raised * (1.0 / total)
    half = prob.astype(BF16)
    first = pl.multiple_of(head * head_size, head_size)
    grads_ref[pl.ds(3 * width + first, head_size), here] = mm(vt[head], half).astype(BF16)
    dprob = mm(vn[head], dt[head, block])
    delta = jnp.sum(prob * dprob, axis=0, keepdims=True)
    dscore = (prob * (dprob - delta)).astype(BF16)
    left = mm(kt[head], dscore)
    grads_ref[pl.ds(first, head_size), here] = (left[:head_size] * scale).astype(BF16)
    eig_acc[:, here] += lam * left[head_size:]
    right = mm(dscore, qn[head, here, :])
    value = mm(half, dn[head, here, :])

    @pl.when(block == 0)
    def _():
        acc_k[...] = right
        acc_v[...] = value

    @pl.when(block > 0)
    def _():
        acc_k[...] += right
        acc_v[...] += value

    @pl.when(block == last_block)
    def _():
        full = acc_k[...]
        flat = full.T
        grads_ref[pl.ds(width + first, head_size), :] = (flat[:head_size] * scale).astype(BF16)
        eig_acc[...] += lam * flat[head_size:]
        gw_ref[pl.ds(head, 1), :] = jnp.sum(
            eig_t[...].astype(F32) * full[:, head_size:], axis=0, keepdims=True
        )
        grads_ref[pl.ds(2 * width + first, head_size), :] = acc_v[...].T.astype(BF16)

    @pl.when((block == last_block) & (head == last_head))
    def _():
        eig_out[...] = eig_acc[:, :size]
        for b in range(blocks):
            part = slice(b * size, (b + 1) * size)
            ret_refs[b][: 3 * width] = grads_ref[: 3 * width, part]
            ret_refs[b][3 * width :] = eig_acc[:, part].astype(BF16)


def terms_kernel(base, nodes_blocks, target, ids_ref, *refs):
    row_refs, cot_refs = refs[:nodes_blocks], refs[nodes_blocks : 2 * nodes_blocks]
    grads_ref, out_ref = refs[2 * nodes_blocks :]
    count, _, width, _ = out_ref.shape

    def columns(ref, index):
        if target % 128 == 0:
            return ref[:, pl.ds(pl.multiple_of(index * target, target), target)]
        fit = 128 // target
        both = ref[:, pl.ds(pl.multiple_of(index // fit * 128, 128), 128)]
        found = both[:, :target]
        for part in range(1, fit):
            here = both[:, part * target : (part + 1) * target]
            found = jnp.where(index % fit == part, here, found)
        return found

    def right_of(pieces, at):
        return jnp.concatenate(
            [jnp.concatenate([columns(ref, a) for ref in pieces], axis=0) for a in at], axis=1
        )

    group = 2 if count % 2 == 0 else 1
    for start in range(0, count, group):
        at = [ids_ref[base + start + i] for i in range(group)]
        first = mm(grads_ref[: 3 * width], right_of(row_refs, at)).astype(BF16)
        second = mm(grads_ref[3 * width :], right_of(cot_refs, at)).astype(BF16)
        for i in range(group):
            lanes = slice(i * target, (i + 1) * target)
            for a in range(3):
                out_ref[start + i, a] = first[a * width : (a + 1) * width, lanes]
            out_ref[start + i, 3] = second[:, lanes]


def pair_kernel(count, keep_ref, got_ref, gw_ref, gw_got_ref, own_ref, gw_out, *piece_refs):
    _, terms, width, target = keep_ref.shape
    sums = gw_ref[...] + gw_got_ref[...]
    high = sums.astype(BF16)
    low = (sums - high.astype(F32)).astype(BF16)
    rows, lanes = sums.shape
    base = terms * width
    gw_out[...] = sums
    own_ref[...] = keep_ref[0].astype(F32) + got_ref[0].astype(F32)
    for s in range(1, count):
        ref = piece_refs[s - 1]
        total = keep_ref[s].astype(F32) + got_ref[s].astype(F32)
        for a in range(terms):
            ref[a * width : (a + 1) * width] = total[a].astype(BF16)
        ref[base:] = jnp.zeros((ref.shape[0] - base, target), BF16)
        ref[base : base + rows, :lanes] = high
        ref[base + 8 : base + 8 + rows, :lanes] = low


def final_kernel(count, own_ref, gw_ref, *refs):
    piece_refs = refs[: count - 1]
    out_ref, gw_out = refs[count - 1 :]
    terms, width, _ = own_ref.shape
    for a in range(terms):
        total = own_ref[a]
        for r in piece_refs:
            total += r[a * width : (a + 1) * width].astype(F32)
        out_ref[a] = total.T
    sums = gw_ref[...]
    rows, lanes = sums.shape
    base = terms * width
    for r in piece_refs:
        sums += r[base : base + rows, :lanes].astype(F32)
        sums += r[base + 8 : base + 8 + rows, :lanes].astype(F32)
    gw_out[...] = sums


def nodes_kernel(blocks, width, ids_ref, eig_ref, *refs):
    ret_refs = refs[:blocks]
    w_refs = refs[blocks : blocks + 3]
    out_ref, eig_out, joined = refs[blocks + 3 :]

    @pl.when(pl.program_id(0) == 0)
    def _():
        total = eig_ref[...]
        for s in range(blocks):
            at = pl.multiple_of(ids_ref[s] * width, width)
            for a in range(3):
                joined[a, pl.ds(at, width)] = ret_refs[s][a * width : (a + 1) * width]
            if s > 0:
                total += ret_refs[s][3 * width :].astype(F32)
        eig_out[...] = total

    total = mm(w_refs[0][...], joined[0])
    total += mm(w_refs[1][...], joined[1])
    total += mm(w_refs[2][...], joined[2])
    out_ref[...] = total.T.astype(BF16)


def body(node_feats, cotangent, w_query, w_key, w_value, w_out, eigvec, eig_weight, block_mask):
    node_size = lax.axis_size("node")
    clus_size = lax.axis_size("clus")
    node_me = lax.axis_index("node")
    clus_me = lax.axis_index("clus")
    own_rows, own_cot = node_feats[0], cotangent[0]
    size, model = own_rows.shape
    heads, eig_count = eig_weight.shape
    nodes = size * node_size
    width = model // node_size
    head_size = width // heads
    scale = head_size ** (-0.5)
    assert math.frexp(scale)[0] == 0.5
    assert clus_size & (clus_size - 1) == 0
    block = nodes
    while block * nodes > 512 * 512 and block > 128:
        block //= 2
    far_first = [s for s in range(node_size - 1, 0, -1)]

    rest = clus_size // 2
    order = jnp.arange(node_size, dtype=jnp.int32)
    order = order ^ node_me if node_size & (node_size - 1) == 0 else (order + node_me) % node_size
    slots = jnp.arange(clus_size, dtype=jnp.int32)
    slots = (2 * (slots % rest) + jnp.where(slots < rest, 1, 0)) ^ clus_me
    ids = jnp.concatenate([order, slots])

    rows = [own_rows] + [None] * (node_size - 1)
    for s in far_first:
        rows[s] = take(own_rows, "node", s, node_size)

    weight, spec = column_blocks(w_out, width)
    d_parts = pl.pallas_call(
        functools.partial(out_grad_kernel, node_size),
        grid_spec=pltpu.PrefetchScalarGridSpec(
            num_scalar_prefetch=1,
            grid=(node_size,),
            in_specs=[whole((size, model)), spec(lambda s, ids: ids[s])],
            out_specs=[whole((size, width))] * node_size,
        ),
        out_shape=[jax.ShapeDtypeStruct((size, width), BF16)] * node_size,
        cost_estimate=pl.CostEstimate(flops=3 * 10**8, bytes_accessed=3 * 2**20, transcendentals=0),
        compiler_params=LIMIT,
        name="out_grad",
    )(ids, own_cot, weight)
    d_att = [d_parts[0]] + [None] * (node_size - 1)
    for s in far_first:
        d_att[s] = give(d_parts[s], "node", s, node_size)
    cots = [own_cot] + [None] * (node_size - 1)
    for s in far_first:
        cots[s] = take(own_cot, "node", s, node_size)

    steps = nodes // block
    both = head_size + eig_count
    weights = [column_blocks(w, width) for w in (w_query, w_key, w_value)]
    results = pl.pallas_call(
        functools.partial(attention_kernel, scale, heads, head_size, node_size),
        grid_spec=pltpu.PrefetchScalarGridSpec(
            num_scalar_prefetch=2,
            grid=(heads, steps),
            in_specs=[whole((size, model))] * node_size
            + [whole((size, width))] * node_size
            + [w[1](lambda h, b, ids, mask: ids[0]) for w in weights]
            + [
                whole((eig_count, nodes)),
                whole((heads, eig_count)),
                whole((eig_count, heads)),
            ],
            out_specs=[
                whole((4 * width, nodes)),
                whole((eig_count, size)),
                whole((heads, eig_count)),
            ]
            + [whole((3 * width + eig_count, size))] * node_size,
            scratch_shapes=[
                pltpu.VMEM((heads, nodes, both), BF16),
                pltpu.VMEM((heads, steps, both, block), BF16),
                pltpu.VMEM((heads, nodes, both), BF16),
                pltpu.VMEM((heads, both, nodes), BF16),
                pltpu.VMEM((heads, nodes, head_size), BF16),
                pltpu.VMEM((heads, head_size, nodes), BF16),
                pltpu.VMEM((heads, nodes, head_size), BF16),
                pltpu.VMEM((heads, steps, head_size, block), BF16),
                pltpu.VMEM((nodes, eig_count), BF16),
                pltpu.VMEM((nodes, both), F32),
                pltpu.VMEM((nodes, head_size), F32),
                pltpu.VMEM((eig_count, nodes), F32),
            ],
        ),
        out_shape=[
            jax.ShapeDtypeStruct((4 * width, nodes), BF16),
            jax.ShapeDtypeStruct((eig_count, size), F32),
            jax.ShapeDtypeStruct((heads, eig_count), F32),
        ]
        + [jax.ShapeDtypeStruct((3 * width + eig_count, size), BF16)] * node_size,
        cost_estimate=pl.CostEstimate(
            flops=8 * 10**9, bytes_accessed=8 * 2**20, transcendentals=10**6
        ),
        compiler_params=LIMIT,
        name="attention",
    )(
        ids,
        block_mask[0],
        *rows,
        *d_att,
        *[w[0] for w in weights],
        eigvec[0],
        eig_weight,
        eig_weight.T,
    )
    grads_t, eig_own, gw_own = results[:3]
    parts = results[3:]

    target = model // clus_size
    smem, vmem = pl.BlockSpec(memory_space=pltpu.SMEM), pl.BlockSpec(memory_space=pltpu.VMEM)

    def terms(base):
        return pl.pallas_call(
            functools.partial(terms_kernel, node_size + base, node_size, target),
            in_specs=[smem] + [vmem] * (2 * node_size + 1),
            out_specs=vmem,
            out_shape=jax.ShapeDtypeStruct((rest, 4, width, target), BF16),
            cost_estimate=pl.CostEstimate(
                flops=2 * 10**9, bytes_accessed=2 * 2**20, transcendentals=0
            ),
            compiler_params=LIMIT,
        )(ids, *rows, *cots, grads_t)

    give_half = terms(0)
    gw_got = give(gw_own, "clus", 1, clus_size)
    got_half = give(give_half, "clus", 1, clus_size)
    keep_half = terms(rest)

    piece_rows = 4 * width + 16
    paired = pl.pallas_call(
        functools.partial(pair_kernel, rest),
        in_specs=[vmem] * 4,
        out_specs=[vmem] * (rest + 1),
        out_shape=[
            jax.ShapeDtypeStruct((4, width, target), F32),
            jax.ShapeDtypeStruct(eig_weight.shape, F32),
        ]
        + [jax.ShapeDtypeStruct((piece_rows, target), BF16)] * (rest - 1),
        cost_estimate=pl.CostEstimate(flops=10**6, bytes_accessed=4 * 2**20, transcendentals=0),
        compiler_params=LIMIT,
        name="pair",
    )(keep_half, got_half, gw_own, gw_got)
    own_sum, gw_pair = paired[:2]
    pieces = [None] * (rest - 1)
    for s in range(rest - 1, 0, -1):
        pieces[s - 1] = give(paired[1 + s], "clus", 2 * s, clus_size)

    returned = [parts[0]] + [None] * (node_size - 1)
    for s in far_first:
        returned[s] = give(parts[s], "node", s, node_size)

    chunk = min(256, model)
    grad_rows, grad_eig = pl.pallas_call(
        functools.partial(nodes_kernel, node_size, width),
        grid_spec=pltpu.PrefetchScalarGridSpec(
            num_scalar_prefetch=1,
            grid=(model // chunk,),
            in_specs=[whole((eig_count, size))]
            + [whole((3 * width + eig_count, size))] * node_size
            + [pl.BlockSpec((chunk, model), lambda g, *_: (g, 0))] * 3,
            out_specs=[
                pl.BlockSpec((size, chunk), lambda g, *_: (0, g)),
                whole((eig_count, size)),
            ],
            scratch_shapes=[pltpu.VMEM((3, model, size), BF16)],
        ),
        out_shape=[
            jax.ShapeDtypeStruct((size, model), BF16),
            jax.ShapeDtypeStruct((eig_count, size), F32),
        ],
        cost_estimate=pl.CostEstimate(flops=10**9, bytes_accessed=7 * 2**20, transcendentals=0),
        compiler_params=LIMIT,
        name="nodes",
    )(ids, eig_own, *returned, w_query, w_key, w_value)

    grad_proj, grad_weight = pl.pallas_call(
        functools.partial(final_kernel, rest),
        in_specs=[vmem] * (rest + 1),
        out_specs=[vmem] * 2,
        out_shape=[
            jax.ShapeDtypeStruct((4, target, width), F32),
            jax.ShapeDtypeStruct(eig_weight.shape, F32),
        ],
        cost_estimate=pl.CostEstimate(flops=10**6, bytes_accessed=2 * 2**20, transcendentals=0),
        compiler_params=LIMIT,
        name="final",
    )(own_sum, gw_pair, *pieces)
    return (grad_rows[None], grad_eig[None], grad_weight, grad_proj)


def solution(mesh):
    placed = (
        P("clus", "node", None),
        P("clus", "node", None),
        P(),
        P(),
        P(),
        P(),
        P("clus", None, None),
        P("node", None),
        P("clus", "node", None, None),
    )
    return jax.shard_map(
        body,
        mesh=mesh,
        in_specs=placed,
        out_specs=(
            P("clus", "node", None),
            P("clus", None, "node"),
            P("node", None),
            P(None, "clus", "node"),
        ),
        check_vma=False,
    )
```

```python
import functools
import math

import jax
import jax.numpy as jnp
from jax import lax
from jax.experimental import pallas as pl
from jax.experimental.pallas import tpu as pltpu
from jax.sharding import PartitionSpec as P


BF16 = jnp.bfloat16
F32 = jnp.float32
LIMIT = pltpu.CompilerParams(vmem_limit_bytes=32 * 2**20)


def mm(a, b):
    return jnp.dot(a, b, preferred_element_type=F32)


def take(value, axis, step, size):
    if size & (size - 1) == 0:
        pairs = [(i, i ^ step) for i in range(size)]
    else:
        pairs = [((i + step) % size, i) for i in range(size)]
    return lax.ppermute(value, axis, pairs)


def give(value, axis, step, size):
    if size & (size - 1) == 0:
        return take(value, axis, step, size)
    return lax.ppermute(value, axis, [(i, (i + step) % size) for i in range(size)])


def column_blocks(weight, width):
    if width % 128 == 0:
        return weight
    return weight.reshape(weight.shape[0], -1, width).transpose(1, 0, 2)


def column_copy(ref, at, width, target, sem):
    if len(ref.shape) == 3:
        return pltpu.make_async_copy(ref.at[at], target, sem)
    at = pl.multiple_of(at * width, width)
    return pltpu.make_async_copy(ref.at[:, pl.ds(at, width)], target, sem)


def out_grad_kernel(count, width, ids_ref, rows_ref, w_ref, *refs):
    out_refs, (held, sems) = refs[:count], refs[count:]
    order = list(range(count - 1, -1, -1))
    copies = {s: column_copy(w_ref, ids_ref[s], width, held.at[s], sems.at[s]) for s in order}
    for s in order:
        copies[s].start()
    for s in order:
        copies[s].wait()
        out_refs[s][...] = mm(rows_ref[...], held[s]).astype(BF16)


def weights_kernel(width, ids_ref, *refs):
    sources, targets, sems = refs[:3], refs[3:6], refs[6]
    copies = [
        column_copy(sources[a], ids_ref[0], width, targets[a], sems.at[a]) for a in range(3)
    ]
    for c in copies:
        c.start()
    for c in copies:
        c.wait()


def attention_kernel(scale, heads, head_size, blocks, ids_ref, mask_ref, *refs):
    row_refs, d_refs = refs[:blocks], refs[blocks : 2 * blocks]
    refs = refs[2 * blocks :]
    wq_ref, wk_ref, wv_ref, eig_ref, lam_ref, lam_t_ref = refs[:6]
    grads_ref, eig_out, gw_ref = refs[6:9]
    ret_refs = refs[9 : 9 + blocks]
    (kw, qe, qn, kt, vn, vt, dn, dt, eig_t, eig_acc) = refs[9 + blocks :]
    eig_count, nodes = eig_ref.shape
    width = heads * head_size
    size = nodes // blocks
    steps, cols = qe.shape[1], qe.shape[3]
    tile_count = mask_ref.shape[1]
    tile = nodes // tile_count
    per = tile_count // blocks

    parts = []
    for s in range(blocks):
        parts.append(eig_ref[:, pl.ds(pl.multiple_of(ids_ref[s] * size, size), size)])
    eig = jnp.concatenate(parts, axis=1)
    turned = eig.T
    eig_t[...] = turned
    rows = jnp.concatenate([r[...] for r in row_refs], axis=0)
    query = mm(rows, wq_ref[...]).astype(BF16)
    query_t = (query.astype(F32) * scale).astype(BF16).T
    keys = mm(rows, wk_ref[...]).astype(BF16)
    keys_t = keys.T
    values = mm(rows, wv_ref[...]).astype(BF16)
    values_t = values.T
    d_att = jnp.concatenate([r[...] for r in d_refs], axis=0)
    d_att_t = d_att.T
    for h in range(heads):
        part = slice(h * head_size, (h + 1) * head_size)
        weighted_t = (turned.astype(F32) * lam_ref[h : h + 1, :]).astype(BF16)
        kw[h] = jnp.concatenate([keys[:, part], weighted_t], axis=1)
        qn[h] = jnp.concatenate([query[:, part], turned], axis=1)
        kt[h] = jnp.concatenate([keys_t[part], eig], axis=0)
        vn[h] = values[:, part]
        vt[h] = values_t[part]
        dn[h] = d_att[:, part]
        for b in range(steps):
            here = slice(b * cols, (b + 1) * cols)
            qe[h, b] = jnp.concatenate([query_t[part, here], eig[:, here]], axis=0)
            dt[h, b] = d_att_t[part, here]
    eig_acc[...] = jnp.zeros_like(eig_acc)
    lane = lax.broadcasted_iota(jnp.int32, (eig_count, heads), 1)

    def one_block(head, lam, first, block, totals):
        here = pl.ds(pl.multiple_of(block * cols, cols), cols)
        scores = mm(kw[head], qe[head, block])
        tiles_here = cols // tile
        columns = []
        for i in range(tiles_here):
            i_tile = block * tiles_here + i
            i_at = ids_ref[i_tile // per] * per + i_tile % per
            found = []
            for j in range(tile_count):
                j_at = ids_ref[j // per] * per + j % per
                part = scores[j * tile : (j + 1) * tile, i * tile : (i + 1) * tile]
                found.append(jnp.where(mask_ref[head, i_at, j_at] > 0, part, -jnp.inf))
            columns.append(jnp.concatenate(found, axis=0))
        masked = jnp.concatenate(columns, axis=1)
        top = jnp.max(masked, axis=0, keepdims=True)
        raised = jnp.exp(masked - top)
        total = jnp.sum(raised, axis=0, keepdims=True)
        prob = raised * (1.0 / total)
        half = prob.astype(BF16)
        grads_ref[pl.ds(3 * width + first, head_size), here] = mm(vt[head], half).astype(BF16)
        dprob = mm(vn[head], dt[head, block])
        delta = jnp.sum(prob * dprob, axis=0, keepdims=True)
        dscore = (prob * (dprob - delta)).astype(BF16)
        left = mm(kt[head], dscore)
        grads_ref[pl.ds(first, head_size), here] = (left[:head_size] * scale).astype(BF16)
        eig_acc[:, here] += lam * left[head_size:]
        right = mm(dscore, qn[head, here, :])
        value = mm(half, dn[head, here, :])
        if totals is None:
            return right, value
        return totals[0] + right, totals[1] + value

    def one_head(head, _):
        lam = jnp.sum(jnp.where(lane == head, lam_t_ref[...], 0.0), axis=1, keepdims=True)
        first = pl.multiple_of(head * head_size, head_size)
        totals = one_block(head, lam, first, 0, None)
        if steps > 1:
            totals = lax.fori_loop(
                1, steps, lambda b, t: one_block(head, lam, first, b, t), totals
            )
        full, value = totals
        flat = full.T
        grads_ref[pl.ds(width + first, head_size), :] = (flat[:head_size] * scale).astype(BF16)
        eig_acc[...] += lam * flat[head_size:]
        gw_ref[pl.ds(head, 1), :] = jnp.sum(
            eig_t[...].astype(F32) * full[:, head_size:], axis=0, keepdims=True
        )
        grads_ref[pl.ds(2 * width + first, head_size), :] = value.T.astype(BF16)
        return 0

    lax.fori_loop(0, heads, one_head, 0)
    eig_out[...] = eig_acc[:, :size]
    for b in range(blocks):
        part = slice(b * size, (b + 1) * size)
        ret_refs[b][: 3 * width] = grads_ref[: 3 * width, part]
        ret_refs[b][3 * width :] = eig_acc[:, part].astype(BF16)


def terms_kernel(base, nodes_blocks, target, ids_ref, *refs):
    row_refs, cot_refs = refs[:nodes_blocks], refs[nodes_blocks : 2 * nodes_blocks]
    grads_ref, out_ref = refs[2 * nodes_blocks :]
    count, _, width, _ = out_ref.shape

    def columns(ref, index):
        if target % 128 == 0:
            return ref[:, pl.ds(pl.multiple_of(index * target, target), target)]
        fit = 128 // target
        both = ref[:, pl.ds(pl.multiple_of(index // fit * 128, 128), 128)]
        found = both[:, :target]
        for part in range(1, fit):
            here = both[:, part * target : (part + 1) * target]
            found = jnp.where(index % fit == part, here, found)
        return found

    def right_of(pieces, at):
        return jnp.concatenate(
            [jnp.concatenate([columns(ref, a) for ref in pieces], axis=0) for a in at], axis=1
        )

    group = 2 if count % 2 == 0 else 1
    for start in range(0, count, group):
        at = [ids_ref[base + start + i] for i in range(group)]
        first = mm(grads_ref[: 3 * width], right_of(row_refs, at)).astype(BF16)
        second = mm(grads_ref[3 * width :], right_of(cot_refs, at)).astype(BF16)
        for i in range(group):
            lanes = slice(i * target, (i + 1) * target)
            for a in range(3):
                out_ref[start + i, a] = first[a * width : (a + 1) * width, lanes]
            out_ref[start + i, 3] = second[:, lanes]


def pair_kernel(count, near, keep_ref, got_ref, gw_ref, gw_got_ref, *refs):
    near_give, near_keep, own_ref, gw_out = refs[:4]
    piece_refs = refs[4:]
    _, terms, width, target = keep_ref.shape
    sums = gw_ref[...] + gw_got_ref[...]
    high = sums.astype(BF16)
    low = (sums - high.astype(F32)).astype(BF16)
    rows, lanes = sums.shape
    base = (terms - near) * width
    gw_out[...] = sums
    for s in range(count):
        total = keep_ref[s].astype(F32) + got_ref[s].astype(F32)
        if s % 2 == 0:
            near_keep[s // 2] = total[:near]
        else:
            near_give[s // 2] = total[:near].astype(BF16)
        if s == 0:
            own_ref[...] = total[near:]
            continue
        ref = piece_refs[s - 1]
        for a in range(terms - near):
            ref[a * width : (a + 1) * width] = total[near + a].astype(BF16)
        ref[base:] = jnp.zeros((ref.shape[0] - base, target), BF16)
        ref[base : base + rows, :lanes] = high
        ref[base + 8 : base + 8 + rows, :lanes] = low


def near_kernel(keep_ref, got_ref, own_ref, *piece_refs):
    own_ref[...] = keep_ref[0] + got_ref[0].astype(F32)
    for s, ref in enumerate(piece_refs):
        ref[...] = (keep_ref[s + 1] + got_ref[s + 1].astype(F32)).astype(BF16)


def final_kernel(near_count, near_own, own_ref, gw_ref, *refs):
    near_refs, piece_refs, (out_ref, gw_out) = refs[:near_count], refs[near_count:-2], refs[-2:]
    near, width, _ = near_own.shape
    terms = own_ref.shape[0]
    for a in range(near):
        total = near_own[a]
        for r in near_refs:
            total += r[a].astype(F32)
        out_ref[a] = total.T
    for a in range(terms):
        total = own_ref[a]
        for r in piece_refs:
            total += r[a * width : (a + 1) * width].astype(F32)
        out_ref[near + a] = total.T
    sums = gw_ref[...]
    rows, lanes = sums.shape
    base = terms * width
    for r in piece_refs:
        sums += r[base : base + rows, :lanes].astype(F32)
        sums += r[base + 8 : base + 8 + rows, :lanes].astype(F32)
    gw_out[...] = sums


def nodes_kernel(blocks, width, ids_ref, eig_ref, *refs):
    ret_refs = refs[:blocks]
    w_refs = refs[blocks : blocks + 3]
    out_ref, eig_out, joined = refs[blocks + 3 :]
    total = eig_ref[...]
    for s in range(blocks):
        at = pl.multiple_of(ids_ref[s] * width, width)
        for a in range(3):
            joined[a, pl.ds(at, width)] = ret_refs[s][a * width : (a + 1) * width]
        if s > 0:
            total += ret_refs[s][3 * width :].astype(F32)
    eig_out[...] = total
    chunk = min(256, out_ref.shape[1])
    for c in range(0, out_ref.shape[1], chunk):
        part = slice(c, c + chunk)
        total = mm(w_refs[0][part], joined[0])
        total += mm(w_refs[1][part], joined[1])
        total += mm(w_refs[2][part], joined[2])
        out_ref[:, part] = total.T.astype(BF16)


def body(node_feats, cotangent, w_query, w_key, w_value, w_out, eigvec, eig_weight, block_mask):
    node_size = lax.axis_size("node")
    clus_size = lax.axis_size("clus")
    node_me = lax.axis_index("node")
    clus_me = lax.axis_index("clus")
    own_rows, own_cot = node_feats[0], cotangent[0]
    size, model = own_rows.shape
    heads, eig_count = eig_weight.shape
    nodes = size * node_size
    width = model // node_size
    head_size = width // heads
    scale = head_size ** (-0.5)
    assert math.frexp(scale)[0] == 0.5
    assert clus_size & (clus_size - 1) == 0
    block = nodes
    while block * nodes > 512 * 512 and block > 128:
        block //= 2
    far_first = [s for s in range(node_size - 1, 0, -1)]

    rest = clus_size // 2
    order = jnp.arange(node_size, dtype=jnp.int32)
    order = order ^ node_me if node_size & (node_size - 1) == 0 else (order + node_me) % node_size
    slots = jnp.arange(clus_size, dtype=jnp.int32)
    slots = (2 * (slots % rest) + jnp.where(slots < rest, 1, 0)) ^ clus_me
    ids = jnp.concatenate([order, slots])

    rows = [own_rows] + [None] * (node_size - 1)
    for s in far_first:
        rows[s] = take(own_rows, "node", s, node_size)

    smem, vmem = pl.BlockSpec(memory_space=pltpu.SMEM), pl.BlockSpec(memory_space=pltpu.VMEM)
    hbm = pl.BlockSpec(memory_space=pltpu.HBM)

    def call(kernel, in_specs, out_shapes, operands, flops, moved, scratch=()):
        return pl.pallas_call(
            kernel,
            in_specs=in_specs,
            out_specs=[vmem] * len(out_shapes),
            out_shape=[jax.ShapeDtypeStruct(*o) for o in out_shapes],
            scratch_shapes=scratch,
            cost_estimate=pl.CostEstimate(flops=flops, bytes_accessed=moved, transcendentals=0),
            compiler_params=LIMIT,
        )(*operands)

    d_parts = call(
        functools.partial(out_grad_kernel, node_size, width),
        [smem, vmem, hbm],
        [((size, width), BF16)] * node_size,
        (ids, own_cot, pltpu.with_memory_space_constraint(column_blocks(w_out, width), pltpu.HBM)),
        3 * 10**8,
        3 * 2**20,
        [pltpu.VMEM((node_size, model, width), BF16), pltpu.SemaphoreType.DMA((node_size,))],
    )
    d_att = [d_parts[0]] + [None] * (node_size - 1)
    for s in far_first:
        d_att[s] = give(d_parts[s], "node", s, node_size)
    cots = [own_cot] + [None] * (node_size - 1)
    for s in far_first:
        cots[s] = take(own_cot, "node", s, node_size)

    weights = call(
        functools.partial(weights_kernel, width),
        [smem] + [hbm] * 3,
        [((model, width), BF16)] * 3,
        (ids, *[pltpu.with_memory_space_constraint(column_blocks(w, width), pltpu.HBM) for w in (w_query, w_key, w_value)]),
        0,
        3 * 2**20,
        [pltpu.SemaphoreType.DMA((3,))],
    )

    steps = nodes // block
    both = head_size + eig_count
    results = call(
        functools.partial(attention_kernel, scale, heads, head_size, node_size),
        [smem, smem] + [vmem] * (2 * node_size + 6),
        [((4 * width, nodes), BF16), ((eig_count, size), F32), ((heads, eig_count), F32)]
        + [((3 * width + eig_count, size), BF16)] * node_size,
        (ids, block_mask[0], *rows, *d_att, *weights, eigvec[0], eig_weight, eig_weight.T),
        8 * 10**9,
        8 * 2**20,
        [
            pltpu.VMEM((heads, nodes, both), BF16),
            pltpu.VMEM((heads, steps, both, block), BF16),
            pltpu.VMEM((heads, nodes, both), BF16),
            pltpu.VMEM((heads, both, nodes), BF16),
            pltpu.VMEM((heads, nodes, head_size), BF16),
            pltpu.VMEM((heads, head_size, nodes), BF16),
            pltpu.VMEM((heads, nodes, head_size), BF16),
            pltpu.VMEM((heads, steps, head_size, block), BF16),
            pltpu.VMEM((nodes, eig_count), BF16),
            pltpu.VMEM((eig_count, nodes), F32),
        ],
    )
    grads_t, eig_own, gw_own = results[:3]
    parts = results[3:]

    target = model // clus_size

    def terms(base):
        return call(
            functools.partial(terms_kernel, node_size + base, node_size, target),
            [smem] + [vmem] * (2 * node_size + 1),
            [((rest, 4, width, target), BF16)],
            (ids, *rows, *cots, grads_t),
            2 * 10**9,
            2 * 2**20,
        )[0]

    give_half = terms(0)
    gw_got = give(gw_own, "clus", 1, clus_size)
    got_half = give(give_half, "clus", 1, clus_size)
    keep_half = terms(rest)

    near, pairs = 2, rest // 2
    piece_rows = (4 - near) * width + 16
    near_give, near_keep, own_sum, gw_pair, *straight = call(
        functools.partial(pair_kernel, rest, near),
        [vmem] * 4,
        [
            ((pairs, near, width, target), BF16),
            ((pairs, near, width, target), F32),
            ((4 - near, width, target), F32),
            (eig_weight.shape, F32),
        ]
        + [((piece_rows, target), BF16)] * (rest - 1),
        (keep_half, got_half, gw_own, gw_got),
        10**6,
        4 * 2**20,
    )
    near_got = give(near_give, "clus", 2, clus_size)
    pieces = [None] * (rest - 1)
    for s in range(rest - 1, 0, -1):
        pieces[s - 1] = give(straight[s - 1], "clus", 2 * s, clus_size)
    near_own, *near_parts = call(
        near_kernel,
        [vmem] * 2,
        [((near, width, target), F32)] + [((near, width, target), BF16)] * (pairs - 1),
        (near_keep, near_got),
        10**6,
        2**20,
    )
    near_pieces = [None] * (pairs - 1)
    for s in range(pairs - 1, 0, -1):
        near_pieces[s - 1] = give(near_parts[s - 1], "clus", 4 * s, clus_size)

    returned = [parts[0]] + [None] * (node_size - 1)
    for s in far_first:
        returned[s] = give(parts[s], "node", s, node_size)

    grad_rows, grad_eig = call(
        functools.partial(nodes_kernel, node_size, width),
        [smem] + [vmem] * (node_size + 4),
        [((size, model), BF16), ((eig_count, size), F32)],
        (ids, eig_own, *returned, w_query, w_key, w_value),
        10**9,
        7 * 2**20,
        [pltpu.VMEM((3, model, size), BF16)],
    )

    grad_proj, grad_weight = call(
        functools.partial(final_kernel, pairs - 1),
        [vmem] * (3 + pairs - 1 + rest - 1),
        [((4, target, width), F32), (eig_weight.shape, F32)],
        (near_own, own_sum, gw_pair, *near_pieces, *pieces),
        10**6,
        2 * 2**20,
    )
    return (grad_rows[None], grad_eig[None], grad_weight, grad_proj)


def solution(mesh):
    placed = (
        P("clus", "node", None),
        P("clus", "node", None),
        P(),
        P(),
        P(),
        P(),
        P("clus", None, None),
        P("node", None),
        P("clus", "node", None, None),
    )
    return jax.shard_map(
        body,
        mesh=mesh,
        in_specs=placed,
        out_specs=(
            P("clus", "node", None),
            P("clus", None, "node"),
            P("node", None),
            P(None, "clus", "node"),
        ),
        check_vma=False,
    )
```

```python
import functools
import math

import jax
import jax.numpy as jnp
from jax import lax
from jax.experimental import pallas as pl
from jax.experimental.pallas import tpu as pltpu
from jax.sharding import PartitionSpec as P


BF16 = jnp.bfloat16
SPAN = 512
F32 = jnp.float32
LIMIT = pltpu.CompilerParams(vmem_limit_bytes=32 * 2**20)


def mm(a, b):
    return jnp.dot(a, b, preferred_element_type=F32)


def take(value, axis, step, size):
    if size & (size - 1) == 0:
        pairs = [(i, i ^ step) for i in range(size)]
    else:
        pairs = [((i + step) % size, i) for i in range(size)]
    return lax.ppermute(value, axis, pairs)


def give(value, axis, step, size):
    if size & (size - 1) == 0:
        return take(value, axis, step, size)
    return lax.ppermute(value, axis, [(i, (i + step) % size) for i in range(size)])


def column_blocks(weight, width):
    if width % 128 == 0:
        return weight
    return weight.reshape(weight.shape[0], -1, width).transpose(1, 0, 2)


def column_copy(ref, at, width, target, sem):
    if len(ref.shape) == 3:
        return pltpu.make_async_copy(ref.at[at], target, sem)
    at = pl.multiple_of(at * width, width)
    return pltpu.make_async_copy(ref.at[:, pl.ds(at, width)], target, sem)


def out_grad_kernel(count, width, ids_ref, rows_ref, w_ref, *refs):
    out_refs, (held, sems) = refs[:count], refs[count:]
    order = list(range(count - 1, -1, -1))
    copies = {s: column_copy(w_ref, ids_ref[s], width, held.at[s], sems.at[s]) for s in order}
    for s in order:
        copies[s].start()
    for s in order:
        copies[s].wait()
        out_refs[s][...] = mm(rows_ref[...], held[s]).astype(BF16)


def split_kernel(first_ref, second_ref, top_ref, bottom_ref):
    half = top_ref.shape[0]
    top_ref[...] = second_ref[:half]
    bottom_ref[...] = first_ref[half:]


def weights_kernel(width, calls, ids_ref, *refs):
    sources, targets, sems = refs[:3], refs[3:-1], refs[-1]
    copies = []
    for c in range(calls):
        for a in range(3):
            at = 3 * c + a
            if calls == 1:
                copies.append(column_copy(sources[a], ids_ref[0], width, targets[at], sems.at[at]))
            else:
                copies.append(
                    column_copy(
                        sources[a],
                        ids_ref[0] * calls + c,
                        width // calls,
                        targets[at],
                        sems.at[at],
                    )
                )
    for c in copies:
        c.start()
    for c in copies:
        c.wait()


def attention_kernel(scale, heads, head_size, blocks, pieces, base, last, ids_ref, mask_ref, *refs):
    row_refs, d_refs = refs[:pieces], refs[pieces : pieces + blocks]
    refs = refs[pieces + blocks :]
    wq_ref, wk_ref, wv_ref, eig_ref, lam_ref, lam_t_ref = refs[:6]
    earlier = base // heads
    prior_refs, refs = refs[6 : 6 + 2 * earlier], refs[6 + 2 * earlier :]
    grads_ref, out_ref, gw_ref = refs[:3]
    result_refs = refs[3:-5]
    qe, qn, dt, dn, left_acc = refs[-5:]
    eig_count, nodes = eig_ref.shape
    width = heads * head_size
    size = nodes // blocks
    steps, cols = qe.shape[1], qe.shape[3]
    tile_count = mask_ref.shape[1]
    tile = nodes // tile_count
    per = tile_count // blocks
    both = 2 * head_size
    assert eig_count == head_size
    groups = -(-heads // 2)

    def fit(array):
        extra = groups * both - array.shape[1]
        if extra == 0:
            return array
        return jnp.concatenate([array, jnp.zeros((array.shape[0], extra), array.dtype)], axis=1)

    parts = []
    for s in range(blocks):
        parts.append(eig_ref[:, pl.ds(pl.multiple_of(ids_ref[s] * size, size), size)])
    eig = jnp.concatenate(parts, axis=1)
    turned = jnp.concatenate([eig, eig], axis=0).T
    wide = turned.astype(F32)
    rows = jnp.concatenate([r[...] for r in row_refs], axis=0)
    query = fit(mm(rows, wq_ref[...]).astype(BF16))
    keys = fit(mm(rows, wk_ref[...]).astype(BF16))
    values = fit(mm(rows, wv_ref[...]).astype(BF16))
    first_column = base * head_size
    d_att = fit(
        jnp.concatenate([r[:, first_column : first_column + width] for r in d_refs], axis=0)
    )
    query_t = (query.astype(F32) * scale).astype(BF16).T
    keys_t = keys.T
    values_t = values.T
    d_att_t = d_att.T
    first_half = lax.broadcasted_iota(jnp.int32, (nodes, both), 1) < head_size
    first_row = lax.broadcasted_iota(jnp.int32, (1, both), 1) < head_size

    def pick(even, first, second):
        return jnp.where(first_half, first, second) if even else jnp.where(first_half, second, first)

    def stack(even, first, second):
        return jnp.concatenate([first, second] if even else [second, first], axis=0)

    for g in range(groups):
        group = slice(g * both, (g + 1) * both)
        dn[g] = d_att[:, group]
        for b in range(steps):
            here = slice(b * cols, (b + 1) * cols)
            dt[g, b] = d_att_t[group, here]
        for h in range(2 * g, min(2 * g + 2, heads)):
            even = h % 2 == 0
            part = slice(h * head_size, (h + 1) * head_size)
            qn[h] = pick(even, query[:, group], turned)
            for b in range(steps):
                here = slice(b * cols, (b + 1) * cols)
                qe[h, b] = stack(even, query_t[part, here], eig[:, here])

    def before(head, block, kw, vn):
        return mm(kw, qe[head, block]), mm(vn, dt[head // 2, block])

    def one_block(head, block, kt, vt, scores, dprob, totals):
        at = block * cols
        here = pl.ds(at if isinstance(block, int) else pl.multiple_of(at, cols), cols)
        tiles_here = cols // tile
        columns = []
        for i in range(tiles_here):
            i_tile = block * tiles_here + i
            i_at = ids_ref[i_tile // per] * per + i_tile % per
            found = []
            for j in range(tile_count):
                j_at = ids_ref[j // per] * per + j % per
                part = scores[j * tile : (j + 1) * tile, i * tile : (i + 1) * tile]
                found.append(jnp.where(mask_ref[base + head, i_at, j_at] > 0, part, -jnp.inf))
            columns.append(jnp.concatenate(found, axis=0))
        masked = jnp.concatenate(columns, axis=1)
        top = jnp.max(masked, axis=0, keepdims=True)
        raised = jnp.exp(masked - top)
        total = jnp.sum(raised, axis=0, keepdims=True)
        prob = raised * (1.0 / total)
        half = prob.astype(BF16)
        first = head * head_size
        out_ref[first : first + head_size, here] = mm(vt, half).astype(BF16)
        value = mm(half, dn[head // 2, here, :])
        delta = jnp.sum(prob * dprob, axis=0, keepdims=True)
        dscore = (prob * (dprob - delta)).astype(BF16)
        left = mm(kt, dscore)
        grads_ref[first : first + head_size, here] = (left[:head_size] * scale).astype(BF16)
        weighted = lam_t_ref[:, base + head : base + head + 1] * left[head_size:]
        if head == 0:
            left_acc[:, here] = weighted
        else:
            left_acc[:, here] += weighted
        right = mm(dscore, qn[head, here, :])
        if totals is None:
            return right, value
        return totals[0] + right, totals[1] + value

    def operands(h):
        even, g = h % 2 == 0, h // 2
        group = slice(g * both, (g + 1) * both)
        part = slice(h * head_size, (h + 1) * head_size)
        lam_row = jnp.concatenate([lam_ref[base + h : base + h + 1, :]] * 2, axis=1)
        kw = pick(even, keys[:, group], (wide * lam_row).astype(BF16))
        kt = jnp.concatenate([keys_t[part], eig], axis=0)
        vn = pick(even, values[:, group], jnp.zeros((nodes, both), BF16))
        return lam_row, kw, kt, values_t[part], vn

    unrolled = [(h, b) for h in range(heads) for b in range(steps)] if steps <= 4 else []
    ready = {}

    def prepare(at):
        if at < len(unrolled):
            h, b = unrolled[at]
            if b == 0:
                ready[h] = operands(h)
            ready[h, b] = before(h, b, ready[h][1], ready[h][4])

    def all_blocks(h):
        if unrolled:
            totals = None
            for b in range(steps):
                prepare(h * steps + b + 1)
                _, _, kt, vt, _ = ready[h]
                totals = one_block(h, b, kt, vt, *ready.pop((h, b)), totals)
            return ready[h][0], totals
        lam_row, kw, kt, vt, vn = operands(h)
        return lam_row, lax.fori_loop(
            1,
            steps,
            lambda b, t: one_block(h, b, kt, vt, *before(h, b, kw, vn), t),
            one_block(h, 0, kt, vt, *before(h, 0, kw, vn), None),
        )

    prepare(0)
    right_total = None
    for g in range(groups):
        group = slice(g * both, (g + 1) * both)
        found = []
        lam_rows = []
        for h in range(2 * g, min(2 * g + 2, heads)):
            lam_row, totals = all_blocks(h)
            lam_rows.append(lam_row)
            found.append(totals)
        if len(found) == 1:
            found.append((jnp.zeros((nodes, both), F32), jnp.zeros((nodes, both), F32)))
            lam_rows.append(jnp.zeros((1, both), F32))
        keep = min(both, width - g * both)
        key_grad = jnp.where(first_half, found[0][0], found[1][0]).T
        grads_ref[width + g * both : width + g * both + keep, :] = (
            key_grad[:keep] * scale
        ).astype(BF16)
        value_grad = jnp.where(first_half, found[0][1], found[1][1]).T
        grads_ref[2 * width + g * both : 2 * width + g * both + keep, :] = value_grad[
            :keep
        ].astype(BF16)
        right = jnp.where(first_half, found[1][0], found[0][0])
        sums = jnp.sum(wide * right, axis=0, keepdims=True)
        gw_ref[2 * g : 2 * g + 1, :] = sums[:, head_size:]
        if 2 * g + 1 < heads:
            gw_ref[2 * g + 1 : 2 * g + 2, :] = sums[:, :head_size]
        right = right * jnp.where(first_row, lam_rows[1], lam_rows[0])
        right_total = right if right_total is None else right_total + right

    flat = right_total.T
    eig_sum = left_acc[...] + flat[:head_size] + flat[head_size:]
    if not last:
        result_refs[0][...] = eig_sum
        return
    for r in prior_refs[1::2]:
        eig_sum += r[...]
    result_refs[0][...] = eig_sum[:, :size]
    for b in range(blocks):
        part = slice(b * size, (b + 1) * size)
        ret_ref, at = result_refs[1 + b], 0
        for r in (*prior_refs[::2], grads_ref):
            ret_ref[at : at + r.shape[0]] = r[:, part]
            at += r.shape[0]
        ret_ref[at:] = eig_sum[:, part].astype(BF16)


def terms_kernel(base, pieces, outs, target, ids_ref, *refs):
    row_refs, refs = refs[:pieces], refs[pieces:]
    cot_refs, (grads_ref, *head_outs, out_ref) = refs[: -2 - outs], refs[-2 - outs :]
    count = out_ref.shape[0]

    def columns(ref, index):
        if target % 128 == 0:
            return ref[:, pl.ds(pl.multiple_of(index * target, target), target)]
        fit = 128 // target
        both = ref[:, pl.ds(pl.multiple_of(index // fit * 128, 128), 128)]
        found = both[:, :target]
        for part in range(1, fit):
            here = both[:, part * target : (part + 1) * target]
            found = jnp.where(index % fit == part, here, found)
        return found

    def right_of(pieces, at):
        return jnp.concatenate(
            [jnp.concatenate([columns(ref, a) for ref in pieces], axis=0) for a in at], axis=1
        )

    group = 2 if count % 2 == 0 else 1
    for start in range(0, count, group):
        at = [ids_ref[base + start + i] for i in range(group)]
        found = [mm(grads_ref[...], right_of(row_refs, at)).astype(BF16)]
        if outs:
            right = right_of(cot_refs, at)
            found += [mm(r[...], right).astype(BF16) for r in head_outs]
        row = 0
        for value in found:
            for i in range(group):
                out_ref[start + i, row : row + value.shape[0]] = value[:, i * target : (i + 1) * target]
            row += value.shape[0]


def put_sums(ref, base, sums):
    rows, lanes = sums.shape
    high = sums.astype(BF16)
    ref[base:] = jnp.zeros((16, ref.shape[1]), BF16)
    ref[base : base + rows, :lanes] = high
    ref[base + 8 : base + 8 + rows, :lanes] = (sums - high.astype(F32)).astype(BF16)


def get_sums(ref, base, shape):
    rows, lanes = shape
    high = ref[base : base + rows, :lanes].astype(F32)
    return high + ref[base + 8 : base + 8 + rows, :lanes].astype(F32)


def pair_kernel(sums, keep_ref, got_ref, *refs):
    if sums:
        gw_refs, gw_got_ref, give_ref, near_ref, gw_out = refs[:sums], *refs[sums:]
    else:
        give_ref, near_ref = refs
    count, rows, _ = keep_ref.shape
    for s in range(count):
        total = keep_ref[s].astype(F32) + got_ref[s].astype(F32)
        if s % 2 == 0:
            near_ref[s // 2] = total
        else:
            give_ref[s // 2 * rows : (s // 2 + 1) * rows] = total.astype(BF16)
    if sums:
        total = jnp.concatenate([r[...] for r in gw_refs], axis=0) + gw_got_ref[...]
        gw_out[...] = total
        put_sums(give_ref, count // 2 * rows, total)


def near_kernel(sums, keep_ref, got_ref, *refs):
    if sums:
        gw_ref, own_ref, gw_out, *piece_refs = refs
    else:
        own_ref, *piece_refs = refs
    count, rows, _ = keep_ref.shape
    own_ref[...] = keep_ref[0] + got_ref[:rows].astype(F32)
    for s, ref in enumerate(piece_refs):
        part = slice((s + 1) * rows, (s + 2) * rows)
        ref[:rows] = (keep_ref[s + 1] + got_ref[part].astype(F32)).astype(BF16)
    if sums:
        total = gw_ref[...] + get_sums(got_ref, count * rows, gw_ref.shape)
        gw_out[...] = total
        for ref in piece_refs:
            put_sums(ref, rows, total)


def final_kernel(calls, count, *refs):
    groups, gw_ref, (out_ref, gw_out) = [], refs[-3], refs[-2:]
    for c in range(calls):
        at = c * (count + 1)
        groups.append((refs[at], refs[at + 1 : at + 1 + count]))
    width = out_ref.shape[2] // calls
    for c, (own_ref, piece_refs) in enumerate(groups):
        total = own_ref[...]
        rows = total.shape[0]
        for r in piece_refs:
            total += r[:rows].astype(F32)
        for a in range(3):
            out_ref[a, :, c * width : (c + 1) * width] = total[a * width : (a + 1) * width].T
        if c == calls - 1:
            out_ref[3] = total[3 * width :].T
            sums = gw_ref[...]
            for r in piece_refs:
                sums += get_sums(r, rows, sums.shape)
            gw_out[...] = sums


def nodes_kernel(blocks, width, calls, ids_ref, eig_ref, *refs):
    ret_refs = refs[:blocks]
    w_refs = refs[blocks : blocks + 3]
    out_ref, eig_out, joined = refs[blocks + 3 :]
    total = eig_ref[...]
    for s in range(blocks):
        part = width // calls
        for c in range(calls):
            at = pl.multiple_of(ids_ref[s] * width + c * part, part)
            for a in range(3):
                row = (3 * c + a) * part
                joined[a, pl.ds(at, part)] = ret_refs[s][row : row + part]
        if s > 0:
            total += ret_refs[s][3 * width :].astype(F32)
    eig_out[...] = total
    chunk = min(256, out_ref.shape[1])
    for c in range(0, out_ref.shape[1], chunk):
        part = slice(c, c + chunk)
        total = mm(w_refs[0][part], joined[0])
        total += mm(w_refs[1][part], joined[1])
        total += mm(w_refs[2][part], joined[2])
        out_ref[:, part] = total.T.astype(BF16)


def body(node_feats, cotangent, w_query, w_key, w_value, w_out, eigvec, eig_weight, block_mask):
    node_size = lax.axis_size("node")
    clus_size = lax.axis_size("clus")
    node_me = lax.axis_index("node")
    clus_me = lax.axis_index("clus")
    own_rows, own_cot = node_feats[0], cotangent[0]
    size, model = own_rows.shape
    heads, eig_count = eig_weight.shape
    nodes = size * node_size
    width = model // node_size
    head_size = width // heads
    scale = head_size ** (-0.5)
    assert math.frexp(scale)[0] == 0.5
    assert clus_size & (clus_size - 1) == 0
    block = nodes
    while block * nodes > SPAN * 512 and block > 128:
        block //= 2
    far_first = [s for s in range(node_size - 1, 0, -1)]

    rest = clus_size // 2
    order = jnp.arange(node_size, dtype=jnp.int32)
    order = order ^ node_me if node_size & (node_size - 1) == 0 else (order + node_me) % node_size
    slots = jnp.arange(clus_size, dtype=jnp.int32)
    slots = (2 * (slots % rest) + jnp.where(slots < rest, 1, 0)) ^ clus_me
    ids = jnp.concatenate([order, slots])

    smem, vmem = pl.BlockSpec(memory_space=pltpu.SMEM), pl.BlockSpec(memory_space=pltpu.VMEM)
    hbm = pl.BlockSpec(memory_space=pltpu.HBM)

    def call(kernel, in_specs, out_shapes, operands, flops, moved, scratch=()):
        return call_here(kernel, in_specs, out_shapes, operands, flops, moved, scratch)

    def call_here(kernel, in_specs, out_shapes, operands, flops, moved, scratch):
        return pl.pallas_call(
            kernel,
            in_specs=in_specs,
            out_specs=[vmem] * len(out_shapes),
            out_shape=[jax.ShapeDtypeStruct(*o) for o in out_shapes],
            scratch_shapes=scratch,
            cost_estimate=pl.CostEstimate(flops=flops, bytes_accessed=moved, transcendentals=0),
            compiler_params=LIMIT,
        )(*operands)

    crossed = node_size == 4 and size % 32 == 0
    rows = [own_rows] + [None] * (node_size - 1)
    for s in far_first:
        if s < 3 or not crossed:
            rows[s] = take(own_rows, "node", s, node_size)

    d_parts = call(
        functools.partial(out_grad_kernel, node_size, width),
        [smem, vmem, hbm],
        [((size, width), BF16)] * node_size,
        (ids, own_cot, pltpu.with_memory_space_constraint(column_blocks(w_out, width), pltpu.HBM)),
        3 * 10**8,
        3 * 2**20,
        [pltpu.VMEM((node_size, model, width), BF16), pltpu.SemaphoreType.DMA((node_size,))],
    )
    d_att = [d_parts[0]] + [None] * (node_size - 1)
    for s in far_first:
        d_att[s] = give(d_parts[s], "node", s, node_size)
    if crossed:
        top, bottom = call(
            split_kernel, [vmem] * 2, [((size // 2, model), BF16)] * 2, (rows[1], rows[2]), 0, 2**19
        )
        rows[3:] = [take(top, "node", 1, node_size), take(bottom, "node", 2, node_size)]
    cots = [own_cot] + [None] * (node_size - 1)
    for s in far_first:
        cots[s] = take(own_cot, "node", s, node_size)

    calls = -(-heads // 2)
    sub_heads = heads // calls
    part_width = width // calls
    assert sub_heads * calls == heads
    weights = call(
        functools.partial(weights_kernel, width, calls),
        [smem] + [hbm] * 3,
        [((model, part_width), BF16)] * (3 * calls),
        (
            ids,
            *[
                pltpu.with_memory_space_constraint(column_blocks(w, width), pltpu.HBM)
                for w in (w_query, w_key, w_value)
            ],
        ),
        0,
        3 * 2**20,
        [pltpu.SemaphoreType.DMA((3 * calls,))],
    )

    steps = nodes // block
    both = 2 * head_size
    groups = -(-sub_heads // 2)
    target = model // clus_size
    pairs = rest // 2
    lam_t = eig_weight.T

    def attention(c, prior):
        last = c == calls - 1
        shapes = [
            ((3 * part_width, nodes), BF16),
            ((part_width, nodes), BF16),
            ((sub_heads, eig_count), F32),
        ]
        if last:
            shapes += [((eig_count, size), F32)]
            shapes += [((3 * width + eig_count, size), BF16)] * node_size
        else:
            shapes += [((eig_count, nodes), F32)]
        return call(
            functools.partial(
                attention_kernel,
                scale,
                sub_heads,
                head_size,
                node_size,
                len(rows),
                c * sub_heads,
                last,
            ),
            [smem, smem] + [vmem] * (len(rows) + node_size + 6 + len(prior)),
            shapes,
            (
                ids,
                block_mask[0],
                *rows,
                *d_att,
                *weights[3 * c : 3 * c + 3],
                eigvec[0],
                eig_weight,
                lam_t,
                *prior,
            ),
            4 * 10**9,
            4 * 2**20,
            [
                pltpu.VMEM((sub_heads, steps, both, block), BF16),
                pltpu.VMEM((sub_heads, nodes, both), BF16),
                pltpu.VMEM((groups, steps, both, block), BF16),
                pltpu.VMEM((groups, nodes, both), BF16),
                pltpu.VMEM((eig_count, nodes), F32),
            ],
        )

    def terms(base, grads_t, outs):
        used = cots if outs else []
        return call(
            functools.partial(terms_kernel, node_size + base, len(rows), len(outs), target),
            [smem] + [vmem] * (len(rows) + len(used) + 1 + len(outs)),
            [((rest, grads_t.shape[0] + len(outs) * part_width, target), BF16)],
            (ids, *rows, *used, grads_t, *outs),
            10**9,
            2**20,
        )[0]

    near_keeps, near_gots, head_outs, weight_parts, prior = [], [], [], [], []
    for c in range(calls):
        last = c == calls - 1
        grads_t, head_out, weight_part, *others = attention(c, prior)
        head_outs.append(head_out)
        weight_parts.append(weight_part)
        prior += [grads_t, others[0]]
        outs = head_outs if last else []
        give_half = terms(0, grads_t, outs)
        got_half = give(give_half, "clus", 1, clus_size)
        keep_half = terms(rest, grads_t, outs)
        group_rows = keep_half.shape[1]
        extra = 16 if last else 0
        operands = [keep_half, got_half]
        shapes = [((pairs * group_rows + extra, target), BF16), ((pairs, group_rows, target), F32)]
        if last:
            mine = jnp.concatenate(weight_parts, axis=0) if calls > 1 else weight_part
            operands += [*weight_parts, give(mine, "clus", 1, clus_size)]
            shapes.append((eig_weight.shape, F32))
        near_give, near_keep, *gw_pair = call(
            functools.partial(pair_kernel, calls if last else 0),
            [vmem] * len(operands),
            shapes,
            operands,
            10**6,
            2**21,
        )
        near_keeps.append(near_keep)
        near_gots.append(give(near_give, "clus", 2, clus_size))
    eig_own, *parts = others

    returned = [parts[0]] + [None] * (node_size - 1)
    for s in far_first:
        returned[s] = give(parts[s], "node", s, node_size)

    totals = []
    for c in range(calls):
        group_rows = near_keeps[c].shape[1]
        last = c == calls - 1
        extra = 16 if last else 0
        shapes = [((group_rows, target), F32)] + ([(eig_weight.shape, F32)] if last else [])
        own, *others = call(
            functools.partial(near_kernel, last),
            [vmem] * (3 if last else 2),
            shapes + [((group_rows + extra, target), BF16)] * (pairs - 1),
            (near_keeps[c], near_gots[c], *(gw_pair if last else [])),
            10**6,
            2**20,
        )
        if last:
            gw_four, *others = others
        totals.append(own)
        found = [None] * (pairs - 1)
        for s in range(pairs - 1, 0, -1):
            found[s - 1] = give(others[s - 1], "clus", 4 * s, clus_size)
        totals += found

    grad_rows, grad_eig = call(
        functools.partial(nodes_kernel, node_size, width, calls),
        [smem] + [vmem] * (node_size + 4),
        [((size, model), BF16), ((eig_count, size), F32)],
        (ids, eig_own, *returned, w_query, w_key, w_value),
        10**9,
        7 * 2**20,
        [pltpu.VMEM((3, model, size), BF16)],
    )

    grad_proj, grad_weight = call(
        functools.partial(final_kernel, calls, pairs - 1),
        [vmem] * (len(totals) + 1),
        [((4, target, width), F32), (eig_weight.shape, F32)],
        (*totals, gw_four),
        10**6,
        2 * 2**20,
    )
    return (grad_rows[None], grad_eig[None], grad_weight, grad_proj)


def solution(mesh):
    placed = (
        P("clus", "node", None),
        P("clus", "node", None),
        P(),
        P(),
        P(),
        P(),
        P("clus", None, None),
        P("node", None),
        P("clus", "node", None, None),
    )

    return jax.shard_map(
        body,
        mesh=mesh,
        in_specs=placed,
        out_specs=(
            P("clus", "node", None),
            P("clus", None, "node"),
            P("node", None),
            P(None, "clus", "node"),
        ),
        check_vma=False,
    )
```

```python
import functools
import math

import jax
import jax.numpy as jnp
from jax import lax
from jax.experimental import pallas as pl
from jax.experimental.pallas import tpu as pltpu
from jax.sharding import PartitionSpec as P


BF16 = jnp.bfloat16
SPAN = 512
F32 = jnp.float32
LIMIT = pltpu.CompilerParams(vmem_limit_bytes=32 * 2**20)


def mm(a, b):
    return jnp.dot(a, b, preferred_element_type=F32)


def take(value, axis, step, size):
    if size & (size - 1) == 0:
        pairs = [(i, i ^ step) for i in range(size)]
    else:
        pairs = [((i + step) % size, i) for i in range(size)]
    return lax.ppermute(value, axis, pairs)


def give(value, axis, step, size):
    if size & (size - 1) == 0:
        return take(value, axis, step, size)
    return lax.ppermute(value, axis, [(i, (i + step) % size) for i in range(size)])


def column_blocks(weight, width):
    if width % 128 == 0:
        return weight
    return weight.reshape(weight.shape[0], -1, width).transpose(1, 0, 2)


def column_copy(ref, at, width, target, sem):
    if len(ref.shape) == 3:
        return pltpu.make_async_copy(ref.at[at], target, sem)
    at = pl.multiple_of(at * width, width)
    return pltpu.make_async_copy(ref.at[:, pl.ds(at, width)], target, sem)


def out_grad_kernel(count, width, ids_ref, rows_ref, w_ref, *refs):
    sources, out_refs, targets = refs[:3], refs[3 : 3 + count], refs[3 + count : 6 + count]
    rows, held, sems = refs[6 + count :]
    row_copy = pltpu.make_async_copy(rows_ref, rows, sems.at[count + 3])
    row_copy.start()
    order = list(range(count - 1, -1, -1))
    copies = {s: column_copy(w_ref, ids_ref[s], width, held.at[s], sems.at[s]) for s in order}
    for s in order:
        copies[s].start()
    others = [
        column_copy(sources[a], ids_ref[0], width, targets[a], sems.at[count + a])
        for a in range(3)
    ]
    for c in others:
        c.start()
    row_copy.wait()
    for s in order:
        copies[s].wait()
        out_refs[s][...] = mm(rows[...], held[s]).astype(BF16)
    for c in others:
        c.wait()


def split_kernel(first_ref, second_ref, top_ref, bottom_ref):
    half = top_ref.shape[0]
    top_ref[...] = second_ref[:half]
    bottom_ref[...] = first_ref[half:]


def attention_kernel(scale, heads, head_size, blocks, pieces, ids_ref, mask_ref, *refs):
    row_refs, d_refs = refs[:pieces], refs[pieces : pieces + blocks]
    refs = refs[pieces + blocks :]
    wq_ref, wk_ref, wv_ref, eig_ref, lam_ref, lam_t_ref = refs[:6]
    grads_ref, out_ref, gw_ref, eig_out = refs[6:10]
    ret_refs = refs[10:-5]
    qe, qn, dt, dn, left_acc = refs[-5:]
    eig_count, nodes = eig_ref.shape
    width = heads * head_size
    size = nodes // blocks
    steps, cols = qe.shape[1], qe.shape[3]
    tile_count = mask_ref.shape[1]
    tile = nodes // tile_count
    per = tile_count // blocks
    both = 2 * head_size
    assert eig_count == head_size
    groups = -(-heads // 2)

    def fit(array):
        extra = groups * both - array.shape[1]
        if extra == 0:
            return array
        return jnp.concatenate([array, jnp.zeros((array.shape[0], extra), array.dtype)], axis=1)

    parts = []
    for s in range(blocks):
        parts.append(eig_ref[:, pl.ds(pl.multiple_of(ids_ref[s] * size, size), size)])
    eig = jnp.concatenate(parts, axis=1)
    turned = jnp.concatenate([eig, eig], axis=0).T
    wide = turned.astype(F32)
    rows = jnp.concatenate([r[...] for r in row_refs], axis=0)
    query = fit(mm(rows, wq_ref[...]).astype(BF16))
    keys = fit(mm(rows, wk_ref[...]).astype(BF16))
    values = fit(mm(rows, wv_ref[...]).astype(BF16))
    d_att = fit(jnp.concatenate([r[...] for r in d_refs], axis=0))
    query_t = (query.astype(F32) * scale).astype(BF16).T
    keys_t = keys.T
    values_t = values.T
    d_att_t = d_att.T
    first_half = lax.broadcasted_iota(jnp.int32, (nodes, both), 1) < head_size
    first_row = lax.broadcasted_iota(jnp.int32, (1, both), 1) < head_size

    def pick(even, first, second):
        return jnp.where(first_half, first, second) if even else jnp.where(first_half, second, first)

    def stack(even, first, second):
        return jnp.concatenate([first, second] if even else [second, first], axis=0)

    for g in range(groups):
        group = slice(g * both, (g + 1) * both)
        dn[g] = d_att[:, group]
        for b in range(steps):
            here = slice(b * cols, (b + 1) * cols)
            dt[g, b] = d_att_t[group, here]
        for h in range(2 * g, min(2 * g + 2, heads)):
            even = h % 2 == 0
            part = slice(h * head_size, (h + 1) * head_size)
            qn[h] = pick(even, query[:, group], turned)
            for b in range(steps):
                here = slice(b * cols, (b + 1) * cols)
                qe[h, b] = stack(even, query_t[part, here], eig[:, here])

    def before(head, block, kw, vn):
        return mm(kw, qe[head, block]), mm(vn, dt[head // 2, block])

    def one_block(head, block, kt, vt, scores, dprob, totals):
        at = block * cols
        here = pl.ds(at if isinstance(block, int) else pl.multiple_of(at, cols), cols)
        tiles_here = cols // tile
        columns = []
        for i in range(tiles_here):
            i_tile = block * tiles_here + i
            i_at = ids_ref[i_tile // per] * per + i_tile % per
            found = []
            for j in range(tile_count):
                j_at = ids_ref[j // per] * per + j % per
                part = scores[j * tile : (j + 1) * tile, i * tile : (i + 1) * tile]
                found.append(jnp.where(mask_ref[head, i_at, j_at] > 0, part, -jnp.inf))
            columns.append(jnp.concatenate(found, axis=0))
        masked = jnp.concatenate(columns, axis=1)
        top = jnp.max(masked, axis=0, keepdims=True)
        raised = jnp.exp(masked - top)
        total = jnp.sum(raised, axis=0, keepdims=True)
        prob = raised * (1.0 / total)
        half = prob.astype(BF16)
        first = head * head_size
        out_ref[first : first + head_size, here] = mm(vt, half).astype(BF16)
        value = mm(half, dn[head // 2, here, :])
        delta = jnp.sum(prob * dprob, axis=0, keepdims=True)
        dscore = (prob * (dprob - delta)).astype(BF16)
        left = mm(kt, dscore)
        grads_ref[first : first + head_size, here] = (left[:head_size] * scale).astype(BF16)
        weighted = lam_t_ref[:, head : head + 1] * left[head_size:]
        if head == 0:
            left_acc[:, here] = weighted
        else:
            left_acc[:, here] += weighted
        right = mm(dscore, qn[head, here, :])
        if totals is None:
            return right, value
        return totals[0] + right, totals[1] + value

    def operands(h):
        even, g = h % 2 == 0, h // 2
        group = slice(g * both, (g + 1) * both)
        part = slice(h * head_size, (h + 1) * head_size)
        lam_row = jnp.concatenate([lam_ref[h : h + 1, :]] * 2, axis=1)
        kw = pick(even, keys[:, group], (wide * lam_row).astype(BF16))
        kt = jnp.concatenate([keys_t[part], eig], axis=0)
        vn = pick(even, values[:, group], jnp.zeros((nodes, both), BF16))
        return lam_row, kw, kt, values_t[part], vn

    unrolled = [(h, b) for h in range(heads) for b in range(steps)] if steps <= 4 else []
    ready = {}

    def prepare(at):
        if at < len(unrolled):
            h, b = unrolled[at]
            if b == 0:
                ready[h] = operands(h)
            ready[h, b] = before(h, b, ready[h][1], ready[h][4])

    def all_blocks(h):
        if unrolled:
            totals = None
            for b in range(steps):
                prepare(h * steps + b + 1)
                _, _, kt, vt, _ = ready[h]
                totals = one_block(h, b, kt, vt, *ready.pop((h, b)), totals)
            return ready[h][0], totals
        lam_row, kw, kt, vt, vn = operands(h)
        return lam_row, lax.fori_loop(
            1,
            steps,
            lambda b, t: one_block(h, b, kt, vt, *before(h, b, kw, vn), t),
            one_block(h, 0, kt, vt, *before(h, 0, kw, vn), None),
        )

    prepare(0)
    right_total = None
    for g in range(groups):
        group = slice(g * both, (g + 1) * both)
        found = []
        lam_rows = []
        for h in range(2 * g, min(2 * g + 2, heads)):
            lam_row, totals = all_blocks(h)
            lam_rows.append(lam_row)
            found.append(totals)
        if len(found) == 1:
            found.append((jnp.zeros((nodes, both), F32), jnp.zeros((nodes, both), F32)))
            lam_rows.append(jnp.zeros((1, both), F32))
        keep = min(both, width - g * both)
        key_grad = jnp.where(first_half, found[0][0], found[1][0]).T
        grads_ref[width + g * both : width + g * both + keep, :] = (
            key_grad[:keep] * scale
        ).astype(BF16)
        value_grad = jnp.where(first_half, found[0][1], found[1][1]).T
        grads_ref[2 * width + g * both : 2 * width + g * both + keep, :] = value_grad[
            :keep
        ].astype(BF16)
        right = jnp.where(first_half, found[1][0], found[0][0])
        sums = jnp.sum(wide * right, axis=0, keepdims=True)
        gw_ref[2 * g : 2 * g + 1, :] = sums[:, head_size:]
        if 2 * g + 1 < heads:
            gw_ref[2 * g + 1 : 2 * g + 2, :] = sums[:, :head_size]
        right = right * jnp.where(first_row, lam_rows[1], lam_rows[0])
        right_total = right if right_total is None else right_total + right

    flat = right_total.T
    eig_sum = left_acc[...] + flat[:head_size] + flat[head_size:]
    eig_out[...] = eig_sum[:, :size]
    for b in range(blocks):
        part = slice(b * size, (b + 1) * size)
        ret_refs[b][: 3 * width] = grads_ref[:, part]
        ret_refs[b][3 * width :] = eig_sum[:, part].astype(BF16)


def terms_kernel(base, pieces, target, ids_ref, *refs):
    row_refs, (grads_ref, out_ref) = refs[:pieces], refs[pieces:]
    count = out_ref.shape[0]

    def columns(ref, index):
        if target % 128 == 0:
            return ref[:, pl.ds(pl.multiple_of(index * target, target), target)]
        fit = 128 // target
        both = ref[:, pl.ds(pl.multiple_of(index // fit * 128, 128), 128)]
        found = both[:, :target]
        for part in range(1, fit):
            here = both[:, part * target : (part + 1) * target]
            found = jnp.where(index % fit == part, here, found)
        return found

    def right_of(pieces, at):
        return jnp.concatenate(
            [jnp.concatenate([columns(ref, a) for ref in pieces], axis=0) for a in at], axis=1
        )

    group = 2 if count % 2 == 0 else 1
    for start in range(0, count, group):
        at = [ids_ref[base + start + i] for i in range(group)]
        value = mm(grads_ref[...], right_of(row_refs, at)).astype(BF16)
        for i in range(group):
            out_ref[start + i] = value[:, i * target : (i + 1) * target]


def put_sums(ref, base, sums):
    rows, lanes = sums.shape
    high = sums.astype(BF16)
    ref[base:] = jnp.zeros((16, ref.shape[1]), BF16)
    ref[base : base + rows, :lanes] = high
    ref[base + 8 : base + 8 + rows, :lanes] = (sums - high.astype(F32)).astype(BF16)


def get_sums(ref, base, shape):
    rows, lanes = shape
    high = ref[base : base + rows, :lanes].astype(F32)
    return high + ref[base + 8 : base + 8 + rows, :lanes].astype(F32)


def pair_kernel(sums, keep_ref, got_ref, *refs):
    if sums:
        gw_ref, gw_got_ref, give_ref, near_ref, gw_out = refs
    else:
        give_ref, near_ref = refs
    count, rows, _ = keep_ref.shape
    for s in range(count):
        total = keep_ref[s].astype(F32) + got_ref[s].astype(F32)
        if s % 2 == 0:
            near_ref[s // 2] = total
        else:
            give_ref[s // 2 * rows : (s // 2 + 1) * rows] = total.astype(BF16)
    if sums:
        total = gw_ref[...] + gw_got_ref[...]
        gw_out[...] = total
        put_sums(give_ref, count // 2 * rows, total)


def near_kernel(sums, keep_ref, got_ref, *refs):
    if sums:
        gw_ref, own_ref, gw_out, *piece_refs = refs
    else:
        own_ref, *piece_refs = refs
    count, rows, _ = keep_ref.shape
    own_ref[...] = keep_ref[0] + got_ref[:rows].astype(F32)
    for s, ref in enumerate(piece_refs):
        part = slice((s + 1) * rows, (s + 2) * rows)
        ref[:rows] = (keep_ref[s + 1] + got_ref[part].astype(F32)).astype(BF16)
    if sums:
        total = gw_ref[...] + get_sums(got_ref, count * rows, gw_ref.shape)
        gw_out[...] = total
        for ref in piece_refs:
            put_sums(ref, rows, total)


def final_kernel(count, *refs):
    gw_ref, out_ref, gw_out = refs[-3:]
    width = out_ref.shape[2]
    found = []
    for c in range(2):
        own_ref, *piece_refs = refs[c * (count + 1) : (c + 1) * (count + 1)]
        rows = own_ref.shape[0]
        total = own_ref[...]
        for r in piece_refs:
            total += r[:rows].astype(F32)
        found += [total[at : at + width] for at in range(0, rows, width)]
        if c == 0:
            sums = gw_ref[...]
            for r in piece_refs:
                sums += get_sums(r, rows, sums.shape)
            gw_out[...] = sums
    for a, total in enumerate(found):
        out_ref[a] = total.T


def nodes_kernel(blocks, width, ids_ref, eig_ref, *refs):
    ret_refs = refs[:blocks]
    w_refs = refs[blocks : blocks + 3]
    out_ref, eig_out, joined = refs[blocks + 3 :]
    total = eig_ref[...]
    for s in range(blocks):
        at = pl.multiple_of(ids_ref[s] * width, width)
        for a in range(3):
            joined[a, pl.ds(at, width)] = ret_refs[s][a * width : (a + 1) * width]
        if s > 0:
            total += ret_refs[s][3 * width :].astype(F32)
    eig_out[...] = total
    chunk = min(256, out_ref.shape[1])
    for c in range(0, out_ref.shape[1], chunk):
        part = slice(c, c + chunk)
        total = mm(w_refs[0][part], joined[0])
        total += mm(w_refs[1][part], joined[1])
        total += mm(w_refs[2][part], joined[2])
        out_ref[:, part] = total.T.astype(BF16)


def body(node_feats, cotangent, w_query, w_key, w_value, w_out, eigvec, eig_weight, block_mask):
    node_size = lax.axis_size("node")
    clus_size = lax.axis_size("clus")
    node_me = lax.axis_index("node")
    clus_me = lax.axis_index("clus")
    own_rows, own_cot = node_feats[0], cotangent[0]
    size, model = own_rows.shape
    heads, eig_count = eig_weight.shape
    nodes = size * node_size
    width = model // node_size
    head_size = width // heads
    scale = head_size ** (-0.5)
    assert math.frexp(scale)[0] == 0.5
    assert clus_size & (clus_size - 1) == 0
    block = nodes
    while block * nodes > SPAN * 512 and block > 128:
        block //= 2
    far_first = [s for s in range(node_size - 1, 0, -1)]

    rest = clus_size // 2
    order = jnp.arange(node_size, dtype=jnp.int32)
    order = order ^ node_me if node_size & (node_size - 1) == 0 else (order + node_me) % node_size
    slots = jnp.arange(clus_size, dtype=jnp.int32)
    slots = (2 * (slots % rest) + jnp.where(slots < rest, 1, 0)) ^ clus_me
    ids = jnp.concatenate([order, slots])

    smem, vmem = pl.BlockSpec(memory_space=pltpu.SMEM), pl.BlockSpec(memory_space=pltpu.VMEM)
    hbm = pl.BlockSpec(memory_space=pltpu.HBM)

    def call(kernel, in_specs, out_shapes, operands, flops, moved, scratch=()):
        return call_here(kernel, in_specs, out_shapes, operands, flops, moved, scratch)

    def call_here(kernel, in_specs, out_shapes, operands, flops, moved, scratch):
        return pl.pallas_call(
            kernel,
            in_specs=in_specs,
            out_specs=[vmem] * len(out_shapes),
            out_shape=[jax.ShapeDtypeStruct(*o) for o in out_shapes],
            scratch_shapes=scratch,
            cost_estimate=pl.CostEstimate(flops=flops, bytes_accessed=moved, transcendentals=0),
            compiler_params=LIMIT,
        )(*operands)

    crossed = node_size == 4 and size % 32 == 0
    rows = [own_rows] + [None] * (node_size - 1)
    for s in far_first:
        if s < 3 or not crossed:
            rows[s] = take(own_rows, "node", s, node_size)

    def held(array):
        return pltpu.with_memory_space_constraint(array, pltpu.HBM)

    made = call(
        functools.partial(out_grad_kernel, node_size, width),
        [smem] + [hbm] * 5,
        [((size, width), BF16)] * node_size + [((model, width), BF16)] * 3,
        (
            ids,
            held(own_cot),
            *[held(column_blocks(w, width)) for w in (w_out, w_query, w_key, w_value)],
        ),
        3 * 10**8,
        3 * 2**20,
        [
            pltpu.VMEM((size, model), BF16),
            pltpu.VMEM((node_size, model, width), BF16),
            pltpu.SemaphoreType.DMA((node_size + 4,)),
        ],
    )
    d_parts, weights = made[:node_size], made[node_size:]
    d_att = [d_parts[0]] + [None] * (node_size - 1)
    for s in far_first:
        d_att[s] = give(d_parts[s], "node", s, node_size)
    if crossed:
        top, bottom = call(
            split_kernel, [vmem] * 2, [((size // 2, model), BF16)] * 2, (rows[1], rows[2]), 0, 2**19
        )
        rows[3:] = [take(top, "node", 1, node_size), take(bottom, "node", 2, node_size)]
    cots = [own_cot] + [None] * (node_size - 1)
    for s in far_first:
        cots[s] = take(own_cot, "node", s, node_size)

    steps = nodes // block
    both = 2 * head_size
    groups = -(-heads // 2)
    target = model // clus_size
    pairs = rest // 2
    grads_t, out_t, gw_own, eig_own, *parts = call(
        functools.partial(attention_kernel, scale, heads, head_size, node_size, len(rows)),
        [smem, smem] + [vmem] * (len(rows) + node_size + 6),
        [
            ((3 * width, nodes), BF16),
            ((width, nodes), BF16),
            ((heads, eig_count), F32),
            ((eig_count, size), F32),
        ]
        + [((3 * width + eig_count, size), BF16)] * node_size,
        (ids, block_mask[0], *rows, *d_att, *weights, eigvec[0], eig_weight, eig_weight.T),
        8 * 10**9,
        8 * 2**20,
        [
            pltpu.VMEM((heads, steps, both, block), BF16),
            pltpu.VMEM((heads, nodes, both), BF16),
            pltpu.VMEM((groups, steps, both, block), BF16),
            pltpu.VMEM((groups, nodes, both), BF16),
            pltpu.VMEM((eig_count, nodes), F32),
        ],
    )

    def terms(base, left, pieces):
        return call(
            functools.partial(terms_kernel, node_size + base, len(pieces), target),
            [smem] + [vmem] * (len(pieces) + 1),
            [((rest, left.shape[0], target), BF16)],
            (ids, *pieces, left),
            10**9,
            2**20,
        )[0]

    near_keeps, near_gots = [], []
    for c, (left, pieces) in enumerate(((grads_t, rows), (out_t, cots))):
        give_half = terms(0, left, pieces)
        got_half = give(give_half, "clus", 1, clus_size)
        keep_half = terms(rest, left, pieces)
        group_rows = left.shape[0]
        operands = [keep_half, got_half]
        shapes = [
            ((pairs * group_rows + (16 if c == 0 else 0), target), BF16),
            ((pairs, group_rows, target), F32),
        ]
        if c == 0:
            operands += [gw_own, give(gw_own, "clus", 1, clus_size)]
            shapes.append((eig_weight.shape, F32))
        near_give, near_keep, *others = call(
            functools.partial(pair_kernel, c == 0),
            [vmem] * len(operands),
            shapes,
            operands,
            10**6,
            2**21,
        )
        if c == 0:
            gw_pair = others[0]
        near_keeps.append(near_keep)
        near_gots.append(give(near_give, "clus", 2, clus_size))

    returned = [parts[0]] + [None] * (node_size - 1)
    for s in far_first:
        returned[s] = give(parts[s], "node", s, node_size)

    totals = []
    for c in range(2):
        group_rows = near_keeps[c].shape[1]
        extra = 16 if c == 0 else 0
        shapes = [((group_rows, target), F32)] + ([(eig_weight.shape, F32)] if c == 0 else [])
        own, *others = call(
            functools.partial(near_kernel, c == 0),
            [vmem] * (3 if c == 0 else 2),
            shapes + [((group_rows + extra, target), BF16)] * (pairs - 1),
            (near_keeps[c], near_gots[c], *([gw_pair] if c == 0 else [])),
            10**6,
            2**20,
        )
        if c == 0:
            gw_four, *others = others
        totals.append(own)
        found = [None] * (pairs - 1)
        for s in range(pairs - 1, 0, -1):
            found[s - 1] = give(others[s - 1], "clus", 4 * s, clus_size)
        totals += found

    grad_rows, grad_eig = call(
        functools.partial(nodes_kernel, node_size, width),
        [smem] + [vmem] * (node_size + 4),
        [((size, model), BF16), ((eig_count, size), F32)],
        (ids, eig_own, *returned, w_query, w_key, w_value),
        10**9,
        7 * 2**20,
        [pltpu.VMEM((3, model, size), BF16)],
    )

    grad_proj, grad_weight = call(
        functools.partial(final_kernel, pairs - 1),
        [vmem] * (len(totals) + 1),
        [((4, target, width), F32), (eig_weight.shape, F32)],
        (*totals, gw_four),
        10**6,
        2 * 2**20,
    )
    return (grad_rows[None], grad_eig[None], grad_weight, grad_proj)


def solution(mesh):
    placed = (
        P("clus", "node", None),
        P("clus", "node", None),
        P(),
        P(),
        P(),
        P(),
        P("clus", None, None),
        P("node", None),
        P("clus", "node", None, None),
    )

    return jax.shard_map(
        body,
        mesh=mesh,
        in_specs=placed,
        out_specs=(
            P("clus", "node", None),
            P("clus", None, "node"),
            P("node", None),
            P(None, "clus", "node"),
        ),
        check_vma=False,
    )
```

```python
import functools
import math

import jax
import jax.numpy as jnp
from jax import lax
from jax.experimental import pallas as pl
from jax.experimental.pallas import tpu as pltpu
from jax.sharding import PartitionSpec as P


BF16 = jnp.bfloat16
SPAN = 512
F32 = jnp.float32
LIMIT = pltpu.CompilerParams(vmem_limit_bytes=32 * 2**20)


def mm(a, b):
    return jnp.dot(a, b, preferred_element_type=F32)


def take(value, axis, step, size):
    if size & (size - 1) == 0:
        pairs = [(i, i ^ step) for i in range(size)]
    else:
        pairs = [((i + step) % size, i) for i in range(size)]
    return lax.ppermute(value, axis, pairs)


def give(value, axis, step, size):
    if size & (size - 1) == 0:
        return take(value, axis, step, size)
    return lax.ppermute(value, axis, [(i, (i + step) % size) for i in range(size)])


def column_blocks(weight, width):
    if width % 128 == 0:
        return weight
    return weight.reshape(weight.shape[0], -1, width).transpose(1, 0, 2)


def column_copy(ref, at, width, target, sem):
    if len(ref.shape) == 3:
        return pltpu.make_async_copy(ref.at[at], target, sem)
    at = pl.multiple_of(at * width, width)
    return pltpu.make_async_copy(ref.at[:, pl.ds(at, width)], target, sem)


def out_grad_kernel(count, width, ids_ref, rows_ref, w_ref, *refs):
    sources, out_refs, targets = refs[:3], refs[3 : 3 + count], refs[3 + count : 6 + count]
    rows, held, sems = refs[6 + count :]
    row_copy = pltpu.make_async_copy(rows_ref, rows, sems.at[count + 3])
    row_copy.start()
    order = list(range(count - 1, -1, -1))
    copies = {s: column_copy(w_ref, ids_ref[s], width, held.at[s], sems.at[s]) for s in order}
    for s in order:
        copies[s].start()
    others = [
        column_copy(sources[a], ids_ref[0], width, targets[a], sems.at[count + a])
        for a in range(3)
    ]
    for c in others:
        c.start()
    row_copy.wait()
    for s in order:
        copies[s].wait()
        out_refs[s][...] = mm(rows[...], held[s]).astype(BF16)
    for c in others:
        c.wait()


def split_kernel(first_ref, second_ref, top_ref, bottom_ref):
    half = top_ref.shape[0]
    top_ref[...] = second_ref[:half]
    bottom_ref[...] = first_ref[half:]


def attention_kernel(scale, heads, head_size, blocks, pieces, ids_ref, mask_ref, *refs):
    row_refs, d_refs = refs[:pieces], refs[pieces : pieces + blocks]
    refs = refs[pieces + blocks :]
    wq_ref, wk_ref, wv_ref, eig_ref, lam_ref, lam_t_ref = refs[:6]
    grads_ref, out_ref, gw_ref, eig_out = refs[6:10]
    ret_refs = refs[10:-5]
    qe, qn, dt, dn, left_acc = refs[-5:]
    eig_count, nodes = eig_ref.shape
    width = heads * head_size
    size = nodes // blocks
    steps, cols = qe.shape[1], qe.shape[3]
    tile_count = mask_ref.shape[1]
    tile = nodes // tile_count
    per = tile_count // blocks
    both = 2 * head_size
    assert eig_count == head_size
    groups = -(-heads // 2)

    def fit(array):
        extra = groups * both - array.shape[1]
        if extra == 0:
            return array
        return jnp.concatenate([array, jnp.zeros((array.shape[0], extra), array.dtype)], axis=1)

    parts = []
    for s in range(blocks):
        parts.append(eig_ref[:, pl.ds(pl.multiple_of(ids_ref[s] * size, size), size)])
    eig = jnp.concatenate(parts, axis=1)
    turned = jnp.concatenate([eig, eig], axis=0).T
    wide = turned.astype(F32)
    rows = jnp.concatenate([r[...] for r in row_refs], axis=0)
    query = fit(mm(rows, wq_ref[...]).astype(BF16))
    keys = fit(mm(rows, wk_ref[...]).astype(BF16))
    values = fit(mm(rows, wv_ref[...]).astype(BF16))
    d_att = fit(jnp.concatenate([r[...] for r in d_refs], axis=0))
    query_t = (query.astype(F32) * scale).astype(BF16).T
    keys_t = keys.T
    values_t = values.T
    d_att_t = d_att.T
    first_half = lax.broadcasted_iota(jnp.int32, (nodes, both), 1) < head_size
    first_row = lax.broadcasted_iota(jnp.int32, (1, both), 1) < head_size

    def pick(even, first, second):
        return jnp.where(first_half, first, second) if even else jnp.where(first_half, second, first)

    def stack(even, first, second):
        return jnp.concatenate([first, second] if even else [second, first], axis=0)

    for g in range(groups):
        group = slice(g * both, (g + 1) * both)
        dn[g] = d_att[:, group]
        for b in range(steps):
            here = slice(b * cols, (b + 1) * cols)
            dt[g, b] = d_att_t[group, here]
        for h in range(2 * g, min(2 * g + 2, heads)):
            even = h % 2 == 0
            part = slice(h * head_size, (h + 1) * head_size)
            qn[h] = pick(even, query[:, group], turned)
            for b in range(steps):
                here = slice(b * cols, (b + 1) * cols)
                qe[h, b] = stack(even, query_t[part, here], eig[:, here])

    def before(head, block, kw, vn):
        return mm(kw, qe[head, block]), mm(vn, dt[head // 2, block])

    def one_block(head, block, kt, vt, scores, dprob, totals):
        at = block * cols
        here = pl.ds(at if isinstance(block, int) else pl.multiple_of(at, cols), cols)
        tiles_here = cols // tile
        columns = []
        for i in range(tiles_here):
            i_tile = block * tiles_here + i
            i_at = ids_ref[i_tile // per] * per + i_tile % per
            found = []
            for j in range(tile_count):
                j_at = ids_ref[j // per] * per + j % per
                part = scores[j * tile : (j + 1) * tile, i * tile : (i + 1) * tile]
                found.append(jnp.where(mask_ref[head, i_at, j_at] > 0, part, -jnp.inf))
            columns.append(jnp.concatenate(found, axis=0))
        masked = jnp.concatenate(columns, axis=1)
        top = jnp.max(masked, axis=0, keepdims=True)
        raised = jnp.exp(masked - top)
        total = jnp.sum(raised, axis=0, keepdims=True)
        prob = raised * (1.0 / total)
        half = prob.astype(BF16)
        first = head * head_size
        out_ref[first : first + head_size, here] = mm(vt, half).astype(BF16)
        value = mm(half, dn[head // 2, here, :])
        delta = jnp.sum(prob * dprob, axis=0, keepdims=True)
        dscore = (prob * (dprob - delta)).astype(BF16)
        left = mm(kt, dscore)
        grads_ref[first : first + head_size, here] = (left[:head_size] * scale).astype(BF16)
        weighted = lam_t_ref[:, head : head + 1] * left[head_size:]
        if head == 0:
            left_acc[:, here] = weighted
        else:
            left_acc[:, here] += weighted
        right = mm(dscore, qn[head, here, :])
        if totals is None:
            return right, value
        return totals[0] + right, totals[1] + value

    def operands(h):
        even, g = h % 2 == 0, h // 2
        group = slice(g * both, (g + 1) * both)
        part = slice(h * head_size, (h + 1) * head_size)
        lam_row = jnp.concatenate([lam_ref[h : h + 1, :]] * 2, axis=1)
        kw = pick(even, keys[:, group], (wide * lam_row).astype(BF16))
        kt = jnp.concatenate([keys_t[part], eig], axis=0)
        vn = pick(even, values[:, group], jnp.zeros((nodes, both), BF16))
        return lam_row, kw, kt, values_t[part], vn

    unrolled = [(h, b) for h in range(heads) for b in range(steps)] if steps <= 4 else []
    ready = {}

    def prepare(at):
        if at < len(unrolled):
            h, b = unrolled[at]
            if b == 0:
                ready[h] = operands(h)
            ready[h, b] = before(h, b, ready[h][1], ready[h][4])

    def all_blocks(h):
        if unrolled:
            totals = None
            for b in range(steps):
                prepare(h * steps + b + 1)
                _, _, kt, vt, _ = ready[h]
                totals = one_block(h, b, kt, vt, *ready.pop((h, b)), totals)
            return ready[h][0], totals
        lam_row, kw, kt, vt, vn = operands(h)
        return lam_row, lax.fori_loop(
            1,
            steps,
            lambda b, t: one_block(h, b, kt, vt, *before(h, b, kw, vn), t),
            one_block(h, 0, kt, vt, *before(h, 0, kw, vn), None),
        )

    prepare(0)
    right_total = None
    for g in range(groups):
        group = slice(g * both, (g + 1) * both)
        found = []
        lam_rows = []
        for h in range(2 * g, min(2 * g + 2, heads)):
            lam_row, totals = all_blocks(h)
            lam_rows.append(lam_row)
            found.append(totals)
        if len(found) == 1:
            found.append((jnp.zeros((nodes, both), F32), jnp.zeros((nodes, both), F32)))
            lam_rows.append(jnp.zeros((1, both), F32))
        keep = min(both, width - g * both)
        key_grad = jnp.where(first_half, found[0][0], found[1][0]).T
        grads_ref[width + g * both : width + g * both + keep, :] = (
            key_grad[:keep] * scale
        ).astype(BF16)
        value_grad = jnp.where(first_half, found[0][1], found[1][1]).T
        grads_ref[2 * width + g * both : 2 * width + g * both + keep, :] = value_grad[
            :keep
        ].astype(BF16)
        right = jnp.where(first_half, found[1][0], found[0][0])
        sums = jnp.sum(wide * right, axis=0, keepdims=True)
        gw_ref[2 * g : 2 * g + 1, :] = sums[:, head_size:]
        if 2 * g + 1 < heads:
            gw_ref[2 * g + 1 : 2 * g + 2, :] = sums[:, :head_size]
        right = right * jnp.where(first_row, lam_rows[1], lam_rows[0])
        right_total = right if right_total is None else right_total + right

    flat = right_total.T
    eig_sum = left_acc[...] + flat[:head_size] + flat[head_size:]
    eig_out[...] = eig_sum[:, :size]
    for b in range(blocks):
        part = slice(b * size, (b + 1) * size)
        ret_refs[b][: 3 * width] = grads_ref[:, part]
        ret_refs[b][3 * width :] = eig_sum[:, part].astype(BF16)


def terms_kernel(base, layout, target, ids_ref, *refs):
    out_ref, operands, at = refs[-1], [], 0
    for lanes, pieces in layout:
        operands.append((refs[at], lanes, refs[at + 1 : at + 1 + pieces]))
        at += 1 + pieces
    count = out_ref.shape[0]

    def columns(ref, index):
        if target % 128 == 0:
            return ref[:, pl.ds(pl.multiple_of(index * target, target), target)]
        fit = 128 // target
        both = ref[:, pl.ds(pl.multiple_of(index // fit * 128, 128), 128)]
        found = both[:, :target]
        for part in range(1, fit):
            here = both[:, part * target : (part + 1) * target]
            found = jnp.where(index % fit == part, here, found)
        return found

    def right_of(pieces, at):
        return jnp.concatenate(
            [jnp.concatenate([columns(ref, a) for ref in pieces], axis=0) for a in at], axis=1
        )

    group = 2 if count % 2 == 0 else 1
    for start in range(0, count, group):
        at = [ids_ref[base + start + i] for i in range(group)]
        row = 0
        for left_ref, (low, high), pieces in operands:
            value = mm(left_ref[low:high], right_of(pieces, at)).astype(BF16)
            for i in range(group):
                out_ref[start + i, row : row + high - low] = value[:, i * target : (i + 1) * target]
            row += high - low


def put_sums(ref, base, sums):
    rows, lanes = sums.shape
    high = sums.astype(BF16)
    ref[base:] = jnp.zeros((16, ref.shape[1]), BF16)
    ref[base : base + rows, :lanes] = high
    ref[base + 8 : base + 8 + rows, :lanes] = (sums - high.astype(F32)).astype(BF16)


def get_sums(ref, base, shape):
    rows, lanes = shape
    high = ref[base : base + rows, :lanes].astype(F32)
    return high + ref[base + 8 : base + 8 + rows, :lanes].astype(F32)


def pair_kernel(sums, keep_ref, got_ref, *refs):
    if sums:
        gw_ref, gw_got_ref, give_ref, near_ref, gw_out = refs
    else:
        give_ref, near_ref = refs
    count, rows, _ = keep_ref.shape
    for s in range(count):
        total = keep_ref[s].astype(F32) + got_ref[s].astype(F32)
        if s % 2 == 0:
            near_ref[s // 2] = total
        else:
            give_ref[s // 2 * rows : (s // 2 + 1) * rows] = total.astype(BF16)
    if sums:
        total = gw_ref[...] + gw_got_ref[...]
        gw_out[...] = total
        put_sums(give_ref, count // 2 * rows, total)


def near_kernel(sums, keep_ref, got_ref, *refs):
    if sums:
        gw_ref, own_ref, gw_out, *piece_refs = refs
    else:
        own_ref, *piece_refs = refs
    count, rows, _ = keep_ref.shape
    own_ref[...] = keep_ref[0] + got_ref[:rows].astype(F32)
    for s, ref in enumerate(piece_refs):
        part = slice((s + 1) * rows, (s + 2) * rows)
        ref[:rows] = (keep_ref[s + 1] + got_ref[part].astype(F32)).astype(BF16)
    if sums:
        total = gw_ref[...] + get_sums(got_ref, count * rows, gw_ref.shape)
        gw_out[...] = total
        for ref in piece_refs:
            put_sums(ref, rows, total)


def final_kernel(count, *refs):
    gw_ref, out_ref, gw_out = refs[-3:]
    width = out_ref.shape[2]
    found = []
    for c in range(2):
        own_ref, *piece_refs = refs[c * (count + 1) : (c + 1) * (count + 1)]
        rows = own_ref.shape[0]
        total = own_ref[...]
        for r in piece_refs:
            total += r[:rows].astype(F32)
        found += [total[at : at + width] for at in range(0, rows, width)]
        if c == 0:
            sums = gw_ref[...]
            for r in piece_refs:
                sums += get_sums(r, rows, sums.shape)
            gw_out[...] = sums
    for a, total in enumerate(found):
        out_ref[a] = total.T


def nodes_kernel(blocks, width, ids_ref, eig_ref, *refs):
    ret_refs = refs[:blocks]
    w_refs = refs[blocks : blocks + 3]
    out_ref, eig_out, joined = refs[blocks + 3 :]
    total = eig_ref[...]
    for s in range(blocks):
        at = pl.multiple_of(ids_ref[s] * width, width)
        for a in range(3):
            joined[a, pl.ds(at, width)] = ret_refs[s][a * width : (a + 1) * width]
        if s > 0:
            total += ret_refs[s][3 * width :].astype(F32)
    eig_out[...] = total
    chunk = min(256, out_ref.shape[1])
    for c in range(0, out_ref.shape[1], chunk):
        part = slice(c, c + chunk)
        total = mm(w_refs[0][part], joined[0])
        total += mm(w_refs[1][part], joined[1])
        total += mm(w_refs[2][part], joined[2])
        out_ref[:, part] = total.T.astype(BF16)


def body(node_feats, cotangent, w_query, w_key, w_value, w_out, eigvec, eig_weight, block_mask):
    node_size = lax.axis_size("node")
    clus_size = lax.axis_size("clus")
    node_me = lax.axis_index("node")
    clus_me = lax.axis_index("clus")
    own_rows, own_cot = node_feats[0], cotangent[0]
    size, model = own_rows.shape
    heads, eig_count = eig_weight.shape
    nodes = size * node_size
    width = model // node_size
    head_size = width // heads
    scale = head_size ** (-0.5)
    assert math.frexp(scale)[0] == 0.5
    assert clus_size & (clus_size - 1) == 0
    block = nodes
    while block * nodes > SPAN * 512 and block > 128:
        block //= 2
    far_first = [s for s in range(node_size - 1, 0, -1)]

    rest = clus_size // 2
    order = jnp.arange(node_size, dtype=jnp.int32)
    order = order ^ node_me if node_size & (node_size - 1) == 0 else (order + node_me) % node_size
    slots = jnp.arange(clus_size, dtype=jnp.int32)
    slots = (2 * (slots % rest) + jnp.where(slots < rest, 1, 0)) ^ clus_me
    ids = jnp.concatenate([order, slots])

    smem, vmem = pl.BlockSpec(memory_space=pltpu.SMEM), pl.BlockSpec(memory_space=pltpu.VMEM)
    hbm = pl.BlockSpec(memory_space=pltpu.HBM)

    def call(kernel, in_specs, out_shapes, operands, flops, moved, scratch=()):
        return call_here(kernel, in_specs, out_shapes, operands, flops, moved, scratch)

    def call_here(kernel, in_specs, out_shapes, operands, flops, moved, scratch):
        return pl.pallas_call(
            kernel,
            in_specs=in_specs,
            out_specs=[vmem] * len(out_shapes),
            out_shape=[jax.ShapeDtypeStruct(*o) for o in out_shapes],
            scratch_shapes=scratch,
            cost_estimate=pl.CostEstimate(flops=flops, bytes_accessed=moved, transcendentals=0),
            compiler_params=LIMIT,
        )(*operands)

    crossed = node_size == 4 and size % 32 == 0
    rows = [own_rows] + [None] * (node_size - 1)
    for s in far_first:
        if s < 3 or not crossed:
            rows[s] = take(own_rows, "node", s, node_size)

    def held(array):
        return pltpu.with_memory_space_constraint(array, pltpu.HBM)

    made = call(
        functools.partial(out_grad_kernel, node_size, width),
        [smem] + [hbm] * 5,
        [((size, width), BF16)] * node_size + [((model, width), BF16)] * 3,
        (
            ids,
            held(own_cot),
            *[held(column_blocks(w, width)) for w in (w_out, w_query, w_key, w_value)],
        ),
        3 * 10**8,
        3 * 2**20,
        [
            pltpu.VMEM((size, model), BF16),
            pltpu.VMEM((node_size, model, width), BF16),
            pltpu.SemaphoreType.DMA((node_size + 4,)),
        ],
    )
    d_parts, weights = made[:node_size], made[node_size:]
    d_att = [d_parts[0]] + [None] * (node_size - 1)
    for s in far_first:
        d_att[s] = give(d_parts[s], "node", s, node_size)
    if crossed:
        top, bottom = call(
            split_kernel, [vmem] * 2, [((size // 2, model), BF16)] * 2, (rows[1], rows[2]), 0, 2**19
        )
        rows[3:] = [take(top, "node", 1, node_size), take(bottom, "node", 2, node_size)]
    cots = [own_cot] + [None] * (node_size - 1)
    for s in far_first:
        cots[s] = take(own_cot, "node", s, node_size)

    steps = nodes // block
    both = 2 * head_size
    groups = -(-heads // 2)
    target = model // clus_size
    pairs = rest // 2
    grads_t, out_t, gw_own, eig_own, *parts = call(
        functools.partial(attention_kernel, scale, heads, head_size, node_size, len(rows)),
        [smem, smem] + [vmem] * (len(rows) + node_size + 6),
        [
            ((3 * width, nodes), BF16),
            ((width, nodes), BF16),
            ((heads, eig_count), F32),
            ((eig_count, size), F32),
        ]
        + [((3 * width + eig_count, size), BF16)] * node_size,
        (ids, block_mask[0], *rows, *d_att, *weights, eigvec[0], eig_weight, eig_weight.T),
        8 * 10**9,
        8 * 2**20,
        [
            pltpu.VMEM((heads, steps, both, block), BF16),
            pltpu.VMEM((heads, nodes, both), BF16),
            pltpu.VMEM((groups, steps, both, block), BF16),
            pltpu.VMEM((groups, nodes, both), BF16),
            pltpu.VMEM((eig_count, nodes), F32),
        ],
    )

    def terms(base, parts):
        operands = [ids]
        for left, _, pieces in parts:
            operands += [left, *pieces]
        layout = tuple((lanes, len(pieces)) for _, lanes, pieces in parts)
        return call(
            functools.partial(terms_kernel, node_size + base, layout, target),
            [smem] + [vmem] * (len(operands) - 1),
            [((rest, sum(high - low for low, high in (p[1] for p in parts)), target), BF16)],
            operands,
            10**9,
            2**20,
        )[0]

    near_keeps, near_gots = [], []
    lanes = (0, 2 * width), (2 * width, 3 * width), (0, width)
    plan = (
        [(grads_t, lanes[0], rows)],
        [(grads_t, lanes[1], rows), (out_t, lanes[2], cots)],
    )
    for c, products in enumerate(plan):
        give_half = terms(0, products)
        got_half = give(give_half, "clus", 1, clus_size)
        keep_half = terms(rest, products)
        group_rows = keep_half.shape[1]
        operands = [keep_half, got_half]
        shapes = [
            ((pairs * group_rows + (16 if c == 0 else 0), target), BF16),
            ((pairs, group_rows, target), F32),
        ]
        if c == 0:
            operands += [gw_own, give(gw_own, "clus", 1, clus_size)]
            shapes.append((eig_weight.shape, F32))
        near_give, near_keep, *others = call(
            functools.partial(pair_kernel, c == 0),
            [vmem] * len(operands),
            shapes,
            operands,
            10**6,
            2**21,
        )
        if c == 0:
            gw_pair = others[0]
        near_keeps.append(near_keep)
        near_gots.append(give(near_give, "clus", 2, clus_size))

    returned = [parts[0]] + [None] * (node_size - 1)
    for s in far_first:
        returned[s] = give(parts[s], "node", s, node_size)

    totals = []
    for c in range(2):
        group_rows = near_keeps[c].shape[1]
        extra = 16 if c == 0 else 0
        shapes = [((group_rows, target), F32)] + ([(eig_weight.shape, F32)] if c == 0 else [])
        own, *others = call(
            functools.partial(near_kernel, c == 0),
            [vmem] * (3 if c == 0 else 2),
            shapes + [((group_rows + extra, target), BF16)] * (pairs - 1),
            (near_keeps[c], near_gots[c], *([gw_pair] if c == 0 else [])),
            10**6,
            2**20,
        )
        if c == 0:
            gw_four, *others = others
        totals.append(own)
        found = [None] * (pairs - 1)
        for s in range(pairs - 1, 0, -1):
            found[s - 1] = give(others[s - 1], "clus", 4 * s, clus_size)
        totals += found

    grad_rows, grad_eig = call(
        functools.partial(nodes_kernel, node_size, width),
        [smem] + [vmem] * (node_size + 4),
        [((size, model), BF16), ((eig_count, size), F32)],
        (ids, eig_own, *returned, w_query, w_key, w_value),
        10**9,
        7 * 2**20,
        [pltpu.VMEM((3, model, size), BF16)],
    )

    grad_proj, grad_weight = call(
        functools.partial(final_kernel, pairs - 1),
        [vmem] * (len(totals) + 1),
        [((4, target, width), F32), (eig_weight.shape, F32)],
        (*totals, gw_four),
        10**6,
        2 * 2**20,
    )
    return (grad_rows[None], grad_eig[None], grad_weight, grad_proj)


def solution(mesh):
    placed = (
        P("clus", "node", None),
        P("clus", "node", None),
        P(),
        P(),
        P(),
        P(),
        P("clus", None, None),
        P("node", None),
        P("clus", "node", None, None),
    )

    return jax.shard_map(
        body,
        mesh=mesh,
        in_specs=placed,
        out_specs=(
            P("clus", "node", None),
            P("clus", None, "node"),
            P("node", None),
            P(None, "clus", "node"),
        ),
        check_vma=False,
    )
```

```python
import functools
import math

import jax
import jax.numpy as jnp
from jax import lax
from jax.experimental import pallas as pl
from jax.experimental.pallas import tpu as pltpu
from jax.sharding import PartitionSpec as P


BF16 = jnp.bfloat16
SPAN = 512
F32 = jnp.float32
LIMIT = pltpu.CompilerParams(vmem_limit_bytes=32 * 2**20)


def mm(a, b):
    return jnp.dot(a, b, preferred_element_type=F32)


def take(value, axis, step, size):
    if size & (size - 1) == 0:
        pairs = [(i, i ^ step) for i in range(size)]
    else:
        pairs = [((i + step) % size, i) for i in range(size)]
    return lax.ppermute(value, axis, pairs)


def give(value, axis, step, size):
    if size & (size - 1) == 0:
        return take(value, axis, step, size)
    return lax.ppermute(value, axis, [(i, (i + step) % size) for i in range(size)])


def column_blocks(weight, width):
    if width % 128 == 0:
        return weight
    return weight.reshape(weight.shape[0], -1, width).transpose(1, 0, 2)


def column_copy(ref, at, width, target, sem):
    if len(ref.shape) == 3:
        return pltpu.make_async_copy(ref.at[at], target, sem)
    at = pl.multiple_of(at * width, width)
    return pltpu.make_async_copy(ref.at[:, pl.ds(at, width)], target, sem)


def out_grad_kernel(count, width, ids_ref, rows_ref, w_ref, *refs):
    sources, out_refs, targets = refs[:3], refs[3 : 3 + count], refs[3 + count : 6 + count]
    rows, held, sems = refs[6 + count :]
    row_copy = pltpu.make_async_copy(rows_ref, rows, sems.at[count + 3])
    row_copy.start()
    order = list(range(count - 1, -1, -1))
    copies = {s: column_copy(w_ref, ids_ref[s], width, held.at[s], sems.at[s]) for s in order}
    for s in order:
        copies[s].start()
    others = [
        column_copy(sources[a], ids_ref[0], width, targets[a], sems.at[count + a])
        for a in range(3)
    ]
    for c in others:
        c.start()
    row_copy.wait()
    for s in order:
        copies[s].wait()
        out_refs[s][...] = mm(rows[...], held[s]).astype(BF16)
    for c in others:
        c.wait()


def pack_kernel(first_ref, second_ref, first_d, second_d, first_out, second_out):
    half = first_ref.shape[0] // 2
    for rows, d_ref, out_ref in (
        (second_ref[:half], first_d, first_out),
        (first_ref[half:], second_d, second_out),
    ):
        out_ref[:half] = rows
        count = rows.shape[1] // d_ref.shape[1]
        high = d_ref.shape[0] // count
        for c in range(count):
            lanes = slice(c * d_ref.shape[1], (c + 1) * d_ref.shape[1])
            out_ref[half:, lanes] = d_ref[c * high : (c + 1) * high]


def unpack(ref, half, width):
    return jnp.concatenate(
        [ref[half:, at : at + width] for at in range(0, ref.shape[1], width)], axis=0
    )


def column_block(ref, rows, index, target):
    if target % 128 == 0:
        return ref[:rows, pl.ds(pl.multiple_of(index * target, target), target)]
    fit = 128 // target
    both = ref[:rows, pl.ds(pl.multiple_of(index // fit * 128, 128), 128)]
    found = both[:, :target]
    for part in range(1, fit):
        here = both[:, part * target : (part + 1) * target]
        found = jnp.where(index % fit == part, here, found)
    return found


def write_terms(base, count, target, ids_ref, operands, put):
    group = 2 if count % 2 == 0 else 1
    for start in range(0, count, group):
        at = [ids_ref[base + start + i] for i in range(group)]
        row = 0
        for left, pieces, sizes in operands:
            right = jnp.concatenate(
                [
                    jnp.concatenate(
                        [column_block(r, n, a, target) for r, n in zip(pieces, sizes)], axis=0
                    )
                    for a in at
                ],
                axis=1,
            )
            value = mm(left, right).astype(BF16)
            for i in range(group):
                put(start + i, row, value[:, i * target : (i + 1) * target])
            row += left.shape[0]


def attention_kernel(
    scale, heads, head_size, blocks, sizes, packed, count, target, ids_ref, mask_ref, *refs
):
    pieces = len(sizes)
    row_refs, refs = refs[:pieces], refs[pieces:]
    d_count = blocks - 2 if packed else blocks
    d_refs, refs = refs[:d_count], refs[d_count:]
    wq_ref, wk_ref, wv_ref, eig_ref, lam_ref, lam_t_ref = refs[:6]
    grads_ref, out_ref, gw_ref, eig_out, give_ref = refs[6:11]
    ret_refs = refs[11:-5]
    qe, qn, dt, dn, left_acc = refs[-5:]
    eig_count, nodes = eig_ref.shape
    width = heads * head_size
    size = nodes // blocks
    steps, cols = qe.shape[1], qe.shape[3]
    tile_count = mask_ref.shape[1]
    tile = nodes // tile_count
    per = tile_count // blocks
    both = 2 * head_size
    assert eig_count == head_size
    groups = -(-heads // 2)

    def fit(array):
        extra = groups * both - array.shape[1]
        if extra == 0:
            return array
        return jnp.concatenate([array, jnp.zeros((array.shape[0], extra), array.dtype)], axis=1)

    parts = []
    for s in range(blocks):
        parts.append(eig_ref[:, pl.ds(pl.multiple_of(ids_ref[s] * size, size), size)])
    eig = jnp.concatenate(parts, axis=1)
    turned = jnp.concatenate([eig, eig], axis=0).T
    wide = turned.astype(F32)
    rows = jnp.concatenate([r[:n] for r, n in zip(row_refs, sizes)], axis=0)
    query = fit(mm(rows, wq_ref[...]).astype(BF16))
    keys = fit(mm(rows, wk_ref[...]).astype(BF16))
    values = fit(mm(rows, wv_ref[...]).astype(BF16))
    d_parts = [r[...] for r in d_refs]
    if packed:
        d_parts[1:1] = [unpack(r, n, width) for r, n in zip(row_refs[3:], sizes[3:])]
    d_att = fit(jnp.concatenate(d_parts, axis=0))
    query_t = (query.astype(F32) * scale).astype(BF16).T
    keys_t = keys.T
    values_t = values.T
    d_att_t = d_att.T
    first_half = lax.broadcasted_iota(jnp.int32, (nodes, both), 1) < head_size
    first_row = lax.broadcasted_iota(jnp.int32, (1, both), 1) < head_size

    def pick(even, first, second):
        return jnp.where(first_half, first, second) if even else jnp.where(first_half, second, first)

    def stack(even, first, second):
        return jnp.concatenate([first, second] if even else [second, first], axis=0)

    for g in range(groups):
        group = slice(g * both, (g + 1) * both)
        dn[g] = d_att[:, group]
        for b in range(steps):
            here = slice(b * cols, (b + 1) * cols)
            dt[g, b] = d_att_t[group, here]
        for h in range(2 * g, min(2 * g + 2, heads)):
            even = h % 2 == 0
            part = slice(h * head_size, (h + 1) * head_size)
            qn[h] = pick(even, query[:, group], turned)
            for b in range(steps):
                here = slice(b * cols, (b + 1) * cols)
                qe[h, b] = stack(even, query_t[part, here], eig[:, here])

    def before(head, block, kw, vn):
        return mm(kw, qe[head, block]), mm(vn, dt[head // 2, block])

    def one_block(head, block, kt, vt, scores, dprob, totals):
        at = block * cols
        here = pl.ds(at if isinstance(block, int) else pl.multiple_of(at, cols), cols)
        tiles_here = cols // tile
        columns = []
        for i in range(tiles_here):
            i_tile = block * tiles_here + i
            i_at = ids_ref[i_tile // per] * per + i_tile % per
            found = []
            for j in range(tile_count):
                j_at = ids_ref[j // per] * per + j % per
                part = scores[j * tile : (j + 1) * tile, i * tile : (i + 1) * tile]
                found.append(jnp.where(mask_ref[head, i_at, j_at] > 0, part, -jnp.inf))
            columns.append(jnp.concatenate(found, axis=0))
        masked = jnp.concatenate(columns, axis=1)
        top = jnp.max(masked, axis=0, keepdims=True)
        raised = jnp.exp(masked - top)
        total = jnp.sum(raised, axis=0, keepdims=True)
        prob = raised * (1.0 / total)
        half = prob.astype(BF16)
        first = head * head_size
        out_ref[first : first + head_size, here] = mm(vt, half).astype(BF16)
        value = mm(half, dn[head // 2, here, :])
        delta = jnp.sum(prob * dprob, axis=0, keepdims=True)
        dscore = (prob * (dprob - delta)).astype(BF16)
        left = mm(kt, dscore)
        grads_ref[first : first + head_size, here] = (left[:head_size] * scale).astype(BF16)
        weighted = lam_t_ref[:, head : head + 1] * left[head_size:]
        if head == 0:
            left_acc[:, here] = weighted
        else:
            left_acc[:, here] += weighted
        right = mm(dscore, qn[head, here, :])
        if totals is None:
            return right, value
        return totals[0] + right, totals[1] + value

    def operands(h):
        even, g = h % 2 == 0, h // 2
        group = slice(g * both, (g + 1) * both)
        part = slice(h * head_size, (h + 1) * head_size)
        lam_row = jnp.concatenate([lam_ref[h : h + 1, :]] * 2, axis=1)
        kw = pick(even, keys[:, group], (wide * lam_row).astype(BF16))
        kt = jnp.concatenate([keys_t[part], eig], axis=0)
        vn = pick(even, values[:, group], jnp.zeros((nodes, both), BF16))
        return lam_row, kw, kt, values_t[part], vn

    unrolled = [(h, b) for h in range(heads) for b in range(steps)] if steps <= 4 else []
    ready = {}

    def prepare(at):
        if at < len(unrolled):
            h, b = unrolled[at]
            if b == 0:
                ready[h] = operands(h)
            ready[h, b] = before(h, b, ready[h][1], ready[h][4])

    def all_blocks(h):
        if unrolled:
            totals = None
            for b in range(steps):
                prepare(h * steps + b + 1)
                _, _, kt, vt, _ = ready[h]
                totals = one_block(h, b, kt, vt, *ready.pop((h, b)), totals)
            return ready[h][0], totals
        lam_row, kw, kt, vt, vn = operands(h)
        return lam_row, lax.fori_loop(
            1,
            steps,
            lambda b, t: one_block(h, b, kt, vt, *before(h, b, kw, vn), t),
            one_block(h, 0, kt, vt, *before(h, 0, kw, vn), None),
        )

    prepare(0)
    right_total = None
    for g in range(groups):
        group = slice(g * both, (g + 1) * both)
        found = []
        lam_rows = []
        for h in range(2 * g, min(2 * g + 2, heads)):
            lam_row, totals = all_blocks(h)
            lam_rows.append(lam_row)
            found.append(totals)
        if len(found) == 1:
            found.append((jnp.zeros((nodes, both), F32), jnp.zeros((nodes, both), F32)))
            lam_rows.append(jnp.zeros((1, both), F32))
        keep = min(both, width - g * both)
        key_grad = jnp.where(first_half, found[0][0], found[1][0]).T
        grads_ref[width + g * both : width + g * both + keep, :] = (
            key_grad[:keep] * scale
        ).astype(BF16)
        value_grad = jnp.where(first_half, found[0][1], found[1][1]).T
        grads_ref[2 * width + g * both : 2 * width + g * both + keep, :] = value_grad[
            :keep
        ].astype(BF16)
        right = jnp.where(first_half, found[1][0], found[0][0])
        sums = jnp.sum(wide * right, axis=0, keepdims=True)
        gw_ref[2 * g : 2 * g + 1, :] = sums[:, head_size:]
        if 2 * g + 1 < heads:
            gw_ref[2 * g + 1 : 2 * g + 2, :] = sums[:, :head_size]
        right = right * jnp.where(first_row, lam_rows[1], lam_rows[0])
        right_total = right if right_total is None else right_total + right

    flat = right_total.T
    eig_sum = left_acc[...] + flat[:head_size] + flat[head_size:]
    eig_out[...] = eig_sum[:, :size]
    for b in range(blocks):
        part = slice(b * size, (b + 1) * size)
        ret_refs[b][: 3 * width] = grads_ref[:, part]
        ret_refs[b][3 * width :] = eig_sum[:, part].astype(BF16)
    left = grads_ref[: 2 * width]
    span = left.shape[0]

    def put(block, row, value):
        at = block * span + row
        give_ref[at : at + value.shape[0]] = value

    write_terms(blocks, count, target, ids_ref, [(left, row_refs, sizes)], put)
    put_sums(give_ref, count * span, gw_ref[...])


def terms_kernel(base, layout, target, flat, ids_ref, *refs):
    out_ref, operands, at = refs[-1], [], 0
    for (low, high), sizes in layout:
        pieces = refs[at + 1 : at + 1 + len(sizes)]
        operands.append((refs[at][low:high], pieces, sizes))
        at += 1 + len(sizes)
    span = sum(high - low for (low, high), _ in layout)

    def put(block, row, value):
        if flat:
            at = block * span + row
            out_ref[at : at + value.shape[0]] = value
        else:
            out_ref[block, row : row + value.shape[0]] = value

    count = out_ref.shape[0] // span if flat else out_ref.shape[0]
    write_terms(base, count, target, ids_ref, operands, put)


def put_sums(ref, base, sums):
    rows, lanes = sums.shape
    high = sums.astype(BF16)
    ref[base:] = jnp.zeros((16, ref.shape[1]), BF16)
    ref[base : base + rows, :lanes] = high
    ref[base + 8 : base + 8 + rows, :lanes] = (sums - high.astype(F32)).astype(BF16)


def get_sums(ref, base, shape):
    rows, lanes = shape
    high = ref[base : base + rows, :lanes].astype(F32)
    return high + ref[base + 8 : base + 8 + rows, :lanes].astype(F32)


def pair_kernel(sums, keep_ref, got_ref, *refs):
    if sums:
        gw_ref, give_ref, near_ref, gw_out = refs
    else:
        give_ref, near_ref = refs
    count, rows, _ = keep_ref.shape
    for s in range(count):
        total = keep_ref[s].astype(F32) + got_ref[s * rows : (s + 1) * rows].astype(F32)
        if s % 2 == 0:
            near_ref[s // 2] = total
        else:
            give_ref[s // 2 * rows : (s // 2 + 1) * rows] = total.astype(BF16)
    if sums:
        total = gw_ref[...] + get_sums(got_ref, count * rows, gw_ref.shape)
        gw_out[...] = total
        put_sums(give_ref, count // 2 * rows, total)


def near_kernel(sums, keep_ref, got_ref, *refs):
    if sums:
        gw_ref, own_ref, gw_out, *piece_refs = refs
    else:
        own_ref, *piece_refs = refs
    count, rows, _ = keep_ref.shape
    own_ref[...] = keep_ref[0] + got_ref[:rows].astype(F32)
    for s, ref in enumerate(piece_refs):
        part = slice((s + 1) * rows, (s + 2) * rows)
        ref[:rows] = (keep_ref[s + 1] + got_ref[part].astype(F32)).astype(BF16)
    if sums:
        total = gw_ref[...] + get_sums(got_ref, count * rows, gw_ref.shape)
        gw_out[...] = total
        for ref in piece_refs:
            put_sums(ref, rows, total)


def final_kernel(count, *refs):
    gw_ref, out_ref, gw_out = refs[-3:]
    width = out_ref.shape[2]
    found = []
    for c in range(2):
        own_ref, *piece_refs = refs[c * (count + 1) : (c + 1) * (count + 1)]
        rows = own_ref.shape[0]
        total = own_ref[...]
        for r in piece_refs:
            total += r[:rows].astype(F32)
        found += [total[at : at + width] for at in range(0, rows, width)]
        if c == 0:
            sums = gw_ref[...]
            for r in piece_refs:
                sums += get_sums(r, rows, sums.shape)
            gw_out[...] = sums
    for a, total in enumerate(found):
        out_ref[a] = total.T


def nodes_kernel(blocks, width, ids_ref, eig_ref, *refs):
    ret_refs = refs[:blocks]
    w_refs = refs[blocks : blocks + 3]
    out_ref, eig_out, joined = refs[blocks + 3 :]
    total = eig_ref[...]
    for s in range(blocks):
        at = pl.multiple_of(ids_ref[s] * width, width)
        for a in range(3):
            joined[a, pl.ds(at, width)] = ret_refs[s][a * width : (a + 1) * width]
        if s > 0:
            total += ret_refs[s][3 * width :].astype(F32)
    eig_out[...] = total
    chunk = min(256, out_ref.shape[1])
    for c in range(0, out_ref.shape[1], chunk):
        part = slice(c, c + chunk)
        total = mm(w_refs[0][part], joined[0])
        total += mm(w_refs[1][part], joined[1])
        total += mm(w_refs[2][part], joined[2])
        out_ref[:, part] = total.T.astype(BF16)


def body(node_feats, cotangent, w_query, w_key, w_value, w_out, eigvec, eig_weight, block_mask):
    node_size = lax.axis_size("node")
    clus_size = lax.axis_size("clus")
    node_me = lax.axis_index("node")
    clus_me = lax.axis_index("clus")
    own_rows, own_cot = node_feats[0], cotangent[0]
    size, model = own_rows.shape
    heads, eig_count = eig_weight.shape
    nodes = size * node_size
    width = model // node_size
    head_size = width // heads
    scale = head_size ** (-0.5)
    assert math.frexp(scale)[0] == 0.5
    assert clus_size & (clus_size - 1) == 0
    block = nodes
    while block * nodes > SPAN * 512 and block > 128:
        block //= 2
    far_first = [s for s in range(node_size - 1, 0, -1)]

    rest = clus_size // 2
    order = jnp.arange(node_size, dtype=jnp.int32)
    order = order ^ node_me if node_size & (node_size - 1) == 0 else (order + node_me) % node_size
    slots = jnp.arange(clus_size, dtype=jnp.int32)
    slots = (2 * (slots % rest) + jnp.where(slots < rest, 1, 0)) ^ clus_me
    ids = jnp.concatenate([order, slots])

    smem, vmem = pl.BlockSpec(memory_space=pltpu.SMEM), pl.BlockSpec(memory_space=pltpu.VMEM)
    hbm = pl.BlockSpec(memory_space=pltpu.HBM)

    def call(kernel, in_specs, out_shapes, operands, flops, moved, scratch=()):
        return call_here(kernel, in_specs, out_shapes, operands, flops, moved, scratch)

    def call_here(kernel, in_specs, out_shapes, operands, flops, moved, scratch):
        return pl.pallas_call(
            kernel,
            in_specs=in_specs,
            out_specs=[vmem] * len(out_shapes),
            out_shape=[jax.ShapeDtypeStruct(*o) for o in out_shapes],
            scratch_shapes=scratch,
            cost_estimate=pl.CostEstimate(flops=flops, bytes_accessed=moved, transcendentals=0),
            compiler_params=LIMIT,
        )(*operands)

    crossed = node_size == 4 and size % 64 == 0
    rows = [own_rows] + [None] * (node_size - 1)
    for s in far_first:
        if s < 3 or not crossed:
            rows[s] = take(own_rows, "node", s, node_size)

    def held(array):
        return pltpu.with_memory_space_constraint(array, pltpu.HBM)

    made = call(
        functools.partial(out_grad_kernel, node_size, width),
        [smem] + [hbm] * 5,
        [((size, width), BF16)] * node_size + [((model, width), BF16)] * 3,
        (
            ids,
            held(own_cot),
            *[held(column_blocks(w, width)) for w in (w_out, w_query, w_key, w_value)],
        ),
        3 * 10**8,
        3 * 2**20,
        [
            pltpu.VMEM((size, model), BF16),
            pltpu.VMEM((node_size, model, width), BF16),
            pltpu.SemaphoreType.DMA((node_size + 4,)),
        ],
    )
    d_parts, weights = made[:node_size], made[node_size:]
    d_att = [d_parts[0]] + [None] * (node_size - 1)
    for s in far_first:
        if s < 3 and crossed:
            continue
        d_att[s] = give(d_parts[s], "node", s, node_size)
    sizes = [size] * node_size
    if crossed:
        high = size // 2 + size * width // model
        packed = call(
            pack_kernel,
            [vmem] * 4,
            [((high, model), BF16)] * 2,
            (rows[1], rows[2], d_parts[1], d_parts[2]),
            0,
            2**19,
        )
        rows[3:] = [give(packed[i], "node", i + 1, node_size) for i in range(2)]
        sizes[3:] = [size // 2] * 2
        d_att = [d_att[0], d_att[3]]
    sizes = tuple(sizes)
    cots = [own_cot] + [None] * (node_size - 1)
    for s in far_first:
        cots[s] = take(own_cot, "node", s, node_size)

    steps = nodes // block
    both = 2 * head_size
    groups = -(-heads // 2)
    target = model // clus_size
    pairs = rest // 2
    grads_t, out_t, gw_own, eig_own, give_first, *parts = call(
        functools.partial(
            attention_kernel,
            scale,
            heads,
            head_size,
            node_size,
            sizes,
            crossed,
            rest,
            target,
        ),
        [smem, smem] + [vmem] * (len(rows) + len(d_att) + 6),
        [
            ((3 * width, nodes), BF16),
            ((width, nodes), BF16),
            ((heads, eig_count), F32),
            ((eig_count, size), F32),
            ((rest * 2 * width + 16, target), BF16),
        ]
        + [((3 * width + eig_count, size), BF16)] * node_size,
        (ids, block_mask[0], *rows, *d_att, *weights, eigvec[0], eig_weight, eig_weight.T),
        8 * 10**9,
        8 * 2**20,
        [
            pltpu.VMEM((heads, steps, both, block), BF16),
            pltpu.VMEM((heads, nodes, both), BF16),
            pltpu.VMEM((groups, steps, both, block), BF16),
            pltpu.VMEM((groups, nodes, both), BF16),
            pltpu.VMEM((eig_count, nodes), F32),
        ],
    )

    def terms(base, products, flat):
        operands = [ids]
        for left, _, pieces, _ in products:
            operands += [left, *pieces]
        layout = tuple((lanes, sizes) for _, lanes, _, sizes in products)
        span = sum(high - low for (low, high), _ in layout)
        return call(
            functools.partial(terms_kernel, node_size + base, layout, target, flat),
            [smem] + [vmem] * (len(operands) - 1),
            [((rest * span, target) if flat else (rest, span, target), BF16)],
            operands,
            10**9,
            2**20,
        )[0]

    near_keeps, near_gots = [], []
    lanes = (0, 2 * width), (2 * width, 3 * width), (0, width)
    plan = (
        [(grads_t, lanes[0], rows, sizes)],
        [(grads_t, lanes[1], rows, sizes), (out_t, lanes[2], cots, (size,) * node_size)],
    )
    for c, products in enumerate(plan):
        give_half = give_first if c == 0 else terms(0, products, True)
        got_half = give(give_half, "clus", 1, clus_size)
        keep_half = terms(rest, products, False)
        group_rows = keep_half.shape[1]
        operands = [keep_half, got_half]
        shapes = [
            ((pairs * group_rows + (16 if c == 0 else 0), target), BF16),
            ((pairs, group_rows, target), F32),
        ]
        if c == 0:
            operands.append(gw_own)
            shapes.append((eig_weight.shape, F32))
        near_give, near_keep, *others = call(
            functools.partial(pair_kernel, c == 0),
            [vmem] * len(operands),
            shapes,
            operands,
            10**6,
            2**21,
        )
        if c == 0:
            gw_pair = others[0]
        near_keeps.append(near_keep)
        near_gots.append(give(near_give, "clus", 2, clus_size))

    returned = [parts[0]] + [None] * (node_size - 1)
    for s in far_first:
        returned[s] = give(parts[s], "node", s, node_size)

    totals = []
    for c in range(2):
        group_rows = near_keeps[c].shape[1]
        extra = 16 if c == 0 else 0
        shapes = [((group_rows, target), F32)] + ([(eig_weight.shape, F32)] if c == 0 else [])
        own, *others = call(
            functools.partial(near_kernel, c == 0),
            [vmem] * (3 if c == 0 else 2),
            shapes + [((group_rows + extra, target), BF16)] * (pairs - 1),
            (near_keeps[c], near_gots[c], *([gw_pair] if c == 0 else [])),
            10**6,
            2**20,
        )
        if c == 0:
            gw_four, *others = others
        totals.append(own)
        found = [None] * (pairs - 1)
        for s in range(pairs - 1, 0, -1):
            found[s - 1] = give(others[s - 1], "clus", 4 * s, clus_size)
        totals += found

    grad_rows, grad_eig = call(
        functools.partial(nodes_kernel, node_size, width),
        [smem] + [vmem] * (node_size + 4),
        [((size, model), BF16), ((eig_count, size), F32)],
        (ids, eig_own, *returned, w_query, w_key, w_value),
        10**9,
        7 * 2**20,
        [pltpu.VMEM((3, model, size), BF16)],
    )

    grad_proj, grad_weight = call(
        functools.partial(final_kernel, pairs - 1),
        [vmem] * (len(totals) + 1),
        [((4, target, width), F32), (eig_weight.shape, F32)],
        (*totals, gw_four),
        10**6,
        2 * 2**20,
    )
    return (grad_rows[None], grad_eig[None], grad_weight, grad_proj)


def solution(mesh):
    placed = (
        P("clus", "node", None),
        P("clus", "node", None),
        P(),
        P(),
        P(),
        P(),
        P("clus", None, None),
        P("node", None),
        P("clus", "node", None, None),
    )

    return jax.shard_map(
        body,
        mesh=mesh,
        in_specs=placed,
        out_specs=(
            P("clus", "node", None),
            P("clus", None, "node"),
            P("node", None),
            P(None, "clus", "node"),
        ),
        check_vma=False,
    )
```

```python
import functools
import math

import jax
import jax.numpy as jnp
from jax import lax
from jax.experimental import pallas as pl
from jax.experimental.pallas import tpu as pltpu
from jax.sharding import PartitionSpec as P


BF16 = jnp.bfloat16
SPAN = 512
FRACTION = 4
F32 = jnp.float32
LIMIT = pltpu.CompilerParams(vmem_limit_bytes=32 * 2**20)


def mm(a, b):
    return jnp.dot(a, b, preferred_element_type=F32)


def take(value, axis, step, size):
    if size & (size - 1) == 0:
        pairs = [(i, i ^ step) for i in range(size)]
    else:
        pairs = [((i + step) % size, i) for i in range(size)]
    return lax.ppermute(value, axis, pairs)


def give(value, axis, step, size):
    if size & (size - 1) == 0:
        return take(value, axis, step, size)
    return lax.ppermute(value, axis, [(i, (i + step) % size) for i in range(size)])


def column_blocks(weight, width):
    if width % 128 == 0:
        return weight
    return weight.reshape(weight.shape[0], -1, width).transpose(1, 0, 2)


def column_copy(ref, at, width, target, sem):
    if len(ref.shape) == 3:
        return pltpu.make_async_copy(ref.at[at], target, sem)
    at = pl.multiple_of(at * width, width)
    return pltpu.make_async_copy(ref.at[:, pl.ds(at, width)], target, sem)


def out_grad_kernel(count, width, ids_ref, rows_ref, w_ref, *refs):
    sources, out_refs, targets = refs[:3], refs[3 : 3 + count], refs[3 + count : 6 + count]
    rows, held, sems = refs[6 + count :]
    row_copy = pltpu.make_async_copy(rows_ref, rows, sems.at[count + 3])
    row_copy.start()
    order = list(range(count - 1, -1, -1))
    copies = {s: column_copy(w_ref, ids_ref[s], width, held.at[s], sems.at[s]) for s in order}
    for s in order:
        copies[s].start()
    others = [
        column_copy(sources[a], ids_ref[0], width, targets[a], sems.at[count + a])
        for a in range(3)
    ]
    for c in others:
        c.start()
    row_copy.wait()
    for s in order:
        copies[s].wait()
        out_refs[s][...] = mm(rows[...], held[s]).astype(BF16)
    for c in others:
        c.wait()


def split_kernel(first_ref, second_ref, top_ref, bottom_ref):
    half = top_ref.shape[0]
    top_ref[...] = second_ref[:half]
    bottom_ref[...] = first_ref[half:]


def column_block(ref, rows, index, target):
    if target % 128 == 0:
        return ref[:rows, pl.ds(pl.multiple_of(index * target, target), target)]
    fit = 128 // target
    both = ref[:rows, pl.ds(pl.multiple_of(index // fit * 128, 128), 128)]
    found = both[:, :target]
    for part in range(1, fit):
        here = both[:, part * target : (part + 1) * target]
        found = jnp.where(index % fit == part, here, found)
    return found


def write_terms(base, count, target, ids_ref, operands, put):
    group = 2 if count % 2 == 0 else 1
    for start in range(0, count, group):
        at = [ids_ref[base + start + i] for i in range(group)]
        row = 0
        for left, pieces, sizes in operands:
            right = jnp.concatenate(
                [
                    jnp.concatenate(
                        [column_block(r, n, a, target) for r, n in zip(pieces, sizes)], axis=0
                    )
                    for a in at
                ],
                axis=1,
            )
            value = mm(left, right).astype(BF16)
            for i in range(group):
                put(start + i, row, value[:, i * target : (i + 1) * target])
            row += left.shape[0]


def attention_kernel(
    scale, heads, head_size, blocks, sizes, count, target, first_rows, ids_ref, mask_ref, *refs
):
    pieces = len(sizes)
    row_refs, refs = refs[:pieces], refs[pieces:]
    d_refs, refs = refs[:blocks], refs[blocks:]
    wq_ref, wk_ref, wv_ref, eig_ref, lam_ref, lam_t_ref = refs[:6]
    grads_ref, out_ref, gw_ref, eig_out, give_ref = refs[6:11]
    ret_refs = refs[11:-5]
    qe, qn, dt, dn, left_acc = refs[-5:]
    eig_count, nodes = eig_ref.shape
    width = heads * head_size
    size = nodes // blocks
    steps, cols = qe.shape[1], qe.shape[3]
    tile_count = mask_ref.shape[1]
    tile = nodes // tile_count
    per = tile_count // blocks
    both = 2 * head_size
    assert eig_count == head_size
    groups = -(-heads // 2)

    def fit(array):
        extra = groups * both - array.shape[1]
        if extra == 0:
            return array
        return jnp.concatenate([array, jnp.zeros((array.shape[0], extra), array.dtype)], axis=1)

    parts = []
    for s in range(blocks):
        parts.append(eig_ref[:, pl.ds(pl.multiple_of(ids_ref[s] * size, size), size)])
    eig = jnp.concatenate(parts, axis=1)
    turned = jnp.concatenate([eig, eig], axis=0).T
    wide = turned.astype(F32)
    rows = jnp.concatenate([r[:n] for r, n in zip(row_refs, sizes)], axis=0)
    query = fit(mm(rows, wq_ref[...]).astype(BF16))
    keys = fit(mm(rows, wk_ref[...]).astype(BF16))
    values = fit(mm(rows, wv_ref[...]).astype(BF16))
    d_att = fit(jnp.concatenate([r[...] for r in d_refs], axis=0))
    query_t = (query.astype(F32) * scale).astype(BF16).T
    keys_t = keys.T
    values_t = values.T
    d_att_t = d_att.T
    first_half = lax.broadcasted_iota(jnp.int32, (nodes, both), 1) < head_size
    first_row = lax.broadcasted_iota(jnp.int32, (1, both), 1) < head_size

    def pick(even, first, second):
        return jnp.where(first_half, first, second) if even else jnp.where(first_half, second, first)

    def stack(even, first, second):
        return jnp.concatenate([first, second] if even else [second, first], axis=0)

    for g in range(groups):
        group = slice(g * both, (g + 1) * both)
        dn[g] = d_att[:, group]
        for b in range(steps):
            here = slice(b * cols, (b + 1) * cols)
            dt[g, b] = d_att_t[group, here]
        for h in range(2 * g, min(2 * g + 2, heads)):
            even = h % 2 == 0
            part = slice(h * head_size, (h + 1) * head_size)
            qn[h] = pick(even, query[:, group], turned)
            for b in range(steps):
                here = slice(b * cols, (b + 1) * cols)
                qe[h, b] = stack(even, query_t[part, here], eig[:, here])

    def before(head, block, kw, vn):
        return mm(kw, qe[head, block]), mm(vn, dt[head // 2, block])

    def one_block(head, block, kt, vt, scores, dprob, totals):
        at = block * cols
        here = pl.ds(at if isinstance(block, int) else pl.multiple_of(at, cols), cols)
        tiles_here = cols // tile
        columns = []
        for i in range(tiles_here):
            i_tile = block * tiles_here + i
            i_at = ids_ref[i_tile // per] * per + i_tile % per
            found = []
            for j in range(tile_count):
                j_at = ids_ref[j // per] * per + j % per
                part = scores[j * tile : (j + 1) * tile, i * tile : (i + 1) * tile]
                found.append(jnp.where(mask_ref[head, i_at, j_at] > 0, part, -jnp.inf))
            columns.append(jnp.concatenate(found, axis=0))
        masked = jnp.concatenate(columns, axis=1)
        top = jnp.max(masked, axis=0, keepdims=True)
        raised = jnp.exp(masked - top)
        total = jnp.sum(raised, axis=0, keepdims=True)
        prob = raised * (1.0 / total)
        half = prob.astype(BF16)
        first = head * head_size
        out_ref[first : first + head_size, here] = mm(vt, half).astype(BF16)
        value = mm(half, dn[head // 2, here, :])
        delta = jnp.sum(prob * dprob, axis=0, keepdims=True)
        dscore = (prob * (dprob - delta)).astype(BF16)
        right = mm(dscore, qn[head, here, :])
        left = mm(kt, dscore)
        grads_ref[first : first + head_size, here] = (left[:head_size] * scale).astype(BF16)
        weighted = lam_t_ref[:, head : head + 1] * left[head_size:]
        if head == 0:
            left_acc[:, here] = weighted
        else:
            left_acc[:, here] += weighted
        if totals is None:
            return right, value
        return totals[0] + right, totals[1] + value

    def operands(h):
        even, g = h % 2 == 0, h // 2
        group = slice(g * both, (g + 1) * both)
        part = slice(h * head_size, (h + 1) * head_size)
        lam_row = jnp.concatenate([lam_ref[h : h + 1, :]] * 2, axis=1)
        kw = pick(even, keys[:, group], (wide * lam_row).astype(BF16))
        kt = jnp.concatenate([keys_t[part], eig], axis=0)
        vn = pick(even, values[:, group], jnp.zeros((nodes, both), BF16))
        return lam_row, kw, kt, values_t[part], vn

    unrolled = [(h, b) for h in range(heads) for b in range(steps)] if steps <= 4 else []
    ready = {}

    def prepare(at):
        if at < len(unrolled):
            h, b = unrolled[at]
            if b == 0:
                ready[h] = operands(h)
            ready[h, b] = before(h, b, ready[h][1], ready[h][4])

    def all_blocks(h):
        if unrolled:
            totals = None
            for b in range(steps):
                prepare(h * steps + b + 1)
                _, _, kt, vt, _ = ready[h]
                totals = one_block(h, b, kt, vt, *ready.pop((h, b)), totals)
            return ready[h][0], totals
        lam_row, kw, kt, vt, vn = operands(h)
        return lam_row, lax.fori_loop(
            1,
            steps,
            lambda b, t: one_block(h, b, kt, vt, *before(h, b, kw, vn), t),
            one_block(h, 0, kt, vt, *before(h, 0, kw, vn), None),
        )

    prepare(0)
    right_total = None
    for g in range(groups):
        group = slice(g * both, (g + 1) * both)
        found = []
        lam_rows = []
        for h in range(2 * g, min(2 * g + 2, heads)):
            lam_row, totals = all_blocks(h)
            lam_rows.append(lam_row)
            found.append(totals)
        if len(found) == 1:
            found.append((jnp.zeros((nodes, both), F32), jnp.zeros((nodes, both), F32)))
            lam_rows.append(jnp.zeros((1, both), F32))
        keep = min(both, width - g * both)
        key_grad = jnp.where(first_half, found[0][0], found[1][0]).T
        grads_ref[width + g * both : width + g * both + keep, :] = (
            key_grad[:keep] * scale
        ).astype(BF16)
        value_grad = jnp.where(first_half, found[0][1], found[1][1]).T
        grads_ref[2 * width + g * both : 2 * width + g * both + keep, :] = value_grad[
            :keep
        ].astype(BF16)
        right = jnp.where(first_half, found[1][0], found[0][0])
        sums = jnp.sum(wide * right, axis=0, keepdims=True)
        gw_ref[2 * g : 2 * g + 1, :] = sums[:, head_size:]
        if 2 * g + 1 < heads:
            gw_ref[2 * g + 1 : 2 * g + 2, :] = sums[:, :head_size]
        right = right * jnp.where(first_row, lam_rows[1], lam_rows[0])
        right_total = right if right_total is None else right_total + right

    flat = right_total.T
    eig_sum = left_acc[...] + flat[:head_size] + flat[head_size:]
    eig_out[...] = eig_sum[:, :size]
    for b in range(blocks):
        part = slice(b * size, (b + 1) * size)
        ret_refs[b][: 3 * width] = grads_ref[:, part]
        ret_refs[b][3 * width :] = eig_sum[:, part].astype(BF16)
    left = grads_ref[:first_rows]
    span = left.shape[0]

    def put(block, row, value):
        at = block * span + row
        give_ref[at : at + value.shape[0]] = value

    write_terms(blocks, count, target, ids_ref, [(left, row_refs, sizes)], put)
    put_sums(give_ref, count * span, gw_ref[...])


def terms_kernel(base, layout, target, flat, ids_ref, *refs):
    out_ref, operands, at = refs[-1], [], 0
    for (low, high), sizes in layout:
        pieces = refs[at + 1 : at + 1 + len(sizes)]
        operands.append((refs[at][low:high], pieces, sizes))
        at += 1 + len(sizes)
    span = sum(high - low for (low, high), _ in layout)

    def put(block, row, value):
        if flat:
            at = block * span + row
            out_ref[at : at + value.shape[0]] = value
        else:
            out_ref[block, row : row + value.shape[0]] = value

    count = out_ref.shape[0] // span if flat else out_ref.shape[0]
    write_terms(base, count, target, ids_ref, operands, put)


def put_sums(ref, base, sums):
    rows, lanes = sums.shape
    high = sums.astype(BF16)
    ref[base:] = jnp.zeros((16, ref.shape[1]), BF16)
    ref[base : base + rows, :lanes] = high
    ref[base + 8 : base + 8 + rows, :lanes] = (sums - high.astype(F32)).astype(BF16)


def get_sums(ref, base, shape):
    rows, lanes = shape
    high = ref[base : base + rows, :lanes].astype(F32)
    return high + ref[base + 8 : base + 8 + rows, :lanes].astype(F32)


def pair_kernel(sums, keep_ref, got_ref, *refs):
    if sums:
        gw_ref, give_ref, near_ref, gw_out = refs
    else:
        give_ref, near_ref = refs
    count, rows, _ = keep_ref.shape
    for s in range(count):
        total = keep_ref[s].astype(F32) + got_ref[s * rows : (s + 1) * rows].astype(F32)
        if s % 2 == 0:
            near_ref[s // 2] = total
        else:
            give_ref[s // 2 * rows : (s // 2 + 1) * rows] = total.astype(BF16)
    if sums:
        total = gw_ref[...] + get_sums(got_ref, count * rows, gw_ref.shape)
        gw_out[...] = total
        put_sums(give_ref, count // 2 * rows, total)


def near_kernel(sums, keep_ref, got_ref, *refs):
    if sums:
        gw_ref, own_ref, gw_out, *piece_refs = refs
    else:
        own_ref, *piece_refs = refs
    count, rows, _ = keep_ref.shape
    own_ref[...] = keep_ref[0] + got_ref[:rows].astype(F32)
    for s, ref in enumerate(piece_refs):
        part = slice((s + 1) * rows, (s + 2) * rows)
        ref[:rows] = (keep_ref[s + 1] + got_ref[part].astype(F32)).astype(BF16)
    if sums:
        total = gw_ref[...] + get_sums(got_ref, count * rows, gw_ref.shape)
        gw_out[...] = total
        for ref in piece_refs:
            put_sums(ref, rows, total)


def final_kernel(count, *refs):
    gw_ref, out_ref, gw_out = refs[-3:]
    width = out_ref.shape[2]
    found = []
    for c in range(2):
        own_ref, *piece_refs = refs[c * (count + 1) : (c + 1) * (count + 1)]
        rows = own_ref.shape[0]
        total = own_ref[...]
        for r in piece_refs:
            total += r[:rows].astype(F32)
        found.append(total)
        if c == 0:
            sums = gw_ref[...]
            for r in piece_refs:
                sums += get_sums(r, rows, sums.shape)
            gw_out[...] = sums
    total = jnp.concatenate(found, axis=0)
    for a in range(out_ref.shape[0]):
        out_ref[a] = total[a * width : (a + 1) * width].T


def nodes_kernel(blocks, width, ids_ref, eig_ref, *refs):
    ret_refs = refs[:blocks]
    w_refs = refs[blocks : blocks + 3]
    out_ref, eig_out, joined = refs[blocks + 3 :]
    total = eig_ref[...]
    for s in range(blocks):
        at = pl.multiple_of(ids_ref[s] * width, width)
        for a in range(3):
            joined[a, pl.ds(at, width)] = ret_refs[s][a * width : (a + 1) * width]
        if s > 0:
            total += ret_refs[s][3 * width :].astype(F32)
    eig_out[...] = total
    chunk = min(256, out_ref.shape[1])
    for c in range(0, out_ref.shape[1], chunk):
        part = slice(c, c + chunk)
        total = mm(w_refs[0][part], joined[0])
        total += mm(w_refs[1][part], joined[1])
        total += mm(w_refs[2][part], joined[2])
        out_ref[:, part] = total.T.astype(BF16)


def body(node_feats, cotangent, w_query, w_key, w_value, w_out, eigvec, eig_weight, block_mask):
    node_size = lax.axis_size("node")
    clus_size = lax.axis_size("clus")
    node_me = lax.axis_index("node")
    clus_me = lax.axis_index("clus")
    own_rows, own_cot = node_feats[0], cotangent[0]
    size, model = own_rows.shape
    heads, eig_count = eig_weight.shape
    nodes = size * node_size
    width = model // node_size
    head_size = width // heads
    scale = head_size ** (-0.5)
    assert math.frexp(scale)[0] == 0.5
    assert clus_size & (clus_size - 1) == 0
    block = nodes
    while block * nodes > SPAN * 512 and block > 128:
        block //= 2
    far_first = [s for s in range(node_size - 1, 0, -1)]

    rest = clus_size // 2
    order = jnp.arange(node_size, dtype=jnp.int32)
    order = order ^ node_me if node_size & (node_size - 1) == 0 else (order + node_me) % node_size
    slots = jnp.arange(clus_size, dtype=jnp.int32)
    slots = (2 * (slots % rest) + jnp.where(slots < rest, 1, 0)) ^ clus_me
    ids = jnp.concatenate([order, slots])

    smem, vmem = pl.BlockSpec(memory_space=pltpu.SMEM), pl.BlockSpec(memory_space=pltpu.VMEM)
    hbm = pl.BlockSpec(memory_space=pltpu.HBM)

    def call(kernel, in_specs, out_shapes, operands, flops, moved, scratch=()):
        return call_here(kernel, in_specs, out_shapes, operands, flops, moved, scratch)

    def call_here(kernel, in_specs, out_shapes, operands, flops, moved, scratch):
        return pl.pallas_call(
            kernel,
            in_specs=in_specs,
            out_specs=[vmem] * len(out_shapes),
            out_shape=[jax.ShapeDtypeStruct(*o) for o in out_shapes],
            scratch_shapes=scratch,
            cost_estimate=pl.CostEstimate(flops=flops, bytes_accessed=moved, transcendentals=0),
            compiler_params=LIMIT,
        )(*operands)

    crossed = node_size == 4 and size % 64 == 0
    rows = [own_rows] + [None] * (node_size - 1)
    for s in far_first:
        if s < 3 or not crossed:
            rows[s] = take(own_rows, "node", s, node_size)

    def held(array):
        return pltpu.with_memory_space_constraint(array, pltpu.HBM)

    made = call(
        functools.partial(out_grad_kernel, node_size, width),
        [smem] + [hbm] * 5,
        [((size, width), BF16)] * node_size + [((model, width), BF16)] * 3,
        (
            ids,
            held(own_cot),
            *[held(column_blocks(w, width)) for w in (w_out, w_query, w_key, w_value)],
        ),
        3 * 10**8,
        3 * 2**20,
        [
            pltpu.VMEM((size, model), BF16),
            pltpu.VMEM((node_size, model, width), BF16),
            pltpu.SemaphoreType.DMA((node_size + 4,)),
        ],
    )
    d_parts, weights = made[:node_size], made[node_size:]
    d_att = [d_parts[0]] + [None] * (node_size - 1)
    for s in far_first:
        d_att[s] = give(d_parts[s], "node", s, node_size)
    sizes = [size] * node_size
    if crossed:
        halves = call(
            split_kernel, [vmem] * 2, [((size // 2, model), BF16)] * 2, (rows[1], rows[2]), 0, 2**19
        )
        rows[3:] = [give(halves[i], "node", i + 1, node_size) for i in range(2)]
        sizes[3:] = [size // 2] * 2
    sizes = tuple(sizes)
    cots = [own_cot] + [None] * (node_size - 1)
    for s in far_first:
        cots[s] = take(own_cot, "node", s, node_size)

    steps = nodes // block
    both = 2 * head_size
    groups = -(-heads // 2)
    target = model // clus_size
    pairs = rest // 2
    first_rows = 2 * width + width // FRACTION
    grads_t, out_t, gw_own, eig_own, give_first, *parts = call(
        functools.partial(
            attention_kernel,
            scale,
            heads,
            head_size,
            node_size,
            sizes,
            rest,
            target,
            first_rows,
        ),
        [smem, smem] + [vmem] * (len(rows) + len(d_att) + 6),
        [
            ((3 * width, nodes), BF16),
            ((width, nodes), BF16),
            ((heads, eig_count), F32),
            ((eig_count, size), F32),
            ((rest * first_rows + 16, target), BF16),
        ]
        + [((3 * width + eig_count, size), BF16)] * node_size,
        (ids, block_mask[0], *rows, *d_att, *weights, eigvec[0], eig_weight, eig_weight.T),
        8 * 10**9,
        8 * 2**20,
        [
            pltpu.VMEM((heads, steps, both, block), BF16),
            pltpu.VMEM((heads, nodes, both), BF16),
            pltpu.VMEM((groups, steps, both, block), BF16),
            pltpu.VMEM((groups, nodes, both), BF16),
            pltpu.VMEM((eig_count, nodes), F32),
        ],
    )

    def terms(base, products, flat):
        operands = [ids]
        for left, _, pieces, _ in products:
            operands += [left, *pieces]
        layout = tuple((lanes, sizes) for _, lanes, _, sizes in products)
        span = sum(high - low for (low, high), _ in layout)
        return call(
            functools.partial(terms_kernel, node_size + base, layout, target, flat),
            [smem] + [vmem] * (len(operands) - 1),
            [((rest * span, target) if flat else (rest, span, target), BF16)],
            operands,
            10**9,
            2**20,
        )[0]

    near_keeps, near_gots = [], []
    lanes = (0, first_rows), (first_rows, 3 * width), (0, width)
    plan = (
        [(grads_t, lanes[0], rows, sizes)],
        [(grads_t, lanes[1], rows, sizes), (out_t, lanes[2], cots, (size,) * node_size)],
    )
    for c, products in enumerate(plan):
        give_half = give_first if c == 0 else terms(0, products, True)
        got_half = give(give_half, "clus", 1, clus_size)
        keep_half = terms(rest, products, False)
        group_rows = keep_half.shape[1]
        operands = [keep_half, got_half]
        shapes = [
            ((pairs * group_rows + (16 if c == 0 else 0), target), BF16),
            ((pairs, group_rows, target), F32),
        ]
        if c == 0:
            operands.append(gw_own)
            shapes.append((eig_weight.shape, F32))
        near_give, near_keep, *others = call(
            functools.partial(pair_kernel, c == 0),
            [vmem] * len(operands),
            shapes,
            operands,
            10**6,
            2**21,
        )
        if c == 0:
            gw_pair = others[0]
        near_keeps.append(near_keep)
        near_gots.append(give(near_give, "clus", 2, clus_size))

    returned = [parts[0]] + [None] * (node_size - 1)
    for s in far_first:
        returned[s] = give(parts[s], "node", s, node_size)

    totals = []
    for c in range(2):
        group_rows = near_keeps[c].shape[1]
        extra = 16 if c == 0 else 0
        shapes = [((group_rows, target), F32)] + ([(eig_weight.shape, F32)] if c == 0 else [])
        own, *others = call(
            functools.partial(near_kernel, c == 0),
            [vmem] * (3 if c == 0 else 2),
            shapes + [((group_rows + extra, target), BF16)] * (pairs - 1),
            (near_keeps[c], near_gots[c], *([gw_pair] if c == 0 else [])),
            10**6,
            2**20,
        )
        if c == 0:
            gw_four, *others = others
        totals.append(own)
        found = [None] * (pairs - 1)
        for s in range(pairs - 1, 0, -1):
            found[s - 1] = give(others[s - 1], "clus", 4 * s, clus_size)
        totals += found

    grad_rows, grad_eig = call(
        functools.partial(nodes_kernel, node_size, width),
        [smem] + [vmem] * (node_size + 4),
        [((size, model), BF16), ((eig_count, size), F32)],
        (ids, eig_own, *returned, w_query, w_key, w_value),
        10**9,
        7 * 2**20,
        [pltpu.VMEM((3, model, size), BF16)],
    )

    grad_proj, grad_weight = call(
        functools.partial(final_kernel, pairs - 1),
        [vmem] * (len(totals) + 1),
        [((4, target, width), F32), (eig_weight.shape, F32)],
        (*totals, gw_four),
        10**6,
        2 * 2**20,
    )
    return (grad_rows[None], grad_eig[None], grad_weight, grad_proj)


def solution(mesh):
    placed = (
        P("clus", "node", None),
        P("clus", "node", None),
        P(),
        P(),
        P(),
        P(),
        P("clus", None, None),
        P("node", None),
        P("clus", "node", None, None),
    )

    return jax.shard_map(
        body,
        mesh=mesh,
        in_specs=placed,
        out_specs=(
            P("clus", "node", None),
            P("clus", None, "node"),
            P("node", None),
            P(None, "clus", "node"),
        ),
        check_vma=False,
    )
```
